32 devices in a mesh: ens: 2 (over y), lat: 4 (over x, core), lon: 4 (over z).
Axes of the slice: x: 2, y: 2, z: 4, core: 2. Of those that a mesh axis runs over, the one named last changes fastest.
Arguments:
- state_now: float32 [6, 1152, 2304], P('ens', 'lat', 'lon'), parts along dimension 0, may hold values from -2 to 2, as said below
- state_old: float32 [6, 1152, 2304], P('ens', 'lat', 'lon'), parts along dimension 0, may hold values from -6 to 6
- polar_cutoff: int32 [576], replicated, may hold values from 1 to 1152, as said below
Outputs:
- state_new: float32 [6, 1152, 2304], P('ens', 'lat', 'lon'), parts along dimension 0
The draws below stay inside these ranges and needn't reach their ends.
There are 2 independent parts, one for each index of `ens`. The reference program is written for one: setup_inputs(seed, part) draws one part's arguments, and reference() takes and returns one part's arrays. A program takes and returns all parts, laid end to end along the dimension named above; an argument that names none is the same for every part. Nothing has to cross between parts.
Inputs may be any that keep to these rules, and one draw needn't show every extreme that they name: `polar_cutoff`: every entry is at least 1 and at most 1152; the two rows next to 45 degrees keep all wavenumbers up to 1152. `state_now`: component 0 (depth) lies between 0.25 and 1.75.
All inputs are finite; a program needn't handle non-finite values.
Results may differ from the reference program's by a relative error of at most 0.00005.
Values sent between devices are 32-bit elements; how exact they have to be, the bound alone decides.
A program may use at most 64 MiB of HBM per device.

```python
import math
import jax
import jax.numpy as jnp

NLON = 2304
NLAT = 1152


def draw_state_now(key, part):
    first_key, second_key = jax.random.split(jax.random.fold_in(key, 11))
    depth = 1.0 + 0.25 * jnp.clip(jax.random.normal(first_key, (NLAT, NLON), jnp.float32), -3.0, 3.0)
    wind = 0.5 * jnp.clip(jax.random.normal(second_key, (2, NLAT, NLON), jnp.float32), -4.0, 4.0)
    return jnp.concatenate([depth[None], wind], axis=0).astype(jnp.float32)


def draw_polar_cutoff(key, part):
    quarter = NLAT // 4
    steps_in = jnp.arange(quarter, dtype=jnp.int32)
    distance = jnp.concatenate([steps_in, quarter - 1 - steps_in])
    base_cut = jnp.maximum((distance + 1) * (NLON // 2) // quarter, 2)
    jitter = jax.random.randint(jax.random.fold_in(key, 23), (2 * quarter,), 0, base_cut // 2 + 1, dtype=jnp.int32)
    jitter = jnp.where(distance == quarter - 1, 0, jitter)
    return (base_cut - jitter).astype(jnp.int32)


def block_levels(own_key, extent, pieces, least, largest):
    def one(position, parts):
        draws = jax.random.uniform(jax.random.fold_in(jax.random.fold_in(own_key, 6), position), (parts,), jnp.float32, least / len(pieces), largest / len(pieces))
        return jnp.repeat(jnp.exp(draws), extent[position] // parts).reshape((-1,) + (1,) * (len(extent) - position - 1))

    loudness = one(*pieces[0])
    for cut in pieces[1:]:
        loudness = loudness * one(*cut)
    return loudness


def bell_draw(stream_key, extent, spread, bound, cuts=(), held_as=jnp.bfloat16):
    values = jax.random.normal(stream_key, extent, jnp.float32) * spread
    if len(cuts) > 0:
        values = block_levels(stream_key, extent, cuts, -0.22, 0.18) * values
    return jnp.clip(values, min=-bound, max=bound).astype(held_as)


def setup_inputs(seed: int = 0, part: int = 0) -> dict:
    streams_of = jax.random.split(jax.random.key(seed), 4)
    part_keys = jax.random.split(jax.random.fold_in(streams_of[3], part), 4)
    return {
        "state_now": draw_state_now(jax.random.fold_in(jax.random.fold_in(streams_of[3], part), 71), part),
        "state_old": bell_draw(part_keys[1], (3, NLAT, NLON), 1.0, 6.0, ((1, 4), (2, 4)), jnp.float32),
        "polar_cutoff": draw_polar_cutoff(jax.random.fold_in(streams_of[3], 71), part),
    }


step_scale = 0.2
coriolis = 2.0
gravity = 1.0


def latitude_terms(row_index, lat_total):
    distance = jnp.minimum(row_index + 0.5, lat_total - row_index - 0.5)
    cosine_lat = jnp.sin(math.pi * distance / lat_total)
    sine_lat = -jnp.cos(math.pi * (row_index + 0.5) / lat_total)
    return cosine_lat, sine_lat


def tendencies(lat_padded, lon_padded, cos_ext, sine_lat, lat_total, lon_total):
    cosine_lat = cos_ext[1:-1]
    zonal_scale = (lon_total / (4.0 * lat_total) / cosine_lat)[:, None]
    metric = (math.pi / lat_total) * sine_lat / cosine_lat
    depth_lon, east_lon, north_lon = lon_padded[0], lon_padded[1], lon_padded[2]
    depth_lat, east_lat, north_lat = lat_padded[0], lat_padded[1], lat_padded[2]
    depth = depth_lon[:, 1:-1]
    east = east_lon[:, 1:-1]
    north = north_lon[:, 1:-1]

    def zonal_change(field):
        return zonal_scale * (field[:, 2:] - field[:, :-2])

    def northward_change(field):
        return 0.5 * (field[2:] - field[:-2])

    mass_flux = depth_lat * north_lat * cos_ext[:, None]
    tend_depth = -zonal_change(depth_lon * east_lon) - northward_change(mass_flux) / cosine_lat[:, None]
    turning = coriolis * sine_lat[:, None] + metric[:, None] * east
    tend_east = -east * zonal_change(east_lon) - north * northward_change(east_lat) + turning * north - gravity * zonal_change(depth_lon)
    tend_north = -east * zonal_change(north_lon) - north * northward_change(north_lat) - turning * east - gravity * northward_change(depth_lat)
    return jnp.stack([tend_depth, tend_east, tend_north])


def reference(state_now, state_old, polar_cutoff):
    row_index = jnp.arange(-1, NLAT + 1, dtype=jnp.int32).astype(jnp.float32)
    cos_ext, sin_ext = latitude_terms(row_index, NLAT)
    lat_padded = jnp.pad(state_now, ((0, 0), (1, 1), (0, 0)))
    lon_padded = jnp.concatenate([state_now[:, :, -1:], state_now, state_now[:, :, :1]], axis=2)
    forcing = tendencies(lat_padded, lon_padded, cos_ext, sin_ext[1:-1], NLAT, NLON)
    quarter = NLAT // 4
    polar_rows = jnp.concatenate([forcing[:, :quarter], forcing[:, NLAT - quarter:]], axis=1)
    spectrum = jnp.fft.rfft(polar_rows, axis=2)
    wavenumber = jnp.arange(NLON // 2 + 1, dtype=jnp.int32)
    keep_mask = wavenumber[None, None, :] <= polar_cutoff[None, :, None]
    smooth = jnp.fft.irfft(jnp.where(keep_mask, spectrum, 0.0), n=NLON, axis=2).astype(forcing.dtype)
    filtered = forcing.at[:, :quarter].set(smooth[:, :quarter]).at[:, NLAT - quarter:].set(smooth[:, quarter:])
    return state_old + step_scale * filtered
```

```python
import functools
import math

import jax
import jax.numpy as jnp
import numpy as np
from jax import lax
from jax.experimental import pallas as pl
from jax.experimental.pallas import tpu as pltpu
from jax.sharding import PartitionSpec as P

LANES = 128
SUB = 8
MESH = pl.DeviceIdType.MESH
step_scale = 0.2
coriolis = 2.0
gravity = 1.0
highest = lax.Precision.HIGHEST


def padded(value, sides, width, wrap):
    for axis, dim in sides:
        devices, length = (lax.axis_size(axis), value.shape[dim])
        up = [(i, (i + 1) % devices) for i in range(devices if wrap else devices - 1)]
        down = [(j, i) for i, j in up]
        last = lax.slice_in_dim(value, length - width, length, axis=dim)
        leading = lax.slice_in_dim(value, 0, width, axis=dim)
        before = lax.ppermute(last, axis, up)
        after = lax.ppermute(leading, axis, down)
        value = jnp.concatenate([before, value, after], axis=dim)
    return value


def latitude_terms(row_index, lat_total):
    distance = jnp.minimum(row_index + 0.5, lat_total - row_index - 0.5)
    cosine_lat = jnp.sin(math.pi * distance / lat_total)
    sine_lat = -jnp.cos(math.pi * (row_index + 0.5) / lat_total)
    return (cosine_lat, sine_lat)


def tendencies(lat_padded, lon_padded, cos_ext, sine_lat, lat_total, lon_total):
    cosine_lat = cos_ext[1:-1]
    zonal_scale = (lon_total / (4.0 * lat_total) / cosine_lat)[:, None]
    metric = math.pi / lat_total * sine_lat / cosine_lat
    depth_lon, east_lon, north_lon = (lon_padded[0], lon_padded[1], lon_padded[2])
    depth_lat, east_lat, north_lat = (lat_padded[0], lat_padded[1], lat_padded[2])
    east = east_lon[:, 1:-1]
    north = north_lon[:, 1:-1]

    def zonal_change(field):
        return zonal_scale * (field[:, 2:] - field[:, :-2])

    def northward_change(field):
        return 0.5 * (field[2:] - field[:-2])

    mass_flux = depth_lat * north_lat * cos_ext[:, None]
    tend_depth = (
        -zonal_change(depth_lon * east_lon) - northward_change(mass_flux) / cosine_lat[:, None]
    )
    turning = coriolis * sine_lat[:, None] + metric[:, None] * east
    tend_east = (
        -east * zonal_change(east_lon)
        - north * northward_change(east_lat)
        + turning * north
        - gravity * zonal_change(depth_lon)
    )
    tend_north = (
        -east * zonal_change(north_lon)
        - north * northward_change(north_lat)
        - turning * east
        - gravity * northward_change(depth_lat)
    )
    return jnp.stack([tend_depth, tend_east, tend_north])


def angle_table(first_count, second_count, period):
    first_idx = jnp.arange(first_count, dtype=jnp.int32)
    second_idx = jnp.arange(second_count, dtype=jnp.int32)
    turns = first_idx[:, None] * second_idx[None, :] % period
    phase = turns.astype(jnp.float32) * (2.0 * math.pi / period)
    return (jnp.cos(phase), jnp.sin(phase))


def low_pass(signal, cutoff):
    count, length = signal.shape
    first = 1
    probe = 1
    while probe * probe <= length:
        if length % probe == 0:
            first = probe
        probe = probe + 1
    second = length // first
    cos_first, sin_first = angle_table(first, first, first)
    cos_second, sin_second = angle_table(second, second, second)
    cos_twist, sin_twist = angle_table(first, second, length)
    grid = signal.reshape(count, first, second)
    part_re = jnp.einsum("cpq,pk->ckq", grid, cos_first, precision=highest)
    part_im = -jnp.einsum("cpq,pk->ckq", grid, sin_first, precision=highest)
    twist_re = part_re * cos_twist + part_im * sin_twist
    twist_im = part_im * cos_twist - part_re * sin_twist
    spec_re = jnp.einsum("ckq,qm->ckm", twist_re, cos_second, precision=highest) + jnp.einsum(
        "ckq,qm->ckm", twist_im, sin_second, precision=highest
    )
    spec_im = jnp.einsum("ckq,qm->ckm", twist_im, cos_second, precision=highest) - jnp.einsum(
        "ckq,qm->ckm", twist_re, sin_second, precision=highest
    )
    wave = (
        jnp.arange(first, dtype=jnp.int32)[:, None]
        + first * jnp.arange(second, dtype=jnp.int32)[None, :]
    )
    limit = cutoff[:, None, None]
    keep = ((wave[None] <= limit) | (wave[None] >= length - limit)).astype(jnp.float32) * (
        1.0 / length
    )
    spec_re = spec_re * keep
    spec_im = spec_im * keep
    back_re = jnp.einsum("ckm,mq->ckq", spec_re, cos_second, precision=highest) - jnp.einsum(
        "ckm,mq->ckq", spec_im, sin_second, precision=highest
    )
    back_im = jnp.einsum("ckm,mq->ckq", spec_im, cos_second, precision=highest) + jnp.einsum(
        "ckm,mq->ckq", spec_re, sin_second, precision=highest
    )
    turn_re = back_re * cos_twist - back_im * sin_twist
    turn_im = back_im * cos_twist + back_re * sin_twist
    result = jnp.einsum("ckq,kp->cpq", turn_re, cos_first, precision=highest) - jnp.einsum(
        "ckq,kp->cpq", turn_im, sin_first, precision=highest
    )
    return result.reshape(count, length)


def per_device(state_now, state_old, polar_cutoff):
    lat_rows = state_now.shape[1]
    lon_cols = state_now.shape[2]
    lat_count = lax.axis_size("lat")
    lon_count = lax.axis_size("lon")
    lat_total = lat_rows * lat_count
    lon_total = lon_cols * lon_count
    lat_place = lax.axis_index("lat")
    lat_padded = padded(state_now, (("lat", 1),), 1, False)
    lon_padded = padded(state_now, (("lon", 2),), 1, True)
    row_index = (lat_place * lat_rows + jnp.arange(-1, lat_rows + 1, dtype=jnp.int32)).astype(
        jnp.float32
    )
    cos_ext, sin_ext = latitude_terms(row_index, lat_total)
    forcing = tendencies(lat_padded, lon_padded, cos_ext, sin_ext[1:-1], lat_total, lon_total)
    groups = lat_count * lon_count
    share = lat_rows // groups
    member = lax.axis_index(("lat", "lon"))
    south_cut = lax.dynamic_slice_in_dim(polar_cutoff, member * share, share)
    north_cut = lax.dynamic_slice_in_dim(polar_cutoff, lat_rows + member * share, share)
    band_cut = jnp.concatenate([south_cut, north_cut])
    block = lax.all_to_all(forcing, ("lat", "lon"), split_axis=1, concat_axis=2, tiled=True)
    items = block.shape[0]
    wide = block.shape[2]
    south_rows = block[:, :, :lon_total]
    north_rows = block[:, :, wide - lon_total :]
    polar_rows = jnp.concatenate([south_rows, north_rows], axis=1)
    smooth = low_pass(polar_rows.reshape(items * 2 * share, lon_total), jnp.tile(band_cut, items))
    smooth = smooth.reshape(items, 2 * share, lon_total)
    rebuilt = jnp.concatenate(
        [smooth[:, :share], block[:, :, lon_total : wide - lon_total], smooth[:, share:]], axis=2
    )
    filtered = lax.all_to_all(rebuilt, ("lat", "lon"), split_axis=2, concat_axis=1, tiled=True)
    return state_old + step_scale * filtered


NEAR = 32
FAR = 16
MAIN = 4 * LANES
ROWS = 16


def split_table(table):
    table = np.asarray(table, np.float32)
    high = table.astype(jnp.bfloat16)
    rest = table - high.astype(np.float32)
    middle = rest.astype(jnp.bfloat16)
    low = (rest - middle.astype(np.float32)).astype(jnp.bfloat16)
    return high, middle, low


def kernel_values(offset, total):
    safe = np.where(offset == 0, 1, offset)
    return np.where(offset == 0, 0.0, 1.0 / (total * np.sin(np.pi * safe / total)))


def stacked(table, cols):
    high, low, _ = split_table(table)
    zero = np.zeros((2 * LANES - 3 * (cols - MAIN), table.shape[1]), high.dtype)
    tail = [high[MAIN:], high[MAIN:], low[MAIN:], zero]
    return np.concatenate([high[:MAIN], high[:MAIN], *tail, low[:MAIN]])


def convolution_tables(cols, lon_count):
    total = cols * lon_count
    width = -(-cols // LANES) * LANES
    here = np.arange(cols)
    target, source = here[:, None], here[None, :]
    local = np.zeros((cols, width))
    local[:, :cols] = step_scale * kernel_values(target - source, total).T
    moments = np.zeros((cols, LANES))
    fields = np.zeros((lon_count, LANES, width))
    lon = np.arange(lon_count)
    places = [(-1, 0, NEAR), (1, NEAR, NEAR), (2, 2 * NEAR, FAR)]
    for step, start, rank in places:
        block = kernel_values(target - source + step * cols, total)
        left, scale, right = np.linalg.svd(block)
        moments[:, start : start + rank] = right[:rank].T
        back = step_scale * scale[:rank, None] * left[:, :rank].T
        for q in lon:
            origin = (q - step) % lon_count
            sign = 1.0 if q - origin == step else -1.0
            fields[q, start : start + rank, :cols] = sign * back
    near_high, near_low = [], []
    for q in lon:
        high, low, _ = split_table(fields[q])
        near_high.append(np.concatenate([high, high, low]))
    return stacked(local, cols), stacked(moments, cols), np.stack(near_high)


def phase_tables(cols, lon_count):
    total = cols * lon_count
    width = -(-cols // LANES) * LANES
    digit = LANES // 2
    coarse, fine = [], []
    for q in range(lon_count):
        m = q * cols + np.arange(cols)[None, :]
        for out, unit in ((coarse, digit), (fine, 1)):
            k = unit * np.arange(digit)[:, None]
            angle = np.pi * ((k * m) % (2 * total)) / total
            table = np.zeros((digit, 2 * width + LANES))
            table[:, :cols] = np.cos(angle)
            table[:, width : width + cols] = np.sin(angle)
            table[:, 2 * width :] = step_scale * k / total
            parts = split_table(table)
            out.append(np.concatenate([*parts, np.zeros_like(parts[0])]))
    return np.stack([np.stack(coarse), np.stack(fine)], axis=1)


def geometry_table(lat_total, lon_total):
    j = np.arange(lat_total, dtype=np.float64)

    def cosine(row):
        return np.sin(np.pi * np.minimum(row + 0.5, lat_total - row - 0.5) / lat_total)

    c = cosine(j)
    s = -np.cos(np.pi * (j + 0.5) / lat_total)
    table = np.zeros((lat_total, LANES))
    table[:, 0] = lon_total / (4.0 * lat_total * c)
    table[:, 1] = 0.5 * cosine(j + 1) / c
    table[:, 2] = 0.5 * cosine(j - 1) / c
    table[:, 3] = coriolis * s
    table[:, 4] = np.pi / lat_total * s / c
    return table.astype(np.float32)


def dot(a, b):
    return lax.dot_general(a, b, (((1,), (0,)), ((), ())), preferred_element_type=jnp.float32)


def high_low(value):
    high = value.astype(jnp.bfloat16)
    back = high.astype(jnp.float32)
    return high, back, value - back


def step_kernel(
    lat_count, lon_count, chunk,
    x_hbm, old_hbm, geo_hbm, cut_hbm, phase_hbm, local_hbm, moment_hbm, field_hbm, out_ref,
    old, xp, geo, cut_ref, phase, local, moment, field, wave, lhs, part, send, recv,
    col_send, col_recv, load_sem, table_sem, row_send_sem, row_recv_sem, col_send_sem,
    col_recv_sem, far_send, far_recv,
):
    rows, cols = out_ref.shape[1], out_ref.shape[2]
    chunks = rows // chunk
    groups = rows // SUB
    total = lon_count * cols
    tiles = -(-cols // LANES)
    width = tiles * LANES
    rest = cols % LANES
    lines = 3 * chunk
    lat = lax.axis_index("lat")
    lon = lax.axis_index("lon")
    west = lax.rem(lon + lon_count - 1, lon_count)
    east = lax.rem(lon + 1, lon_count)
    across = lax.rem(lon + 2, lon_count)
    polar = jnp.logical_or(lat == 0, lat == lat_count - 1)
    has_south = lat > 0
    has_north = lat < lat_count - 1

    def aligned(i):
        return pl.multiple_of(i, SUB)

    load = pltpu.make_async_copy(x_hbm, xp.at[:, pl.ds(SUB, rows), :], load_sem)
    load.start()
    first_loads = [
        pltpu.make_async_copy(geo_hbm.at[pl.ds(aligned(lat * rows), rows), :], geo, table_sem.at[0]),
        pltpu.make_async_copy(cut_hbm, cut_ref, table_sem.at[1]),
        pltpu.make_async_copy(phase_hbm.at[lon], phase, table_sem.at[2]),
    ]
    old_load = pltpu.make_async_copy(old_hbm, old, table_sem.at[3])
    late_loads = [
        pltpu.make_async_copy(moment_hbm, moment, table_sem.at[4]),
        pltpu.make_async_copy(local_hbm, local, table_sem.at[5]),
        pltpu.make_async_copy(field_hbm.at[lon], field, table_sem.at[6]),
    ]
    for copy in [*first_loads, old_load, *late_loads]:
        copy.start()

    barrier = pltpu.get_barrier_semaphore()
    for k in range(1, lon_count):
        pl.semaphore_signal(
            barrier, inc=1, device_id={"lon": lax.rem(lon + k, lon_count)}, device_id_type=MESH
        )

    @pl.when(has_south)
    def _():
        pl.semaphore_signal(barrier, inc=1, device_id={"lat": lat - 1}, device_id_type=MESH)

    @pl.when(has_north)
    def _():
        pl.semaphore_signal(barrier, inc=1, device_id={"lat": lat + 1}, device_id_type=MESH)

    load.wait()
    lane = lax.broadcasted_iota(jnp.int32, (SUB, LANES), 1)
    lane2 = lax.broadcasted_iota(jnp.int32, (ROWS, LANES), 1)

    packed = [jnp.zeros((SUB, LANES), jnp.float32) for _ in range(6)]
    for g in range(groups):
        here = lane == g
        for c in range(3):
            block = slice(SUB + g * SUB, 2 * SUB + g * SUB)
            packed[2 * c] = jnp.where(here, xp[c, block, 0:1], packed[2 * c])
            packed[2 * c + 1] = jnp.where(here, xp[c, block, cols - 1 : cols], packed[2 * c + 1])
    for c in range(3):
        col_send[0, c] = packed[2 * c]
        col_send[1, c] = packed[2 * c + 1]

    pl.semaphore_wait(
        barrier, lon_count - 1 + has_south.astype(jnp.int32) + has_north.astype(jnp.int32)
    )

    def to_south():
        return pltpu.make_async_remote_copy(
            src_ref=x_hbm.at[:, pl.ds(0, SUB), :], dst_ref=xp.at[:, pl.ds(rows + SUB, SUB), :],
            send_sem=row_send_sem.at[0], recv_sem=row_recv_sem.at[0],
            device_id={"lat": lat - 1}, device_id_type=MESH,
        )

    def to_north():
        return pltpu.make_async_remote_copy(
            src_ref=x_hbm.at[:, pl.ds(rows - SUB, SUB), :], dst_ref=xp.at[:, pl.ds(0, SUB), :],
            send_sem=row_send_sem.at[1], recv_sem=row_recv_sem.at[1],
            device_id={"lat": lat + 1}, device_id_type=MESH,
        )

    @pl.when(has_south)
    def _():
        to_south().start()

    @pl.when(has_north)
    def _():
        to_north().start()

    zero_rows = jnp.zeros((3, SUB, cols), jnp.float32)

    @pl.when(jnp.logical_not(has_south))
    def _():
        xp[:, 0:SUB, :] = zero_rows

    @pl.when(jnp.logical_not(has_north))
    def _():
        xp[:, rows + SUB : rows + 2 * SUB, :] = zero_rows

    def column_copy(side, target):
        return pltpu.make_async_remote_copy(
            src_ref=col_send.at[side], dst_ref=col_recv.at[side],
            send_sem=col_send_sem.at[side], recv_sem=col_recv_sem.at[side],
            device_id={"lon": target}, device_id_type=MESH,
        )

    first_out = column_copy(0, west)
    last_out = column_copy(1, east)
    first_out.start()
    last_out.start()
    for copy in first_loads:
        copy.wait()

    def halos_arrive():
        first_out.wait()
        last_out.wait()

        @pl.when(has_south)
        def _():
            to_south().wait_send()
            to_north().wait_recv()

        @pl.when(has_north)
        def _():
            to_north().wait_send()
            to_south().wait_recv()

    def tile_of(t):
        return slice(t * LANES, min((t + 1) * LANES, cols))

    def read(ref, c, start, count, t):
        value = ref[c, pl.ds(aligned(start), count), tile_of(t)]
        if t == tiles - 1 and rest:
            value = jnp.concatenate([value, jnp.zeros((count, LANES - rest), jnp.float32)], axis=1)
        return value

    def edge(side, c, b, place):
        both = []
        for i in range(ROWS // SUB):
            g = b * (ROWS // SUB) + i
            both.append(pltpu.roll(col_recv[side, c], lax.rem(place + LANES - g, LANES), 1))
        return jnp.concatenate(both, axis=0)

    def tendency_block(b):
        start = aligned(b * ROWS)
        terms = geo[pl.ds(start, ROWS), :]
        zonal, up, down, turn, metric = [terms[:, i : i + 1] for i in range(5)]
        here = [[read(xp, c, start + SUB, ROWS, t) for t in range(tiles)] for c in range(3)]
        ahead = [[pltpu.roll(v, LANES - 1, 1) for v in here[c]] for c in range(3)]
        behind = [[pltpu.roll(v, 1, 1) for v in here[c]] for c in range(3)]
        last_lane = (rest or LANES) - 1
        values = []
        for t in range(tiles):
            east_of, west_of, north, south = [], [], [], []
            for c in range(3):
                if t < tiles - 1:
                    east_of.append(jnp.where(lane2 == LANES - 1, ahead[c][t + 1], ahead[c][t]))
                else:
                    right = edge(0, c, b, last_lane)
                    east_of.append(jnp.where(lane2 == last_lane, right, ahead[c][t]))
                left = behind[c][t - 1] if t > 0 else edge(1, c, b, 0)
                west_of.append(jnp.where(lane2 == 0, left, behind[c][t]))
                after = read(xp, c, start + SUB + ROWS, SUB, t)
                before = read(xp, c, start, SUB, t)
                north.append(pltpu.roll(jnp.concatenate([here[c][t], after], axis=0), ROWS + SUB - 1, 0)[:ROWS])
                south.append(pltpu.roll(jnp.concatenate([before, here[c][t]], axis=0), 1, 0)[SUB:])
            u, v = here[1][t], here[2][t]
            t_h = -zonal * (east_of[0] * east_of[1] - west_of[0] * west_of[1]) - (
                up * (north[0] * north[2]) - down * (south[0] * south[2])
            )
            turning = turn + metric * u
            zu = zonal * u
            hv = 0.5 * v
            t_u = (
                turning * v - zu * (east_of[1] - west_of[1]) - hv * (north[1] - south[1])
                - zonal * (east_of[0] - west_of[0])
            )
            t_v = (
                -turning * u - zu * (east_of[2] - west_of[2]) - hv * (north[2] - south[2])
                - 0.5 * (north[0] - south[0])
            )
            values.append((t_h, t_u, t_v))
        return start, values

    def put(c, start, t, value):
        out_ref[c, pl.ds(start, ROWS), tile_of(t)] = value[:, : min(LANES, cols - t * LANES)]

    @pl.when(polar)
    def _():
        cut_start = jnp.where(lat == 0, 0, rows)
        cuts = cut_ref[...].astype(jnp.float32)[None, :]

        @pl.loop(0, rows // chunk)
        def _(i):
            start = pl.multiple_of(i * chunk, chunk)
            wanted = cut_start + start + lax.broadcasted_iota(jnp.int32, (chunk, 2 * rows), 0)
            hit = wanted == lax.broadcasted_iota(jnp.int32, (chunk, 2 * rows), 1)
            limit = jnp.sum(jnp.where(hit, cuts, 0.0), axis=1, keepdims=True)
            turns = jnp.minimum(2.0 * limit + 1.0, float(total))
            digit = LANES // 2
            upper = jnp.floor(turns * (1.0 / digit))
            lower = turns - digit * upper
            place = lax.rem(lax.broadcasted_iota(jnp.int32, (chunk, LANES), 1), digit).astype(jnp.float32)

            def lookup(value, k):
                found = (place == value).astype(jnp.bfloat16)
                return dot(jnp.concatenate([found, found], axis=1), phase[k])

            a, z = lookup(upper, 0), lookup(lower, 1)
            at = pl.ds(start, chunk)
            wave[at, :width] = a[:, :width] * z[:, :width] - a[:, width : 2 * width] * z[:, width : 2 * width]
            wave[at, width : 2 * width] = (
                a[:, width : 2 * width] * z[:, :width] + a[:, :width] * z[:, width : 2 * width]
            )
            wave[at, 2 * width :] = a[:, 2 * width :] + z[:, 2 * width :]

    halos_arrive()
    old_load.wait()
    for copy in late_loads:
        copy.wait()

    @pl.when(jnp.logical_not(polar))
    def _():
        @pl.loop(0, rows // ROWS)
        def _(b):
            start, values = tendency_block(b)
            for c in range(3):
                for t in range(tiles):
                    put(c, start, t, read(old, c, start, ROWS, t) + step_scale * values[t][c])

    span_near = lines // 2
    span_far = lines // 4
    spans = [(0, span_near), (span_near, span_near), (2 * span_near, span_far)]

    def far_copy(i, k):
        first, count = spans[k]
        return pltpu.make_async_remote_copy(
            src_ref=send.at[i, pl.ds(first, count), :], dst_ref=recv.at[i, pl.ds(first, count), :],
            send_sem=far_send.at[i, k], recv_sem=far_recv.at[i, k],
            device_id={"lon": (west, east, across)[k]}, device_id_type=MESH,
        )

    def place_of(i):
        return jnp.where(lat == 0, i, chunks - 1 - i)

    def operand(i):
        value = lhs[i]
        return jnp.concatenate([value, value[:, :MAIN]], axis=1)

    def turned(value, shift):
        shift = shift % LANES
        return pltpu.roll(value, shift, 1) if shift else value

    def merged(slots, size):
        at = lax.broadcasted_iota(jnp.int32, slots[0].shape, 1)
        total_value = slots[-1]
        for s in range(len(slots) - 2, -1, -1):
            total_value = jnp.where(at < (s + 1) * size, slots[s], total_value)
        return total_value

    @pl.when(polar)
    def _():
        @pl.loop(0, chunks)
        def _(i):
            chunk_at = place_of(i) * chunk

            @pl.loop(0, chunk // ROWS)
            def _(b):
                start, values = tendency_block(chunk_at // ROWS + b)
                at = pl.ds(start, ROWS)
                own = wave[at, 2 * width :]
                for t in range(tiles):
                    turn_cos = wave[at, t * LANES : (t + 1) * LANES]
                    turn_sin = wave[at, width + t * LANES : width + (t + 1) * LANES]
                    for c in range(3):
                        value = values[t][c]
                        put(c, start, t, read(old, c, start, ROWS, t) + own * value)
                        for channel, factor in enumerate((turn_cos, turn_sin)):
                            line = pl.ds(pl.multiple_of(channel * lines + c * chunk + b * ROWS, ROWS), ROWS)
                            high, back, low = high_low(value * factor)
                            if t < tiles - 1:
                                lhs[i, line, t * LANES : (t + 1) * LANES] = high
                                lhs[i, line, MAIN + t * LANES : MAIN + (t + 1) * LANES] = low.astype(jnp.bfloat16)
                            else:
                                mixed = jnp.where(lane2 < rest, back, pltpu.roll(low, rest, 1))
                                lhs[i, line, 2 * MAIN : 2 * MAIN + LANES] = mixed.astype(jnp.bfloat16)
                                lhs[i, line, 2 * MAIN + LANES :] = high

            moments = dot(operand(i), moment[...])
            for k, (first, size) in enumerate(((0, NEAR), (NEAR, NEAR), (2 * NEAR, FAR))):
                count = spans[k][1]
                slots = []
                for s in range(LANES // size):
                    origin = (s % 2) * lines + (s // 2) * count
                    slots.append(turned(moments[origin : origin + count], s * size - first))
                send[i, pl.ds(spans[k][0], count), :] = merged(slots, size)
                far_copy(i, k).start()

        @pl.loop(0, chunks)
        def _(i):
            part[i] = dot(operand(i), local[...])

        @pl.loop(0, chunks)
        def _(i):
            for k in range(3):
                far_copy(i, k).wait_recv()
            start = pl.multiple_of(place_of(i) * chunk, ROWS)
            gathered = []
            for k, (first, size) in enumerate(((0, NEAR), (NEAR, NEAR), (2 * NEAR, FAR))):
                value = recv[i, pl.ds(spans[k][0], spans[k][1]), :]
                slots = [turned(value, first - s * size) for s in range(LANES // size)]
                gathered.append(jnp.concatenate(slots[0::2] + slots[1::2], axis=0))
            at_lane = lax.broadcasted_iota(jnp.int32, (2 * lines, LANES), 1)
            coming = jnp.where(
                at_lane < NEAR, gathered[0],
                jnp.where(at_lane < 2 * NEAR, gathered[1], jnp.where(at_lane < 2 * NEAR + FAR, gathered[2], 0.0)),
            )
            high, _, low = high_low(coming)
            whole = part[i] + dot(jnp.concatenate([high, low.astype(jnp.bfloat16), high], axis=1), field[...])
            at = pl.ds(start, chunk)
            turn_cos = wave[at, :cols]
            turn_sin = wave[at, width : width + cols]
            for c in range(3):
                by_cos = whole[c * chunk : (c + 1) * chunk, :cols]
                by_sin = whole[lines + c * chunk : lines + (c + 1) * chunk, :cols]
                out_ref[c, at, :] = out_ref[c, at, :] + turn_sin * by_cos - turn_cos * by_sin

        @pl.loop(0, chunks)
        def _(i):
            for k in range(3):
                far_copy(i, k).wait_send()


def fused_step(mesh_shape, tables, state_now, state_old, polar_cutoff):
    lat_count, lon_count = mesh_shape
    comps, rows, cols = state_now.shape
    chunk = chunk_rows(rows)
    chunks = rows // chunk
    lines = comps * chunk
    width = -(-cols // LANES) * LANES
    geo, phase, local, moment, field = tables
    operands = [
        pltpu.with_memory_space_constraint(jnp.asarray(a), pltpu.HBM)
        for a in (state_now, state_old, geo, polar_cutoff, phase, local, moment, field)
    ]
    hbm_spec = pl.BlockSpec(memory_space=pltpu.HBM)
    vmem_spec = pl.BlockSpec(memory_space=pltpu.VMEM)
    dma = pltpu.SemaphoreType.DMA
    exchange = pltpu.VMEM((chunks, lines // 2 * 2 + lines // 4, LANES), jnp.float32)
    return pl.pallas_call(
        functools.partial(step_kernel, lat_count, lon_count, chunk),
        out_shape=jax.ShapeDtypeStruct(state_now.shape, jnp.float32),
        in_specs=[hbm_spec] * 8,
        out_specs=vmem_spec,
        scratch_shapes=[
            pltpu.VMEM((comps, rows, cols), jnp.float32),
            pltpu.VMEM((comps, rows + 2 * SUB, cols), jnp.float32),
            pltpu.VMEM((rows, LANES), jnp.float32),
            pltpu.VMEM((2 * rows,), jnp.int32),
            pltpu.VMEM(phase.shape[1:], jnp.bfloat16),
            pltpu.VMEM(local.shape, jnp.bfloat16),
            pltpu.VMEM(moment.shape, jnp.bfloat16),
            pltpu.VMEM(field.shape[1:], jnp.bfloat16),
            pltpu.VMEM((rows, 2 * width + LANES), jnp.float32),
            pltpu.VMEM((chunks, 2 * lines, 2 * MAIN + 2 * LANES), jnp.bfloat16),
            pltpu.VMEM((chunks, 2 * lines, width), jnp.float32),
            exchange,
            exchange,
            pltpu.VMEM((2, comps, SUB, LANES), jnp.float32),
            pltpu.VMEM((2, comps, SUB, LANES), jnp.float32),
            dma, dma((7,)), dma((2,)), dma((2,)), dma((2,)), dma((2,)),
            dma((chunks, 3)), dma((chunks, 3)),
        ],
        compiler_params=pltpu.CompilerParams(
            collective_id=0, has_side_effects=True, vmem_limit_bytes=56 * 1024 * 1024
        ),
    )(*operands)


def chunk_rows(rows):
    return rows // 3 if rows % 96 == 0 else 0


def solution(mesh):
    lat_count, lon_count = mesh.shape["lat"], mesh.shape["lon"]

    def step(state_now, state_old, polar_cutoff):
        comps, lat_total, lon_total = state_now.shape
        rows, cols = lat_total // lat_count, lon_total // lon_count
        fits = (
            lat_count == 4 and lon_count == 4 and lat_total == 4 * rows and chunk_rows(rows) > 0
            and cols == MAIN + LANES // 2 and rows // SUB <= LANES and comps == 3 * mesh.shape["ens"]
        )
        body = per_device
        if fits:
            tables = (
                geometry_table(lat_total, lon_total), phase_tables(cols, lon_count),
                *convolution_tables(cols, lon_count),
            )
            body = functools.partial(fused_step, (lat_count, lon_count), tables)
        return jax.shard_map(
            body,
            mesh=mesh,
            in_specs=(P("ens", "lat", "lon"), P("ens", "lat", "lon"), P()),
            out_specs=P("ens", "lat", "lon"),
            check_vma=False,
        )(state_now, state_old, polar_cutoff)

    return step
```

```python
import functools
import math

import jax
import jax.numpy as jnp
import numpy as np
from jax import lax
from jax.experimental import pallas as pl
from jax.experimental.pallas import tpu as pltpu
from jax.sharding import PartitionSpec as P

LANES = 128
SUB = 8
MESH = pl.DeviceIdType.MESH
step_scale = 0.2
coriolis = 2.0
gravity = 1.0
highest = lax.Precision.HIGHEST


def padded(value, sides, width, wrap):
    for axis, dim in sides:
        devices, length = (lax.axis_size(axis), value.shape[dim])
        up = [(i, (i + 1) % devices) for i in range(devices if wrap else devices - 1)]
        down = [(j, i) for i, j in up]
        last = lax.slice_in_dim(value, length - width, length, axis=dim)
        leading = lax.slice_in_dim(value, 0, width, axis=dim)
        before = lax.ppermute(last, axis, up)
        after = lax.ppermute(leading, axis, down)
        value = jnp.concatenate([before, value, after], axis=dim)
    return value


def latitude_terms(row_index, lat_total):
    distance = jnp.minimum(row_index + 0.5, lat_total - row_index - 0.5)
    cosine_lat = jnp.sin(math.pi * distance / lat_total)
    sine_lat = -jnp.cos(math.pi * (row_index + 0.5) / lat_total)
    return (cosine_lat, sine_lat)


def tendencies(lat_padded, lon_padded, cos_ext, sine_lat, lat_total, lon_total):
    cosine_lat = cos_ext[1:-1]
    zonal_scale = (lon_total / (4.0 * lat_total) / cosine_lat)[:, None]
    metric = math.pi / lat_total * sine_lat / cosine_lat
    depth_lon, east_lon, north_lon = (lon_padded[0], lon_padded[1], lon_padded[2])
    depth_lat, east_lat, north_lat = (lat_padded[0], lat_padded[1], lat_padded[2])
    east = east_lon[:, 1:-1]
    north = north_lon[:, 1:-1]

    def zonal_change(field):
        return zonal_scale * (field[:, 2:] - field[:, :-2])

    def northward_change(field):
        return 0.5 * (field[2:] - field[:-2])

    mass_flux = depth_lat * north_lat * cos_ext[:, None]
    tend_depth = (
        -zonal_change(depth_lon * east_lon) - northward_change(mass_flux) / cosine_lat[:, None]
    )
    turning = coriolis * sine_lat[:, None] + metric[:, None] * east
    tend_east = (
        -east * zonal_change(east_lon)
        - north * northward_change(east_lat)
        + turning * north
        - gravity * zonal_change(depth_lon)
    )
    tend_north = (
        -east * zonal_change(north_lon)
        - north * northward_change(north_lat)
        - turning * east
        - gravity * northward_change(depth_lat)
    )
    return jnp.stack([tend_depth, tend_east, tend_north])


def angle_table(first_count, second_count, period):
    first_idx = jnp.arange(first_count, dtype=jnp.int32)
    second_idx = jnp.arange(second_count, dtype=jnp.int32)
    turns = first_idx[:, None] * second_idx[None, :] % period
    phase = turns.astype(jnp.float32) * (2.0 * math.pi / period)
    return (jnp.cos(phase), jnp.sin(phase))


def low_pass(signal, cutoff):
    count, length = signal.shape
    first = 1
    probe = 1
    while probe * probe <= length:
        if length % probe == 0:
            first = probe
        probe = probe + 1
    second = length // first
    cos_first, sin_first = angle_table(first, first, first)
    cos_second, sin_second = angle_table(second, second, second)
    cos_twist, sin_twist = angle_table(first, second, length)
    grid = signal.reshape(count, first, second)
    part_re = jnp.einsum("cpq,pk->ckq", grid, cos_first, precision=highest)
    part_im = -jnp.einsum("cpq,pk->ckq", grid, sin_first, precision=highest)
    twist_re = part_re * cos_twist + part_im * sin_twist
    twist_im = part_im * cos_twist - part_re * sin_twist
    spec_re = jnp.einsum("ckq,qm->ckm", twist_re, cos_second, precision=highest) + jnp.einsum(
        "ckq,qm->ckm", twist_im, sin_second, precision=highest
    )
    spec_im = jnp.einsum("ckq,qm->ckm", twist_im, cos_second, precision=highest) - jnp.einsum(
        "ckq,qm->ckm", twist_re, sin_second, precision=highest
    )
    wave = (
        jnp.arange(first, dtype=jnp.int32)[:, None]
        + first * jnp.arange(second, dtype=jnp.int32)[None, :]
    )
    limit = cutoff[:, None, None]
    keep = ((wave[None] <= limit) | (wave[None] >= length - limit)).astype(jnp.float32) * (
        1.0 / length
    )
    spec_re = spec_re * keep
    spec_im = spec_im * keep
    back_re = jnp.einsum("ckm,mq->ckq", spec_re, cos_second, precision=highest) - jnp.einsum(
        "ckm,mq->ckq", spec_im, sin_second, precision=highest
    )
    back_im = jnp.einsum("ckm,mq->ckq", spec_im, cos_second, precision=highest) + jnp.einsum(
        "ckm,mq->ckq", spec_re, sin_second, precision=highest
    )
    turn_re = back_re * cos_twist - back_im * sin_twist
    turn_im = back_im * cos_twist + back_re * sin_twist
    result = jnp.einsum("ckq,kp->cpq", turn_re, cos_first, precision=highest) - jnp.einsum(
        "ckq,kp->cpq", turn_im, sin_first, precision=highest
    )
    return result.reshape(count, length)


def per_device(state_now, state_old, polar_cutoff):
    lat_rows = state_now.shape[1]
    lon_cols = state_now.shape[2]
    lat_count = lax.axis_size("lat")
    lon_count = lax.axis_size("lon")
    lat_total = lat_rows * lat_count
    lon_total = lon_cols * lon_count
    lat_place = lax.axis_index("lat")
    lat_padded = padded(state_now, (("lat", 1),), 1, False)
    lon_padded = padded(state_now, (("lon", 2),), 1, True)
    row_index = (lat_place * lat_rows + jnp.arange(-1, lat_rows + 1, dtype=jnp.int32)).astype(
        jnp.float32
    )
    cos_ext, sin_ext = latitude_terms(row_index, lat_total)
    forcing = tendencies(lat_padded, lon_padded, cos_ext, sin_ext[1:-1], lat_total, lon_total)
    groups = lat_count * lon_count
    share = lat_rows // groups
    member = lax.axis_index(("lat", "lon"))
    south_cut = lax.dynamic_slice_in_dim(polar_cutoff, member * share, share)
    north_cut = lax.dynamic_slice_in_dim(polar_cutoff, lat_rows + member * share, share)
    band_cut = jnp.concatenate([south_cut, north_cut])
    block = lax.all_to_all(forcing, ("lat", "lon"), split_axis=1, concat_axis=2, tiled=True)
    items = block.shape[0]
    wide = block.shape[2]
    south_rows = block[:, :, :lon_total]
    north_rows = block[:, :, wide - lon_total :]
    polar_rows = jnp.concatenate([south_rows, north_rows], axis=1)
    smooth = low_pass(polar_rows.reshape(items * 2 * share, lon_total), jnp.tile(band_cut, items))
    smooth = smooth.reshape(items, 2 * share, lon_total)
    rebuilt = jnp.concatenate(
        [smooth[:, :share], block[:, :, lon_total : wide - lon_total], smooth[:, share:]], axis=2
    )
    filtered = lax.all_to_all(rebuilt, ("lat", "lon"), split_axis=2, concat_axis=1, tiled=True)
    return state_old + step_scale * filtered


NEAR = 32
FAR = 16
MAIN = 4 * LANES
ROWS = 16
EDGE = 2 * NEAR + FAR


def split_table(table):
    table = np.asarray(table, np.float32)
    high = table.astype(jnp.bfloat16)
    rest = table - high.astype(np.float32)
    middle = rest.astype(jnp.bfloat16)
    low = (rest - middle.astype(np.float32)).astype(jnp.bfloat16)
    return high, middle, low


def kernel_values(offset, total):
    safe = np.where(offset == 0, 1, offset)
    return np.where(offset == 0, 0.0, 1.0 / (total * np.sin(np.pi * safe / total)))


def stacked(table, cols):
    high, low, _ = split_table(table)
    zero = np.zeros((2 * LANES - 3 * (cols - MAIN), table.shape[1]), high.dtype)
    tail = [high[MAIN:], high[MAIN:], low[MAIN:], zero]
    return np.concatenate([high[:MAIN], high[:MAIN], *tail, low[:MAIN]])


def edge_columns(cols, lon_count):
    start = np.arange(lon_count) * cols
    return np.stack([start, start + cols - 1], axis=1).reshape(-1)


def convolution_tables(cols, lon_count):
    total = cols * lon_count
    width = -(-cols // LANES) * LANES
    here = np.arange(cols)
    target, source = here[:, None], here[None, :]
    local = np.zeros((cols, width))
    local[:, :cols] = step_scale * kernel_values(target - source, total).T
    moments = np.zeros((cols, LANES))
    fields = np.zeros((lon_count, LANES, width))
    lon = np.arange(lon_count)
    edge = edge_columns(cols, lon_count)
    places = [(-1, 0, NEAR), (1, NEAR, NEAR), (2, 2 * NEAR, FAR)]
    for step, start, rank in places:
        block = kernel_values(target - source + step * cols, total)
        left, scale, right = np.linalg.svd(block)
        moments[:, start : start + rank] = right[:rank].T
        back = step_scale * scale[:rank, None] * left[:, :rank].T
        for q in lon:
            origin = (q - step) % lon_count
            sign = 1.0 if q - origin == step else -1.0
            fields[q, start : start + rank, :cols] = sign * back
    piled = []
    for q in lon:
        offset = q * cols + here[None, :] - edge[:, None]
        fields[q, EDGE : EDGE + len(edge), :cols] = step_scale * kernel_values(offset, total)
        high, low, _ = split_table(fields[q])
        piled.append(np.concatenate([high, high, low]))
    return stacked(local, cols), stacked(moments, cols), np.stack(piled)


def phase_tables(cols, lon_count):
    total = cols * lon_count
    width = -(-cols // LANES) * LANES
    digit = LANES // 2
    coarse, fine = [], []
    edge = edge_columns(cols, lon_count)
    at_edge = MAIN + EDGE + np.arange(len(edge))
    for q in range(lon_count):
        m = q * cols + np.arange(cols)[None, :]
        for out, unit in ((coarse, digit), (fine, 1)):
            k = unit * np.arange(digit)[:, None]
            table = np.zeros((digit, 2 * width + LANES))
            for columns, places in ((m, np.arange(cols)), (edge[None, :], at_edge)):
                angle = np.pi * ((k * columns) % (2 * total)) / total
                table[:, places] = np.cos(angle)
                table[:, width + places] = np.sin(angle)
            table[:, 2 * width :] = step_scale * k / total
            parts = split_table(table)
            out.append(np.concatenate([*parts, np.zeros_like(parts[0])]))
    return np.stack([np.stack(coarse), np.stack(fine)], axis=1)


def geometry_table(lat_total, lon_total):
    j = np.arange(lat_total, dtype=np.float64)

    def cosine(row):
        return np.sin(np.pi * np.minimum(row + 0.5, lat_total - row - 0.5) / lat_total)

    c = cosine(j)
    s = -np.cos(np.pi * (j + 0.5) / lat_total)
    table = np.zeros((lat_total, LANES))
    table[:, 0] = lon_total / (4.0 * lat_total * c)
    table[:, 1] = 0.5 * cosine(j + 1) / c
    table[:, 2] = 0.5 * cosine(j - 1) / c
    table[:, 3] = coriolis * s
    table[:, 4] = np.pi / lat_total * s / c
    return table.astype(np.float32)


def edge_scale(geo, lat_count, lon_count):
    rows = len(geo) // lat_count
    edges = 2 * lon_count
    per = LANES // edges
    count = -(-(rows // SUB) // per)
    table = np.zeros((lat_count, count, SUB, LANES), np.float32)
    for lat in range(lat_count):
        for g in range(rows // SUB):
            zonal = geo[lat * rows + g * SUB : lat * rows + (g + 1) * SUB, 0]
            for k in range(edges):
                table[lat, g // per, :, g % per * edges + k] = zonal if k % 2 == 0 else -zonal
    return table


def dot(a, b):
    return lax.dot_general(a, b, (((1,), (0,)), ((), ())), preferred_element_type=jnp.float32)


def high_low(value):
    high = value.astype(jnp.bfloat16)
    back = high.astype(jnp.float32)
    return high, back, value - back


def step_kernel(
    lat_count, lon_count, chunk,
    x_hbm, old_hbm, geo_hbm, scale_hbm, cut_hbm, phase_hbm, local_hbm, moment_hbm, field_hbm, out_ref,
    old, xp, geo, scale, cut_ref, phase, local, moment, field, wave, lhs, part, send, recv,
    edge_send, edge_recv, delta, load_sem, table_sem, row_send_sem, row_recv_sem, edge_send_sem,
    edge_recv_sem, far_send, far_recv,
):
    rows, cols = out_ref.shape[1], out_ref.shape[2]
    chunks = rows // chunk
    blocks = rows // ROWS
    per_chunk = chunk // ROWS
    groups = rows // SUB
    total = lon_count * cols
    tiles = -(-cols // LANES)
    width = tiles * LANES
    rest = cols % LANES
    lines = 3 * chunk
    edges = 2 * lon_count
    edge_groups = LANES // edges
    edge_vregs = scale.shape[0]
    lat = lax.axis_index("lat")
    lon = lax.axis_index("lon")
    west = lax.rem(lon + lon_count - 1, lon_count)
    east = lax.rem(lon + 1, lon_count)
    across = lax.rem(lon + 2, lon_count)
    polar = jnp.logical_or(lat == 0, lat == lat_count - 1)
    has_south = lat > 0
    has_north = lat < lat_count - 1

    def aligned(i):
        return pl.multiple_of(i, SUB)

    load = pltpu.make_async_copy(x_hbm, xp.at[:, pl.ds(SUB, rows), :], load_sem)
    load.start()
    geo_load = pltpu.make_async_copy(
        geo_hbm.at[pl.ds(aligned(lat * rows), rows), :], geo, table_sem.at[0]
    )
    wave_loads = [
        pltpu.make_async_copy(cut_hbm, cut_ref, table_sem.at[1]),
        pltpu.make_async_copy(phase_hbm.at[lon], phase, table_sem.at[2]),
    ]
    old_load = pltpu.make_async_copy(old_hbm, old, table_sem.at[3])
    moment_load = pltpu.make_async_copy(moment_hbm, moment, table_sem.at[4])
    local_load = pltpu.make_async_copy(local_hbm, local, table_sem.at[5])
    field_load = pltpu.make_async_copy(field_hbm.at[lon], field, table_sem.at[6])
    scale_load = pltpu.make_async_copy(scale_hbm.at[lat], scale, table_sem.at[7])
    for copy in [geo_load, *wave_loads, old_load, moment_load, scale_load, local_load, field_load]:
        copy.start()

    barrier = pltpu.get_barrier_semaphore()
    for k in range(1, lon_count):
        pl.semaphore_signal(
            barrier, inc=1, device_id={"lon": lax.rem(lon + k, lon_count)}, device_id_type=MESH
        )

    @pl.when(has_south)
    def _():
        pl.semaphore_signal(barrier, inc=1, device_id={"lat": lat - 1}, device_id_type=MESH)

    @pl.when(has_north)
    def _():
        pl.semaphore_signal(barrier, inc=1, device_id={"lat": lat + 1}, device_id_type=MESH)

    load.wait()
    lane = lax.broadcasted_iota(jnp.int32, (SUB, LANES), 1)
    lane2 = lax.broadcasted_iota(jnp.int32, (ROWS, LANES), 1)
    sub = lax.broadcasted_iota(jnp.int32, (SUB, LANES), 0)

    for c in range(3):
        for w in range(edge_vregs):
            packed = jnp.zeros((SUB, LANES), jnp.float32)
            for g in range(w * edge_groups, min((w + 1) * edge_groups, groups)):
                block = slice(SUB + g * SUB, 2 * SUB + g * SUB)
                at = g % edge_groups * edges
                packed = jnp.where(lane == at, xp[c, block, 0:1], packed)
                packed = jnp.where(lane == at + 1, xp[c, block, cols - 1 : cols], packed)
            edge_send[c, w] = pltpu.roll(packed, 2 * lon, 1)

    def to_south():
        return pltpu.make_async_remote_copy(
            src_ref=x_hbm.at[:, pl.ds(0, SUB), :], dst_ref=xp.at[:, pl.ds(rows + SUB, SUB), :],
            send_sem=row_send_sem.at[0], recv_sem=row_recv_sem.at[0],
            device_id={"lat": lat - 1}, device_id_type=MESH,
        )

    def to_north():
        return pltpu.make_async_remote_copy(
            src_ref=x_hbm.at[:, pl.ds(rows - SUB, SUB), :], dst_ref=xp.at[:, pl.ds(0, SUB), :],
            send_sem=row_send_sem.at[1], recv_sem=row_recv_sem.at[1],
            device_id={"lat": lat + 1}, device_id_type=MESH,
        )

    zero_rows = jnp.zeros((3, SUB, cols), jnp.float32)

    @pl.when(jnp.logical_not(has_south))
    def _():
        xp[:, 0:SUB, :] = zero_rows

    @pl.when(jnp.logical_not(has_north))
    def _():
        xp[:, rows + SUB : rows + 2 * SUB, :] = zero_rows

    def edge_copy(k, source):
        target = lax.rem(source + k, lon_count)
        return pltpu.make_async_remote_copy(
            src_ref=edge_send, dst_ref=edge_recv.at[k],
            send_sem=edge_send_sem.at[k], recv_sem=edge_recv_sem.at[k],
            device_id={"lon": target}, device_id_type=MESH,
        )

    def neighbours_enter():
        pl.semaphore_wait(
            barrier, lon_count - 1 + has_south.astype(jnp.int32) + has_north.astype(jnp.int32)
        )

        @pl.when(has_south)
        def _():
            to_south().start()

        @pl.when(has_north)
        def _():
            to_north().start()

        for k in range(1, lon_count):
            edge_copy(k, lon).start()

    def halos_arrive():
        @pl.when(has_south)
        def _():
            to_south().wait_send()
            to_north().wait_recv()

        @pl.when(has_north)
        def _():
            to_north().wait_send()
            to_south().wait_recv()

    def edges_arrive():
        for k in range(1, lon_count):
            edge_copy(k, lon).wait()
        scale_load.wait()
        k_of = lax.rem(lane, edges)

        def beside(value):
            plus = pltpu.roll(value, 1, 1)
            minus = pltpu.roll(value, LANES - 1, 1)
            last = pltpu.roll(value, LANES - edges + 1, 1)
            first = pltpu.roll(value, edges - 1, 1)
            inner = jnp.where(lax.rem(k_of, 2) == 0, plus, minus)
            return jnp.where(k_of == 0, last, jnp.where(k_of == edges - 1, first, inner))

        for w in range(edge_vregs):
            own = [edge_send[c, w] for c in range(3)]
            for c in range(3):
                for k in range(1, lon_count):
                    own[c] = own[c] + edge_recv[k, c, w]
            h, u, v = [beside(value) for value in own]
            factor = scale[w]
            delta[0, w] = factor * (h * u)
            delta[1, w] = factor * (own[1] * u + h)
            delta[2, w] = factor * (own[1] * v)

    def edge_terms(c, start, count):
        terms = []
        for i in range(count // SUB):
            g = start // SUB + i
            value = delta[c, g // edge_groups]
            shift = lax.rem(EDGE + LANES - lax.rem(g, edge_groups) * edges, LANES)
            value = pltpu.roll(value, shift, 1)
            terms.append(jnp.where(jnp.logical_and(lane >= EDGE, lane < EDGE + edges), value, 0.0))
        return jnp.concatenate(terms, axis=0)

    def add_edges(c, start, count, value):
        at_lane = lax.broadcasted_iota(jnp.int32, (count, LANES), 1)
        first = pltpu.roll(value, LANES - EDGE - 2 * lon, 1)
        last = pltpu.roll(value, LANES - EDGE - 2 * lon - 1 + rest - 1, 1)
        at = pl.ds(start, count)
        out_ref[c, at, :LANES] = out_ref[c, at, :LANES] + jnp.where(at_lane == 0, first, 0.0)
        end = jnp.where(at_lane == rest - 1, last, 0.0)[:, :rest]
        out_ref[c, at, cols - rest :] = out_ref[c, at, cols - rest :] + end

    def tile_of(t):
        return slice(t * LANES, min((t + 1) * LANES, cols))

    def read(ref, c, start, count, t):
        value = ref[c, pl.ds(aligned(start), count), tile_of(t)]
        if t == tiles - 1 and rest:
            value = jnp.concatenate([value, jnp.zeros((count, LANES - rest), jnp.float32)], axis=1)
        return value

    def tendency_block(b, use):
        start = pl.multiple_of(b * ROWS, ROWS)
        terms = geo[pl.ds(start, ROWS), :]
        zonal, up, down, turn, metric = [
            jnp.broadcast_to(terms[:, i : i + 1], (ROWS, LANES)) for i in range(5)
        ]
        held = {}

        def here(c, t):
            if (0, c, t) not in held:
                held[0, c, t] = read(xp, c, start + SUB, ROWS, t)
            return held[0, c, t]

        def moved(c, t, shift):
            if (shift, c, t) not in held:
                held[shift, c, t] = pltpu.roll(here(c, t), shift, 1)
            return held[shift, c, t]

        for t in range(tiles):
            east_of, west_of, north, south = [], [], [], []
            for c in range(3):
                right = moved(c, t + 1, LANES - 1) if t < tiles - 1 else 0.0
                edge_lane = LANES - 1 if t < tiles - 1 else (rest or LANES) - 1
                east_of.append(jnp.where(lane2 == edge_lane, right, moved(c, t, LANES - 1)))
                left = moved(c, t - 1, 1) if t > 0 else 0.0
                west_of.append(jnp.where(lane2 == 0, left, moved(c, t, 1)))
                value = here(c, t)
                low, high = value[:SUB], value[SUB:]
                after = read(xp, c, start + SUB + ROWS, SUB, t)
                before = read(xp, c, start, SUB, t)
                north.append(jnp.concatenate([
                    pltpu.roll(jnp.where(sub == 0, high, low), SUB - 1, 0),
                    pltpu.roll(jnp.where(sub == 0, after, high), SUB - 1, 0),
                ], axis=0))
                south.append(jnp.concatenate([
                    pltpu.roll(jnp.where(sub == SUB - 1, before, low), 1, 0),
                    pltpu.roll(jnp.where(sub == SUB - 1, low, high), 1, 0),
                ], axis=0))
            u, v = here(1, t), here(2, t)
            t_h = -zonal * (east_of[0] * east_of[1] - west_of[0] * west_of[1]) - (
                up * (north[0] * north[2]) - down * (south[0] * south[2])
            )
            turning = turn + metric * u
            zu = zonal * u
            hv = 0.5 * v
            t_u = (
                turning * v - zu * (east_of[1] - west_of[1]) - hv * (north[1] - south[1])
                - zonal * (east_of[0] - west_of[0])
            )
            t_v = (
                -turning * u - zu * (east_of[2] - west_of[2]) - hv * (north[2] - south[2])
                - 0.5 * (north[0] - south[0])
            )
            use(start, t, (t_h, t_u, t_v))

    def put(c, start, t, value):
        out_ref[c, pl.ds(start, ROWS), tile_of(t)] = value[:, : min(LANES, cols - t * LANES)]

    def plain(start, t, values):
        for c in range(3):
            put(c, start, t, read(old, c, start, ROWS, t) + step_scale * values[c])

    span_near = lines // 2
    span_far = lines // 4
    spans = [(0, span_near), (span_near, span_near), (2 * span_near, span_far)]
    ranks = [(0, NEAR), (NEAR, NEAR), (2 * NEAR, FAR)]

    def far_copy(i, k):
        first, count = spans[k]
        return pltpu.make_async_remote_copy(
            src_ref=send.at[i, pl.ds(first, count), :], dst_ref=recv.at[i, pl.ds(first, count), :],
            send_sem=far_send.at[i, k], recv_sem=far_recv.at[i, k],
            device_id={"lon": (west, east, across)[k]}, device_id_type=MESH,
        )

    def far_start(i):
        for k in range(3):
            far_copy(i, k).start()

    def ordered(i, count):
        return jnp.where(lat == 0, i, count - 1 - i)

    def operand(i):
        value = lhs[i]
        return jnp.concatenate([value, value[:, :MAIN]], axis=1)

    def turned(value, shift):
        shift = shift % LANES
        return pltpu.roll(value, shift, 1) if shift else value

    def merged(slots, size):
        at = lax.broadcasted_iota(jnp.int32, slots[0].shape, 1)
        whole = slots[-1]
        for s in range(len(slots) - 2, -1, -1):
            whole = jnp.where(at < (s + 1) * size, slots[s], whole)
        return whole

    def modulated(i, b):
        def use(start, t, values):
            at = pl.ds(start, ROWS)
            own = wave[at, 2 * width :]
            turn_cos = wave[at, t * LANES : (t + 1) * LANES]
            turn_sin = wave[at, width + t * LANES : width + (t + 1) * LANES]
            for c in range(3):
                value = values[c]
                put(c, start, t, read(old, c, start, ROWS, t) + own * value)
                for channel, factor in enumerate((turn_cos, turn_sin)):
                    first = channel * lines + c * chunk + lax.rem(b, per_chunk) * ROWS
                    line = pl.ds(pl.multiple_of(first, ROWS), ROWS)
                    high, back, low = high_low(value * factor)
                    if t < tiles - 1:
                        lhs[i, line, t * LANES : (t + 1) * LANES] = high
                        lhs[i, line, MAIN + t * LANES : MAIN + (t + 1) * LANES] = low.astype(jnp.bfloat16)
                    else:
                        mixed = jnp.where(lane2 < rest, back, pltpu.roll(low, rest, 1))
                        lhs[i, line, 2 * MAIN : 2 * MAIN + LANES] = mixed.astype(jnp.bfloat16)
                        lhs[i, line, 2 * MAIN + LANES :] = high

        return use

    def make_lines(i, first, count):
        @pl.loop(first // 2, (first + count) // 2)
        def _(pair):
            for p in range(2):
                b = ordered(pair * 2 + p, blocks)
                tendency_block(b, modulated(i, b))

    def make_moments(i):
        moments = dot(operand(i), moment[...])
        for k, (first, size) in enumerate(ranks):
            count = spans[k][1]
            slots = []
            for s in range(LANES // size):
                origin = (s % 2) * lines + (s // 2) * count
                slots.append(turned(moments[origin : origin + count], s * size - first))
            send[i, pl.ds(spans[k][0], count), :] = merged(slots, size)

    def make_local(i):
        part[i] = dot(operand(i), local[...])

    @pl.when(polar)
    def _():
        cut_start = jnp.where(lat == 0, 0, rows)
        for copy in wave_loads:
            copy.wait()
        cuts = cut_ref[...].astype(jnp.float32)[None, :]

        @pl.loop(0, rows // chunk)
        def _(i):
            start = pl.multiple_of(i * chunk, chunk)
            wanted = cut_start + start + lax.broadcasted_iota(jnp.int32, (chunk, 2 * rows), 0)
            hit = wanted == lax.broadcasted_iota(jnp.int32, (chunk, 2 * rows), 1)
            limit = jnp.sum(jnp.where(hit, cuts, 0.0), axis=1, keepdims=True)
            turns = jnp.minimum(2.0 * limit + 1.0, float(total))
            digit = LANES // 2
            upper = jnp.floor(turns * (1.0 / digit))
            lower = turns - digit * upper
            place = lax.rem(lax.broadcasted_iota(jnp.int32, (chunk, LANES), 1), digit).astype(jnp.float32)

            def lookup(value, k):
                found = (place == value).astype(jnp.bfloat16)
                return dot(jnp.concatenate([found, found], axis=1), phase[k])

            a, z = lookup(upper, 0), lookup(lower, 1)
            at = pl.ds(start, chunk)
            wave[at, :width] = a[:, :width] * z[:, :width] - a[:, width : 2 * width] * z[:, width : 2 * width]
            wave[at, width : 2 * width] = (
                a[:, width : 2 * width] * z[:, :width] + a[:, :width] * z[:, width : 2 * width]
            )
            wave[at, 2 * width :] = a[:, 2 * width :] + z[:, 2 * width :]

        geo_load.wait()
        old_load.wait()
        moment_load.wait()
        make_lines(0, 0, per_chunk)
        make_moments(0)

    neighbours_enter()

    @pl.when(jnp.logical_not(polar))
    def _():
        for copy in wave_loads:
            copy.wait()
        geo_load.wait()
        old_load.wait()
        moment_load.wait()
        local_load.wait()
        field_load.wait()

        @pl.loop(0, blocks // 2 - 1)
        def _(pair):
            for p in range(2):
                tendency_block(2 * pair + 1 + p, plain)

        halos_arrive()

        @pl.loop(0, 2)
        def _(side):
            tendency_block(side * (blocks - 1), plain)

        edges_arrive()

        @pl.loop(0, blocks)
        def _(b):
            start = pl.multiple_of(b * ROWS, ROWS)
            for c in range(3):
                add_edges(c, start, ROWS, step_scale * edge_terms(c, start, ROWS))

    @pl.when(polar)
    def _():
        far_start(0)

        @pl.loop(1, chunks - 1)
        def _(i):
            make_lines(i, i * per_chunk, per_chunk)
            make_moments(i)
            far_start(i)

        make_lines(chunks - 1, (chunks - 1) * per_chunk, per_chunk - 2)
        local_load.wait()

        @pl.loop(0, chunks - 1)
        def _(i):
            make_local(i)

        halos_arrive()
        make_lines(chunks - 1, blocks - 2, 2)
        make_moments(chunks - 1)
        far_start(chunks - 1)
        make_local(chunks - 1)
        edges_arrive()
        field_load.wait()

        @pl.loop(0, chunks)
        def _(i):
            start = pl.multiple_of(ordered(i, chunks) * chunk, ROWS)
            at = pl.ds(start, chunk)
            turn_cos = wave[at, :width]
            turn_sin = wave[at, width : 2 * width]
            terms = [edge_terms(c, start, chunk) for c in range(3)]
            at_edge = jnp.concatenate(
                [term * turn[:, width - LANES :] for turn in (turn_cos, turn_sin) for term in terms], axis=0
            )
            for k in range(3):
                far_copy(i, k).wait_recv()
            gathered = []
            for k, (first, size) in enumerate(ranks):
                value = recv[i, pl.ds(spans[k][0], spans[k][1]), :]
                slots = [turned(value, first - s * size) for s in range(LANES // size)]
                gathered.append(jnp.concatenate(slots[0::2] + slots[1::2], axis=0))
            at_lane = lax.broadcasted_iota(jnp.int32, (2 * lines, LANES), 1)
            coming = jnp.where(
                at_lane < NEAR, gathered[0],
                jnp.where(at_lane < 2 * NEAR, gathered[1], jnp.where(at_lane < EDGE, gathered[2], at_edge)),
            )
            high, _, low = high_low(coming)
            whole = part[i] + dot(jnp.concatenate([high, low.astype(jnp.bfloat16), high], axis=1), field[...])
            own = wave[at, 2 * width :]
            for c in range(3):
                by_cos = whole[c * chunk : (c + 1) * chunk, :cols]
                by_sin = whole[lines + c * chunk : lines + (c + 1) * chunk, :cols]
                out_ref[c, at, :] = out_ref[c, at, :] + turn_sin[:, :cols] * by_cos - turn_cos[:, :cols] * by_sin
                add_edges(c, start, chunk, own * terms[c])

        @pl.loop(0, chunks)
        def _(i):
            for k in range(3):
                far_copy(i, k).wait_send()


def fused_step(mesh_shape, tables, state_now, state_old, polar_cutoff):
    lat_count, lon_count = mesh_shape
    comps, rows, cols = state_now.shape
    chunk = chunk_rows(rows)
    chunks = rows // chunk
    lines = comps * chunk
    width = -(-cols // LANES) * LANES
    geo, scale, phase, local, moment, field = tables
    operands = [
        pltpu.with_memory_space_constraint(jnp.asarray(a), pltpu.HBM)
        for a in (state_now, state_old, geo, scale, polar_cutoff, phase, local, moment, field)
    ]
    hbm_spec = pl.BlockSpec(memory_space=pltpu.HBM)
    vmem_spec = pl.BlockSpec(memory_space=pltpu.VMEM)
    dma = pltpu.SemaphoreType.DMA
    edge = (comps, *scale.shape[1:])
    exchange = pltpu.VMEM((chunks, lines // 2 * 2 + lines // 4, LANES), jnp.float32)
    return pl.pallas_call(
        functools.partial(step_kernel, lat_count, lon_count, chunk),
        out_shape=jax.ShapeDtypeStruct(state_now.shape, jnp.float32),
        in_specs=[hbm_spec] * 9,
        out_specs=vmem_spec,
        scratch_shapes=[
            pltpu.VMEM((comps, rows, cols), jnp.float32),
            pltpu.VMEM((comps, rows + 2 * SUB, cols), jnp.float32),
            pltpu.VMEM((rows, LANES), jnp.float32),
            pltpu.VMEM(scale.shape[1:], jnp.float32),
            pltpu.VMEM((2 * rows,), jnp.int32),
            pltpu.VMEM(phase.shape[1:], jnp.bfloat16),
            pltpu.VMEM(local.shape, jnp.bfloat16),
            pltpu.VMEM(moment.shape, jnp.bfloat16),
            pltpu.VMEM(field.shape[1:], jnp.bfloat16),
            pltpu.VMEM((rows, 2 * width + LANES), jnp.float32),
            pltpu.VMEM((chunks, 2 * lines, 2 * MAIN + 2 * LANES), jnp.bfloat16),
            pltpu.VMEM((chunks, 2 * lines, width), jnp.float32),
            exchange,
            exchange,
            pltpu.VMEM(edge, jnp.float32),
            pltpu.VMEM((lon_count, *edge), jnp.float32),
            pltpu.VMEM(edge, jnp.float32),
            dma, dma((8,)), dma((2,)), dma((2,)), dma((lon_count,)), dma((lon_count,)),
            dma((chunks, 3)), dma((chunks, 3)),
        ],
        compiler_params=pltpu.CompilerParams(
            collective_id=0, has_side_effects=True, vmem_limit_bytes=40 * 1024 * 1024
        ),
    )(*operands)


def chunk_rows(rows):
    return rows // 3 if rows % 96 == 0 else 0


def solution(mesh):
    lat_count, lon_count = mesh.shape["lat"], mesh.shape["lon"]

    def step(state_now, state_old, polar_cutoff):
        comps, lat_total, lon_total = state_now.shape
        rows, cols = lat_total // lat_count, lon_total // lon_count
        fits = (
            lat_count == 4 and lon_count == 4 and lat_total == 4 * rows and chunk_rows(rows) > 0
            and cols == MAIN + LANES // 2 and rows // SUB <= LANES and comps == 3 * mesh.shape["ens"]
        )
        body = per_device
        if fits:
            geo = geometry_table(lat_total, lon_total)
            tables = (
                geo, edge_scale(geo, lat_count, lon_count), phase_tables(cols, lon_count),
                *convolution_tables(cols, lon_count),
            )
            body = functools.partial(fused_step, (lat_count, lon_count), tables)
        return jax.shard_map(
            body,
            mesh=mesh,
            in_specs=(P("ens", "lat", "lon"), P("ens", "lat", "lon"), P()),
            out_specs=P("ens", "lat", "lon"),
            check_vma=False,
        )(state_now, state_old, polar_cutoff)

    return step
```

```python
import functools
import math

import jax
import jax.numpy as jnp
import numpy as np
from jax import lax
from jax.experimental import pallas as pl
from jax.experimental.pallas import tpu as pltpu
from jax.sharding import PartitionSpec as P

LANES = 128
SUB = 8
MESH = pl.DeviceIdType.MESH
step_scale = 0.2
coriolis = 2.0
gravity = 1.0
highest = lax.Precision.HIGHEST


def padded(value, sides, width, wrap):
    for axis, dim in sides:
        devices, length = (lax.axis_size(axis), value.shape[dim])
        up = [(i, (i + 1) % devices) for i in range(devices if wrap else devices - 1)]
        down = [(j, i) for i, j in up]
        last = lax.slice_in_dim(value, length - width, length, axis=dim)
        leading = lax.slice_in_dim(value, 0, width, axis=dim)
        before = lax.ppermute(last, axis, up)
        after = lax.ppermute(leading, axis, down)
        value = jnp.concatenate([before, value, after], axis=dim)
    return value


def latitude_terms(row_index, lat_total):
    distance = jnp.minimum(row_index + 0.5, lat_total - row_index - 0.5)
    cosine_lat = jnp.sin(math.pi * distance / lat_total)
    sine_lat = -jnp.cos(math.pi * (row_index + 0.5) / lat_total)
    return (cosine_lat, sine_lat)


def tendencies(lat_padded, lon_padded, cos_ext, sine_lat, lat_total, lon_total):
    cosine_lat = cos_ext[1:-1]
    zonal_scale = (lon_total / (4.0 * lat_total) / cosine_lat)[:, None]
    metric = math.pi / lat_total * sine_lat / cosine_lat
    depth_lon, east_lon, north_lon = (lon_padded[0], lon_padded[1], lon_padded[2])
    depth_lat, east_lat, north_lat = (lat_padded[0], lat_padded[1], lat_padded[2])
    east = east_lon[:, 1:-1]
    north = north_lon[:, 1:-1]

    def zonal_change(field):
        return zonal_scale * (field[:, 2:] - field[:, :-2])

    def northward_change(field):
        return 0.5 * (field[2:] - field[:-2])

    mass_flux = depth_lat * north_lat * cos_ext[:, None]
    tend_depth = (
        -zonal_change(depth_lon * east_lon) - northward_change(mass_flux) / cosine_lat[:, None]
    )
    turning = coriolis * sine_lat[:, None] + metric[:, None] * east
    tend_east = (
        -east * zonal_change(east_lon)
        - north * northward_change(east_lat)
        + turning * north
        - gravity * zonal_change(depth_lon)
    )
    tend_north = (
        -east * zonal_change(north_lon)
        - north * northward_change(north_lat)
        - turning * east
        - gravity * northward_change(depth_lat)
    )
    return jnp.stack([tend_depth, tend_east, tend_north])


def angle_table(first_count, second_count, period):
    first_idx = jnp.arange(first_count, dtype=jnp.int32)
    second_idx = jnp.arange(second_count, dtype=jnp.int32)
    turns = first_idx[:, None] * second_idx[None, :] % period
    phase = turns.astype(jnp.float32) * (2.0 * math.pi / period)
    return (jnp.cos(phase), jnp.sin(phase))


def low_pass(signal, cutoff):
    count, length = signal.shape
    first = 1
    probe = 1
    while probe * probe <= length:
        if length % probe == 0:
            first = probe
        probe = probe + 1
    second = length // first
    cos_first, sin_first = angle_table(first, first, first)
    cos_second, sin_second = angle_table(second, second, second)
    cos_twist, sin_twist = angle_table(first, second, length)
    grid = signal.reshape(count, first, second)
    part_re = jnp.einsum("cpq,pk->ckq", grid, cos_first, precision=highest)
    part_im = -jnp.einsum("cpq,pk->ckq", grid, sin_first, precision=highest)
    twist_re = part_re * cos_twist + part_im * sin_twist
    twist_im = part_im * cos_twist - part_re * sin_twist
    spec_re = jnp.einsum("ckq,qm->ckm", twist_re, cos_second, precision=highest) + jnp.einsum(
        "ckq,qm->ckm", twist_im, sin_second, precision=highest
    )
    spec_im = jnp.einsum("ckq,qm->ckm", twist_im, cos_second, precision=highest) - jnp.einsum(
        "ckq,qm->ckm", twist_re, sin_second, precision=highest
    )
    wave = (
        jnp.arange(first, dtype=jnp.int32)[:, None]
        + first * jnp.arange(second, dtype=jnp.int32)[None, :]
    )
    limit = cutoff[:, None, None]
    keep = ((wave[None] <= limit) | (wave[None] >= length - limit)).astype(jnp.float32) * (
        1.0 / length
    )
    spec_re = spec_re * keep
    spec_im = spec_im * keep
    back_re = jnp.einsum("ckm,mq->ckq", spec_re, cos_second, precision=highest) - jnp.einsum(
        "ckm,mq->ckq", spec_im, sin_second, precision=highest
    )
    back_im = jnp.einsum("ckm,mq->ckq", spec_im, cos_second, precision=highest) + jnp.einsum(
        "ckm,mq->ckq", spec_re, sin_second, precision=highest
    )
    turn_re = back_re * cos_twist - back_im * sin_twist
    turn_im = back_im * cos_twist + back_re * sin_twist
    result = jnp.einsum("ckq,kp->cpq", turn_re, cos_first, precision=highest) - jnp.einsum(
        "ckq,kp->cpq", turn_im, sin_first, precision=highest
    )
    return result.reshape(count, length)


def per_device(state_now, state_old, polar_cutoff):
    lat_rows = state_now.shape[1]
    lon_cols = state_now.shape[2]
    lat_count = lax.axis_size("lat")
    lon_count = lax.axis_size("lon")
    lat_total = lat_rows * lat_count
    lon_total = lon_cols * lon_count
    lat_place = lax.axis_index("lat")
    lat_padded = padded(state_now, (("lat", 1),), 1, False)
    lon_padded = padded(state_now, (("lon", 2),), 1, True)
    row_index = (lat_place * lat_rows + jnp.arange(-1, lat_rows + 1, dtype=jnp.int32)).astype(
        jnp.float32
    )
    cos_ext, sin_ext = latitude_terms(row_index, lat_total)
    forcing = tendencies(lat_padded, lon_padded, cos_ext, sin_ext[1:-1], lat_total, lon_total)
    groups = lat_count * lon_count
    share = lat_rows // groups
    member = lax.axis_index(("lat", "lon"))
    south_cut = lax.dynamic_slice_in_dim(polar_cutoff, member * share, share)
    north_cut = lax.dynamic_slice_in_dim(polar_cutoff, lat_rows + member * share, share)
    band_cut = jnp.concatenate([south_cut, north_cut])
    block = lax.all_to_all(forcing, ("lat", "lon"), split_axis=1, concat_axis=2, tiled=True)
    items = block.shape[0]
    wide = block.shape[2]
    south_rows = block[:, :, :lon_total]
    north_rows = block[:, :, wide - lon_total :]
    polar_rows = jnp.concatenate([south_rows, north_rows], axis=1)
    smooth = low_pass(polar_rows.reshape(items * 2 * share, lon_total), jnp.tile(band_cut, items))
    smooth = smooth.reshape(items, 2 * share, lon_total)
    rebuilt = jnp.concatenate(
        [smooth[:, :share], block[:, :, lon_total : wide - lon_total], smooth[:, share:]], axis=2
    )
    filtered = lax.all_to_all(rebuilt, ("lat", "lon"), split_axis=2, concat_axis=1, tiled=True)
    return state_old + step_scale * filtered


NEAR = 28
FAR = 16
MAIN = 4 * LANES
ROWS = 16
EDGE = 2 * NEAR + FAR
RANKS = [(0, NEAR, 32), (NEAR, NEAR, 32), (2 * NEAR, FAR, 16)]


def split_table(table):
    table = np.asarray(table, np.float32)
    high = table.astype(jnp.bfloat16)
    rest = table - high.astype(np.float32)
    middle = rest.astype(jnp.bfloat16)
    low = (rest - middle.astype(np.float32)).astype(jnp.bfloat16)
    return high, middle, low


def kernel_values(offset, total):
    safe = np.where(offset == 0, 1, offset)
    return np.where(offset == 0, 0.0, 1.0 / (total * np.sin(np.pi * safe / total)))


def stacked(table, cols):
    high, low, _ = split_table(table)
    zero = np.zeros((2 * LANES - 3 * (cols - MAIN), table.shape[1]), high.dtype)
    tail = [high[MAIN:], high[MAIN:], low[MAIN:], zero]
    return np.concatenate([high[:MAIN], high[:MAIN], *tail, low[:MAIN]])


def edge_columns(cols, lon_count):
    start = np.arange(lon_count) * cols
    return np.stack([start, start + cols - 1], axis=1).reshape(-1)


def convolution_tables(cols, lon_count):
    total = cols * lon_count
    width = -(-cols // LANES) * LANES
    here = np.arange(cols)
    target, source = here[:, None], here[None, :]
    local = np.zeros((cols, width))
    local[:, :cols] = step_scale * kernel_values(target - source, total).T
    moments = np.zeros((cols, LANES))
    fields = np.zeros((lon_count, LANES, width))
    lon = np.arange(lon_count)
    edge = edge_columns(cols, lon_count)
    places = [(-1, 0, NEAR), (1, NEAR, NEAR), (2, 2 * NEAR, FAR)]
    for step, start, rank in places:
        block = kernel_values(target - source + step * cols, total)
        left, scale, right = np.linalg.svd(block)
        moments[:, start : start + rank] = right[:rank].T
        back = step_scale * scale[:rank, None] * left[:, :rank].T
        for q in lon:
            origin = (q - step) % lon_count
            sign = 1.0 if q - origin == step else -1.0
            fields[q, start : start + rank, :cols] = sign * back
    piled = []
    for q in lon:
        offset = q * cols + here[None, :] - edge[:, None]
        fields[q, EDGE : EDGE + len(edge), :cols] = step_scale * kernel_values(offset, total)
        high, low, _ = split_table(fields[q])
        used = EDGE + len(edge)
        gap = np.zeros((2 * LANES - 3 * used, width), high.dtype)
        piled.append(np.concatenate([high[:used], high[:used], low[:used], gap]))
    local = stacked(local, cols)
    first = np.concatenate([stacked(moments, cols), local[:, MAIN:]], axis=1)
    return local[:, :MAIN], first, np.stack(piled)


def phase_tables(cols, lon_count):
    total = cols * lon_count
    width = -(-cols // LANES) * LANES
    digit = LANES // 2
    coarse, fine = [], []
    edge = edge_columns(cols, lon_count)
    at_edge = MAIN + EDGE + np.arange(len(edge))
    for q in range(lon_count):
        m = q * cols + np.arange(cols)[None, :]
        for out, unit in ((coarse, digit), (fine, 1)):
            k = unit * np.arange(digit)[:, None]
            table = np.zeros((digit, 2 * width + LANES))
            for columns, places in ((m, np.arange(cols)), (edge[None, :], at_edge)):
                angle = np.pi * ((k * columns) % (2 * total)) / total
                table[:, places] = np.cos(angle)
                table[:, width + places] = np.sin(angle)
            table[:, 2 * width :] = step_scale * k / total
            parts = split_table(table)
            out.append(np.concatenate([*parts, np.zeros_like(parts[0])]))
    return np.stack([np.stack(coarse), np.stack(fine)], axis=1)


def geometry_table(lat_total, lon_total):
    j = np.arange(lat_total, dtype=np.float64)

    def cosine(row):
        return np.sin(np.pi * np.minimum(row + 0.5, lat_total - row - 0.5) / lat_total)

    c = cosine(j)
    s = -np.cos(np.pi * (j + 0.5) / lat_total)
    table = np.zeros((lat_total, LANES))
    table[:, 0] = lon_total / (4.0 * lat_total * c)
    table[:, 1] = 0.5 * cosine(j + 1) / c
    table[:, 2] = 0.5 * cosine(j - 1) / c
    table[:, 3] = coriolis * s
    table[:, 4] = np.pi / lat_total * s / c
    return table.astype(np.float32)


def edge_scale(geo, lat_count, lon_count):
    rows = len(geo) // lat_count
    edges = 2 * lon_count
    per = LANES // edges
    count = -(-(rows // SUB) // per)
    table = np.zeros((lat_count, count, SUB, LANES), np.float32)
    for lat in range(lat_count):
        for g in range(rows // SUB):
            zonal = geo[lat * rows + g * SUB : lat * rows + (g + 1) * SUB, 0]
            for k in range(edges):
                table[lat, g // per, :, g % per * edges + k] = zonal if k % 2 == 0 else -zonal
    return table


def dot(a, b):
    return lax.dot_general(a, b, (((1,), (0,)), ((), ())), preferred_element_type=jnp.float32)


def high_low(value):
    high = value.astype(jnp.bfloat16)
    back = high.astype(jnp.float32)
    return high, back, value - back


def step_kernel(
    lat_count, lon_count, chunk,
    x_hbm, old_hbm, geo_hbm, scale_hbm, cut_hbm, phase_hbm, local_hbm, moment_hbm, field_hbm, out_ref,
    old, xp, geo, scale, cut_ref, phase, local, moment, field, wave, lhs, part, send, recv,
    edge_send, edge_recv, delta, load_sem, table_sem, row_send_sem, row_recv_sem, edge_send_sem,
    edge_recv_sem, far_send, far_recv,
):
    rows, cols = out_ref.shape[1], out_ref.shape[2]
    chunks = rows // chunk
    blocks = rows // ROWS
    per_chunk = chunk // ROWS
    groups = rows // SUB
    total = lon_count * cols
    tiles = -(-cols // LANES)
    width = tiles * LANES
    rest = cols % LANES
    lines = 3 * chunk
    edges = 2 * lon_count
    edge_groups = LANES // edges
    edge_vregs = scale.shape[0]
    lat = lax.axis_index("lat")
    lon = lax.axis_index("lon")
    west = lax.rem(lon + lon_count - 1, lon_count)
    east = lax.rem(lon + 1, lon_count)
    across = lax.rem(lon + 2, lon_count)
    polar = jnp.logical_or(lat == 0, lat == lat_count - 1)
    has_south = lat > 0
    has_north = lat < lat_count - 1

    def aligned(i):
        return pl.multiple_of(i, SUB)

    load = pltpu.make_async_copy(x_hbm, xp.at[:, pl.ds(SUB, rows), :], load_sem)
    load.start()
    geo_load = pltpu.make_async_copy(
        geo_hbm.at[pl.ds(aligned(lat * rows), rows), :], geo, table_sem.at[0]
    )
    wave_loads = [
        pltpu.make_async_copy(cut_hbm, cut_ref, table_sem.at[1]),
        pltpu.make_async_copy(phase_hbm.at[lon], phase, table_sem.at[2]),
    ]
    old_load = pltpu.make_async_copy(old_hbm, old, table_sem.at[3])
    moment_load = pltpu.make_async_copy(moment_hbm, moment, table_sem.at[4])
    local_load = pltpu.make_async_copy(local_hbm, local, table_sem.at[5])
    field_load = pltpu.make_async_copy(field_hbm.at[lon], field, table_sem.at[6])
    scale_load = pltpu.make_async_copy(scale_hbm.at[lat], scale, table_sem.at[7])
    for copy in [geo_load, *wave_loads, old_load, moment_load, scale_load, local_load, field_load]:
        copy.start()

    barrier = pltpu.get_barrier_semaphore()
    for k in range(1, lon_count):
        pl.semaphore_signal(
            barrier, inc=1, device_id={"lon": lax.rem(lon + k, lon_count)}, device_id_type=MESH
        )

    @pl.when(has_south)
    def _():
        pl.semaphore_signal(barrier, inc=1, device_id={"lat": lat - 1}, device_id_type=MESH)

    @pl.when(has_north)
    def _():
        pl.semaphore_signal(barrier, inc=1, device_id={"lat": lat + 1}, device_id_type=MESH)

    load.wait()
    lane = lax.broadcasted_iota(jnp.int32, (SUB, LANES), 1)
    lane2 = lax.broadcasted_iota(jnp.int32, (ROWS, LANES), 1)
    sub = lax.broadcasted_iota(jnp.int32, (SUB, LANES), 0)

    for first in range(0, 3 * edge_vregs, lon_count):
        packed = jnp.zeros((SUB, LANES), jnp.float32)
        for a in range(first, min(first + lon_count, 3 * edge_vregs)):
            c, w = a // edge_vregs, a % edge_vregs
            for g in range(w * edge_groups, min((w + 1) * edge_groups, groups)):
                block = slice(SUB + g * SUB, 2 * SUB + g * SUB)
                at = g % edge_groups * edges + 2 * (a - first)
                packed = jnp.where(lane == at, xp[c, block, 0:1], packed)
                packed = jnp.where(lane == at + 1, xp[c, block, cols - 1 : cols], packed)
        edge_send[first // lon_count] = packed

    def to_south():
        return pltpu.make_async_remote_copy(
            src_ref=x_hbm.at[:, pl.ds(0, SUB), :], dst_ref=xp.at[:, pl.ds(rows + SUB, SUB), :],
            send_sem=row_send_sem.at[0], recv_sem=row_recv_sem.at[0],
            device_id={"lat": lat - 1}, device_id_type=MESH,
        )

    def to_north():
        return pltpu.make_async_remote_copy(
            src_ref=x_hbm.at[:, pl.ds(rows - SUB, SUB), :], dst_ref=xp.at[:, pl.ds(0, SUB), :],
            send_sem=row_send_sem.at[1], recv_sem=row_recv_sem.at[1],
            device_id={"lat": lat + 1}, device_id_type=MESH,
        )

    zero_rows = jnp.zeros((3, SUB, cols), jnp.float32)

    @pl.when(jnp.logical_not(has_south))
    def _():
        xp[:, 0:SUB, :] = zero_rows

    @pl.when(jnp.logical_not(has_north))
    def _():
        xp[:, rows + SUB : rows + 2 * SUB, :] = zero_rows

    def edge_copy(k, source):
        target = lax.rem(source + k, lon_count)
        return pltpu.make_async_remote_copy(
            src_ref=edge_send, dst_ref=edge_recv.at[k],
            send_sem=edge_send_sem.at[k], recv_sem=edge_recv_sem.at[k],
            device_id={"lon": target}, device_id_type=MESH,
        )

    def neighbours_enter():
        pl.semaphore_wait(
            barrier, lon_count - 1 + has_south.astype(jnp.int32) + has_north.astype(jnp.int32)
        )

        @pl.when(has_south)
        def _():
            to_south().start()

        @pl.when(has_north)
        def _():
            to_north().start()

        for k in (1, lon_count - 1):
            edge_copy(k, lon).start()

        @pl.when(polar)
        def _():
            for k in range(2, lon_count - 1):
                edge_copy(k, lon).start()

    def halos_arrive():
        @pl.when(has_south)
        def _():
            to_south().wait_send()
            to_north().wait_recv()

        @pl.when(has_north)
        def _():
            to_north().wait_send()
            to_south().wait_recv()

    def edges_arrive():
        for k in (1, lon_count - 1):
            edge_copy(k, lon).wait()

        @pl.when(polar)
        def _():
            for k in range(2, lon_count - 1):
                edge_copy(k, lon).wait()

        @pl.when(jnp.logical_not(polar))
        def _():
            for k in range(2, lon_count - 1):
                edge_recv[k] = jnp.zeros(edge_recv.shape[1:], jnp.float32)

        scale_load.wait()
        k_of = lax.rem(lane, edges)

        def beside(value):
            plus = pltpu.roll(value, 1, 1)
            minus = pltpu.roll(value, LANES - 1, 1)
            last = pltpu.roll(value, LANES - edges + 1, 1)
            first = pltpu.roll(value, edges - 1, 1)
            inner = jnp.where(lax.rem(k_of, 2) == 0, plus, minus)
            return jnp.where(k_of == 0, last, jnp.where(k_of == edges - 1, first, inner))

        for w in range(edge_vregs):
            own = []
            for c in range(3):
                a = c * edge_vregs + w
                slot = a % lon_count
                parts = []
                for k in range(lon_count):
                    source = lax.rem(lon + lon_count - k, lon_count)
                    value = edge_recv[k, a // lon_count] if k else edge_send[a // lon_count]
                    value = jnp.where(k_of // 2 == slot, value, 0.0)
                    parts.append(pltpu.roll(value, lax.rem(2 * (source - slot) + LANES, LANES), 1))
                own.append((parts[0] + parts[1]) + (parts[2] + parts[3]))
            h, u, v = [beside(value) for value in own]
            factor = scale[w]
            delta[0, w] = factor * (h * u)
            delta[1, w] = factor * (own[1] * u + h)
            delta[2, w] = factor * (own[1] * v)

    def edge_terms(c, start, count):
        terms = []
        for i in range(count // SUB):
            g = start // SUB + i
            value = delta[c, g // edge_groups]
            shift = lax.rem(EDGE + LANES - lax.rem(g, edge_groups) * edges, LANES)
            value = pltpu.roll(value, shift, 1)
            terms.append(jnp.where(jnp.logical_and(lane >= EDGE, lane < EDGE + edges), value, 0.0))
        return jnp.concatenate(terms, axis=0)

    def add_edges(c, start, count, value):
        at_lane = lax.broadcasted_iota(jnp.int32, (count, LANES), 1)
        first = pltpu.roll(value, LANES - EDGE - 2 * lon, 1)
        last = pltpu.roll(value, LANES - EDGE - 2 * lon - 1 + rest - 1, 1)
        at = pl.ds(start, count)
        out_ref[c, at, :LANES] = out_ref[c, at, :LANES] + jnp.where(at_lane == 0, first, 0.0)
        end = jnp.where(at_lane == rest - 1, last, 0.0)[:, :rest]
        out_ref[c, at, cols - rest :] = out_ref[c, at, cols - rest :] + end

    def tile_of(t):
        return slice(t * LANES, min((t + 1) * LANES, cols))

    def read(ref, c, start, count, t):
        value = ref[c, pl.ds(aligned(start), count), tile_of(t)]
        if t == tiles - 1 and rest:
            value = jnp.concatenate([value, jnp.zeros((count, LANES - rest), jnp.float32)], axis=1)
        return value

    def tendency_block(b, use):
        start = pl.multiple_of(b * ROWS, ROWS)
        terms = geo[pl.ds(start, ROWS), :]
        zonal, up, down, turn, metric = [
            jnp.broadcast_to(terms[:, i : i + 1], (ROWS, LANES)) for i in range(5)
        ]
        held = {}

        def here(c, t):
            if (0, c, t) not in held:
                held[0, c, t] = read(xp, c, start + SUB, ROWS, t)
            return held[0, c, t]

        def moved(c, t, shift):
            if (shift, c, t) not in held:
                held[shift, c, t] = pltpu.roll(here(c, t), shift, 1)
            return held[shift, c, t]

        for t in range(tiles):
            east_of, west_of, north, south = [], [], [], []
            for c in range(3):
                right = moved(c, t + 1, LANES - 1) if t < tiles - 1 else 0.0
                edge_lane = LANES - 1 if t < tiles - 1 else (rest or LANES) - 1
                east_of.append(jnp.where(lane2 == edge_lane, right, moved(c, t, LANES - 1)))
                left = moved(c, t - 1, 1) if t > 0 else 0.0
                west_of.append(jnp.where(lane2 == 0, left, moved(c, t, 1)))
                value = here(c, t)
                low, high = value[:SUB], value[SUB:]
                after = read(xp, c, start + SUB + ROWS, SUB, t)
                before = read(xp, c, start, SUB, t)
                north.append(jnp.concatenate([
                    pltpu.roll(jnp.where(sub == 0, high, low), SUB - 1, 0),
                    pltpu.roll(jnp.where(sub == 0, after, high), SUB - 1, 0),
                ], axis=0))
                south.append(jnp.concatenate([
                    pltpu.roll(jnp.where(sub == SUB - 1, before, low), 1, 0),
                    pltpu.roll(jnp.where(sub == SUB - 1, low, high), 1, 0),
                ], axis=0))
            u, v = here(1, t), here(2, t)
            t_h = -zonal * (east_of[0] * east_of[1] - west_of[0] * west_of[1]) - (
                up * (north[0] * north[2]) - down * (south[0] * south[2])
            )
            turning = turn + metric * u
            zu = zonal * u
            hv = 0.5 * v
            t_u = (
                turning * v - zu * (east_of[1] - west_of[1]) - hv * (north[1] - south[1])
                - zonal * (east_of[0] - west_of[0])
            )
            t_v = (
                -turning * u - zu * (east_of[2] - west_of[2]) - hv * (north[2] - south[2])
                - 0.5 * (north[0] - south[0])
            )
            use(start, t, (t_h, t_u, t_v))

    def put(c, start, t, value):
        out_ref[c, pl.ds(start, ROWS), tile_of(t)] = value[:, : min(LANES, cols - t * LANES)]

    def plain(start, t, values):
        for c in range(3):
            put(c, start, t, read(old, c, start, ROWS, t) + step_scale * values[c])

    span_near = lines // 2
    span_far = lines // 4
    spans = [(0, span_near), (span_near, span_near), (2 * span_near, span_far)]

    def far_copy(i, k):
        first, count = spans[k]
        return pltpu.make_async_remote_copy(
            src_ref=send.at[i, pl.ds(first, count), :], dst_ref=recv.at[i, pl.ds(first, count), :],
            send_sem=far_send.at[i, k], recv_sem=far_recv.at[i, k],
            device_id={"lon": (west, east, across)[k]}, device_id_type=MESH,
        )

    def far_start(i):
        for k in range(3):
            far_copy(i, k).start()

    def ordered(i, count):
        return jnp.where(lat == 0, i, count - 1 - i)

    def operand(i):
        value = lhs[i]
        return jnp.concatenate([value, value[:, :MAIN]], axis=1)

    def turned(value, shift):
        shift = shift % LANES
        return pltpu.roll(value, shift, 1) if shift else value

    def merged(slots, size):
        at = lax.broadcasted_iota(jnp.int32, slots[0].shape, 1)
        whole = slots[-1]
        for s in range(len(slots) - 2, -1, -1):
            whole = jnp.where(at < (s + 1) * size, slots[s], whole)
        return whole

    def modulated(i, b):
        def use(start, t, values):
            at = pl.ds(start, ROWS)
            own = wave[at, 2 * width :]
            turn_cos = wave[at, t * LANES : (t + 1) * LANES]
            turn_sin = wave[at, width + t * LANES : width + (t + 1) * LANES]
            for c in range(3):
                value = values[c]
                put(c, start, t, read(old, c, start, ROWS, t) + own * value)
                for channel, factor in enumerate((turn_cos, turn_sin)):
                    first = channel * lines + c * chunk + lax.rem(b, per_chunk) * ROWS
                    line = pl.ds(pl.multiple_of(first, ROWS), ROWS)
                    high, back, low = high_low(value * factor)
                    if t < tiles - 1:
                        lhs[i, line, t * LANES : (t + 1) * LANES] = high
                        lhs[i, line, MAIN + t * LANES : MAIN + (t + 1) * LANES] = low.astype(jnp.bfloat16)
                    else:
                        mixed = jnp.where(lane2 < rest, back, pltpu.roll(low, rest, 1))
                        lhs[i, line, 2 * MAIN : 2 * MAIN + LANES] = mixed.astype(jnp.bfloat16)
                        lhs[i, line, 2 * MAIN + LANES :] = high

        return use

    def make_lines(i, first, count):
        @pl.loop(first // 2, (first + count) // 2)
        def _(pair):
            for p in range(2):
                b = ordered(pair * 2 + p, blocks)
                tendency_block(b, modulated(i, b))

    def make_moments(i):
        both = dot(operand(i), moment[...])
        part[i, :, MAIN:] = both[:, LANES:]
        moments = both[:, :LANES]
        for k, (first, _, size) in enumerate(RANKS):
            count = spans[k][1]
            slots = []
            for s in range(LANES // size):
                origin = (s % 2) * lines + (s // 2) * count
                slots.append(turned(moments[origin : origin + count], s * size - first))
            send[i, pl.ds(spans[k][0], count), :] = merged(slots, size)

    def make_local(i):
        part[i, :, :MAIN] = dot(operand(i), local[...])

    @pl.when(polar)
    def _():
        cut_start = jnp.where(lat == 0, 0, rows)
        for copy in wave_loads:
            copy.wait()
        cuts = cut_ref[...].astype(jnp.float32)[None, :]

        @pl.loop(0, rows // chunk)
        def _(i):
            start = pl.multiple_of(i * chunk, chunk)
            wanted = cut_start + start + lax.broadcasted_iota(jnp.int32, (chunk, 2 * rows), 0)
            hit = wanted == lax.broadcasted_iota(jnp.int32, (chunk, 2 * rows), 1)
            limit = jnp.sum(jnp.where(hit, cuts, 0.0), axis=1, keepdims=True)
            turns = jnp.minimum(2.0 * limit + 1.0, float(total))
            digit = LANES // 2
            upper = jnp.floor(turns * (1.0 / digit))
            lower = turns - digit * upper
            place = lax.rem(lax.broadcasted_iota(jnp.int32, (chunk, LANES), 1), digit).astype(jnp.float32)

            def lookup(value, k):
                found = (place == value).astype(jnp.bfloat16)
                return dot(jnp.concatenate([found, found], axis=1), phase[k])

            a, z = lookup(upper, 0), lookup(lower, 1)
            at = pl.ds(start, chunk)
            wave[at, :width] = a[:, :width] * z[:, :width] - a[:, width : 2 * width] * z[:, width : 2 * width]
            wave[at, width : 2 * width] = (
                a[:, width : 2 * width] * z[:, :width] + a[:, :width] * z[:, width : 2 * width]
            )
            wave[at, 2 * width :] = a[:, 2 * width :] + z[:, 2 * width :]

        geo_load.wait()
        old_load.wait()
        moment_load.wait()
        make_lines(0, 0, per_chunk)
        make_moments(0)

    neighbours_enter()

    @pl.when(jnp.logical_not(polar))
    def _():
        for copy in wave_loads:
            copy.wait()
        geo_load.wait()
        old_load.wait()
        moment_load.wait()
        local_load.wait()
        field_load.wait()

        @pl.loop(0, blocks // 2 - 1)
        def _(pair):
            for p in range(2):
                tendency_block(2 * pair + 1 + p, plain)

        halos_arrive()

        @pl.loop(0, 2)
        def _(side):
            tendency_block(side * (blocks - 1), plain)

        edges_arrive()

        @pl.loop(0, blocks)
        def _(b):
            start = pl.multiple_of(b * ROWS, ROWS)
            for c in range(3):
                add_edges(c, start, ROWS, step_scale * edge_terms(c, start, ROWS))

    @pl.when(polar)
    def _():
        far_start(0)

        @pl.loop(1, chunks - 1)
        def _(i):
            make_lines(i, i * per_chunk, per_chunk)
            make_moments(i)
            far_start(i)

        make_lines(chunks - 1, (chunks - 1) * per_chunk, per_chunk - 2)
        local_load.wait()

        @pl.loop(0, chunks - 1)
        def _(i):
            make_local(i)

        halos_arrive()
        make_lines(chunks - 1, blocks - 2, 2)
        make_moments(chunks - 1)
        far_start(chunks - 1)
        make_local(chunks - 1)
        edges_arrive()
        field_load.wait()

        @pl.loop(0, chunks)
        def _(i):
            start = pl.multiple_of(ordered(i, chunks) * chunk, ROWS)
            at = pl.ds(start, chunk)
            turn_cos = wave[at, :width]
            turn_sin = wave[at, width : 2 * width]
            terms = [edge_terms(c, start, chunk) for c in range(3)]
            at_edge = jnp.concatenate(
                [term * turn[:, width - LANES :] for turn in (turn_cos, turn_sin) for term in terms], axis=0
            )
            for k in range(3):
                far_copy(i, k).wait_recv()
            gathered = []
            for k, (first, _, size) in enumerate(RANKS):
                value = recv[i, pl.ds(spans[k][0], spans[k][1]), :]
                slots = [turned(value, first - s * size) for s in range(LANES // size)]
                gathered.append(jnp.concatenate(slots[0::2] + slots[1::2], axis=0))
            at_lane = lax.broadcasted_iota(jnp.int32, (2 * lines, LANES), 1)
            coming = jnp.where(
                at_lane < NEAR, gathered[0],
                jnp.where(at_lane < 2 * NEAR, gathered[1], jnp.where(at_lane < EDGE, gathered[2], at_edge)),
            )
            _, high, low = high_low(coming)
            used = EDGE + edges
            low = pltpu.roll(low, used, 1)
            left = jnp.where(at_lane < used, high, low)
            right = jnp.where(at_lane < 2 * used - LANES, low, pltpu.roll(high, 2 * used - LANES, 1))
            factors = jnp.concatenate([left.astype(jnp.bfloat16), right.astype(jnp.bfloat16)], axis=1)
            whole = part[i] + dot(factors, field[...])
            own = wave[at, 2 * width :]
            for c in range(3):
                by_cos = whole[c * chunk : (c + 1) * chunk, :cols]
                by_sin = whole[lines + c * chunk : lines + (c + 1) * chunk, :cols]
                out_ref[c, at, :] = out_ref[c, at, :] + turn_sin[:, :cols] * by_cos - turn_cos[:, :cols] * by_sin
                add_edges(c, start, chunk, own * terms[c])

        @pl.loop(0, chunks)
        def _(i):
            for k in range(3):
                far_copy(i, k).wait_send()


def fused_step(mesh_shape, tables, state_now, state_old, polar_cutoff):
    lat_count, lon_count = mesh_shape
    comps, rows, cols = state_now.shape
    chunk = chunk_rows(rows)
    chunks = rows // chunk
    lines = comps * chunk
    width = -(-cols // LANES) * LANES
    geo, scale, phase, local, moment, field = tables
    operands = [
        pltpu.with_memory_space_constraint(jnp.asarray(a), pltpu.HBM)
        for a in (state_now, state_old, geo, scale, polar_cutoff, phase, local, moment, field)
    ]
    hbm_spec = pl.BlockSpec(memory_space=pltpu.HBM)
    vmem_spec = pl.BlockSpec(memory_space=pltpu.VMEM)
    dma = pltpu.SemaphoreType.DMA
    packed = (-(-comps * scale.shape[1] // lon_count), SUB, LANES)
    exchange = pltpu.VMEM((chunks, lines // 2 * 2 + lines // 4, LANES), jnp.float32)
    return pl.pallas_call(
        functools.partial(step_kernel, lat_count, lon_count, chunk),
        out_shape=jax.ShapeDtypeStruct(state_now.shape, jnp.float32),
        in_specs=[hbm_spec] * 9,
        out_specs=vmem_spec,
        scratch_shapes=[
            pltpu.VMEM((comps, rows, cols), jnp.float32),
            pltpu.VMEM((comps, rows + 2 * SUB, cols), jnp.float32),
            pltpu.VMEM((rows, LANES), jnp.float32),
            pltpu.VMEM(scale.shape[1:], jnp.float32),
            pltpu.VMEM((2 * rows,), jnp.int32),
            pltpu.VMEM(phase.shape[1:], jnp.bfloat16),
            pltpu.VMEM(local.shape, jnp.bfloat16),
            pltpu.VMEM(moment.shape, jnp.bfloat16),
            pltpu.VMEM(field.shape[1:], jnp.bfloat16),
            pltpu.VMEM((rows, 2 * width + LANES), jnp.float32),
            pltpu.VMEM((chunks, 2 * lines, 2 * MAIN + 2 * LANES), jnp.bfloat16),
            pltpu.VMEM((chunks, 2 * lines, width), jnp.float32),
            exchange,
            exchange,
            pltpu.VMEM(packed, jnp.float32),
            pltpu.VMEM((lon_count, *packed), jnp.float32),
            pltpu.VMEM((comps, *scale.shape[1:]), jnp.float32),
            dma, dma((8,)), dma((2,)), dma((2,)), dma((lon_count,)), dma((lon_count,)),
            dma((chunks, 3)), dma((chunks, 3)),
        ],
        compiler_params=pltpu.CompilerParams(
            collective_id=0, has_side_effects=True, vmem_limit_bytes=40 * 1024 * 1024
        ),
    )(*operands)


def chunk_rows(rows):
    return rows // 3 if rows % 96 == 0 else 0


def solution(mesh):
    lat_count, lon_count = mesh.shape["lat"], mesh.shape["lon"]

    def step(state_now, state_old, polar_cutoff):
        comps, lat_total, lon_total = state_now.shape
        rows, cols = lat_total // lat_count, lon_total // lon_count
        fits = (
            lat_count == 4 and lon_count == 4 and lat_total == 4 * rows and chunk_rows(rows) > 0
            and cols == MAIN + LANES // 2 and rows // SUB <= LANES and comps == 3 * mesh.shape["ens"]
        )
        body = per_device
        if fits:
            geo = geometry_table(lat_total, lon_total)
            tables = (
                geo, edge_scale(geo, lat_count, lon_count), phase_tables(cols, lon_count),
                *convolution_tables(cols, lon_count),
            )
            body = functools.partial(fused_step, (lat_count, lon_count), tables)
        return jax.shard_map(
            body,
            mesh=mesh,
            in_specs=(P("ens", "lat", "lon"), P("ens", "lat", "lon"), P()),
            out_specs=P("ens", "lat", "lon"),
            check_vma=False,
        )(state_now, state_old, polar_cutoff)

    return step
```

```python
import functools
import math

import jax
import jax.numpy as jnp
import numpy as np
from jax import lax
from jax.experimental import pallas as pl
from jax.experimental.pallas import tpu as pltpu
from jax.sharding import PartitionSpec as P

LANES = 128
SUB = 8
MESH = pl.DeviceIdType.MESH
step_scale = 0.2
coriolis = 2.0
gravity = 1.0
highest = lax.Precision.HIGHEST


def padded(value, sides, width, wrap):
    for axis, dim in sides:
        devices, length = (lax.axis_size(axis), value.shape[dim])
        up = [(i, (i + 1) % devices) for i in range(devices if wrap else devices - 1)]
        down = [(j, i) for i, j in up]
        last = lax.slice_in_dim(value, length - width, length, axis=dim)
        leading = lax.slice_in_dim(value, 0, width, axis=dim)
        before = lax.ppermute(last, axis, up)
        after = lax.ppermute(leading, axis, down)
        value = jnp.concatenate([before, value, after], axis=dim)
    return value


def latitude_terms(row_index, lat_total):
    distance = jnp.minimum(row_index + 0.5, lat_total - row_index - 0.5)
    cosine_lat = jnp.sin(math.pi * distance / lat_total)
    sine_lat = -jnp.cos(math.pi * (row_index + 0.5) / lat_total)
    return (cosine_lat, sine_lat)


def tendencies(lat_padded, lon_padded, cos_ext, sine_lat, lat_total, lon_total):
    cosine_lat = cos_ext[1:-1]
    zonal_scale = (lon_total / (4.0 * lat_total) / cosine_lat)[:, None]
    metric = math.pi / lat_total * sine_lat / cosine_lat
    depth_lon, east_lon, north_lon = (lon_padded[0], lon_padded[1], lon_padded[2])
    depth_lat, east_lat, north_lat = (lat_padded[0], lat_padded[1], lat_padded[2])
    east = east_lon[:, 1:-1]
    north = north_lon[:, 1:-1]

    def zonal_change(field):
        return zonal_scale * (field[:, 2:] - field[:, :-2])

    def northward_change(field):
        return 0.5 * (field[2:] - field[:-2])

    mass_flux = depth_lat * north_lat * cos_ext[:, None]
    tend_depth = (
        -zonal_change(depth_lon * east_lon) - northward_change(mass_flux) / cosine_lat[:, None]
    )
    turning = coriolis * sine_lat[:, None] + metric[:, None] * east
    tend_east = (
        -east * zonal_change(east_lon)
        - north * northward_change(east_lat)
        + turning * north
        - gravity * zonal_change(depth_lon)
    )
    tend_north = (
        -east * zonal_change(north_lon)
        - north * northward_change(north_lat)
        - turning * east
        - gravity * northward_change(depth_lat)
    )
    return jnp.stack([tend_depth, tend_east, tend_north])


def angle_table(first_count, second_count, period):
    first_idx = jnp.arange(first_count, dtype=jnp.int32)
    second_idx = jnp.arange(second_count, dtype=jnp.int32)
    turns = first_idx[:, None] * second_idx[None, :] % period
    phase = turns.astype(jnp.float32) * (2.0 * math.pi / period)
    return (jnp.cos(phase), jnp.sin(phase))


def low_pass(signal, cutoff):
    count, length = signal.shape
    first = 1
    probe = 1
    while probe * probe <= length:
        if length % probe == 0:
            first = probe
        probe = probe + 1
    second = length // first
    cos_first, sin_first = angle_table(first, first, first)
    cos_second, sin_second = angle_table(second, second, second)
    cos_twist, sin_twist = angle_table(first, second, length)
    grid = signal.reshape(count, first, second)
    part_re = jnp.einsum("cpq,pk->ckq", grid, cos_first, precision=highest)
    part_im = -jnp.einsum("cpq,pk->ckq", grid, sin_first, precision=highest)
    twist_re = part_re * cos_twist + part_im * sin_twist
    twist_im = part_im * cos_twist - part_re * sin_twist
    spec_re = jnp.einsum("ckq,qm->ckm", twist_re, cos_second, precision=highest) + jnp.einsum(
        "ckq,qm->ckm", twist_im, sin_second, precision=highest
    )
    spec_im = jnp.einsum("ckq,qm->ckm", twist_im, cos_second, precision=highest) - jnp.einsum(
        "ckq,qm->ckm", twist_re, sin_second, precision=highest
    )
    wave = (
        jnp.arange(first, dtype=jnp.int32)[:, None]
        + first * jnp.arange(second, dtype=jnp.int32)[None, :]
    )
    limit = cutoff[:, None, None]
    keep = ((wave[None] <= limit) | (wave[None] >= length - limit)).astype(jnp.float32) * (
        1.0 / length
    )
    spec_re = spec_re * keep
    spec_im = spec_im * keep
    back_re = jnp.einsum("ckm,mq->ckq", spec_re, cos_second, precision=highest) - jnp.einsum(
        "ckm,mq->ckq", spec_im, sin_second, precision=highest
    )
    back_im = jnp.einsum("ckm,mq->ckq", spec_im, cos_second, precision=highest) + jnp.einsum(
        "ckm,mq->ckq", spec_re, sin_second, precision=highest
    )
    turn_re = back_re * cos_twist - back_im * sin_twist
    turn_im = back_im * cos_twist + back_re * sin_twist
    result = jnp.einsum("ckq,kp->cpq", turn_re, cos_first, precision=highest) - jnp.einsum(
        "ckq,kp->cpq", turn_im, sin_first, precision=highest
    )
    return result.reshape(count, length)


def per_device(state_now, state_old, polar_cutoff):
    lat_rows = state_now.shape[1]
    lon_cols = state_now.shape[2]
    lat_count = lax.axis_size("lat")
    lon_count = lax.axis_size("lon")
    lat_total = lat_rows * lat_count
    lon_total = lon_cols * lon_count
    lat_place = lax.axis_index("lat")
    lat_padded = padded(state_now, (("lat", 1),), 1, False)
    lon_padded = padded(state_now, (("lon", 2),), 1, True)
    row_index = (lat_place * lat_rows + jnp.arange(-1, lat_rows + 1, dtype=jnp.int32)).astype(
        jnp.float32
    )
    cos_ext, sin_ext = latitude_terms(row_index, lat_total)
    forcing = tendencies(lat_padded, lon_padded, cos_ext, sin_ext[1:-1], lat_total, lon_total)
    groups = lat_count * lon_count
    share = lat_rows // groups
    member = lax.axis_index(("lat", "lon"))
    south_cut = lax.dynamic_slice_in_dim(polar_cutoff, member * share, share)
    north_cut = lax.dynamic_slice_in_dim(polar_cutoff, lat_rows + member * share, share)
    band_cut = jnp.concatenate([south_cut, north_cut])
    block = lax.all_to_all(forcing, ("lat", "lon"), split_axis=1, concat_axis=2, tiled=True)
    items = block.shape[0]
    wide = block.shape[2]
    south_rows = block[:, :, :lon_total]
    north_rows = block[:, :, wide - lon_total :]
    polar_rows = jnp.concatenate([south_rows, north_rows], axis=1)
    smooth = low_pass(polar_rows.reshape(items * 2 * share, lon_total), jnp.tile(band_cut, items))
    smooth = smooth.reshape(items, 2 * share, lon_total)
    rebuilt = jnp.concatenate(
        [smooth[:, :share], block[:, :, lon_total : wide - lon_total], smooth[:, share:]], axis=2
    )
    filtered = lax.all_to_all(rebuilt, ("lat", "lon"), split_axis=2, concat_axis=1, tiled=True)
    return state_old + step_scale * filtered


NEAR = 28
FAR = 16
MAIN = 4 * LANES
ROWS = 16
EDGE = 2 * NEAR + FAR
RANKS = [(0, NEAR, 32), (NEAR, NEAR, 32), (2 * NEAR, FAR, 16)]


def split_table(table):
    table = np.asarray(table, np.float32)
    high = table.astype(jnp.bfloat16)
    rest = table - high.astype(np.float32)
    middle = rest.astype(jnp.bfloat16)
    low = (rest - middle.astype(np.float32)).astype(jnp.bfloat16)
    return high, middle, low


def kernel_values(offset, total):
    safe = np.where(offset == 0, 1, offset)
    return np.where(offset == 0, 0.0, 1.0 / (total * np.sin(np.pi * safe / total)))


def stacked(table, cols):
    high, low, _ = split_table(table)
    zero = np.zeros((2 * LANES - 3 * (cols - MAIN), table.shape[1]), high.dtype)
    tail = [high[MAIN:], high[MAIN:], low[MAIN:], zero]
    return np.concatenate([high[:MAIN], high[:MAIN], *tail, low[:MAIN]])


def edge_columns(cols, lon_count):
    start = np.arange(lon_count) * cols
    return np.stack([start, start + cols - 1], axis=1).reshape(-1)


def convolution_tables(cols, lon_count):
    total = cols * lon_count
    width = -(-cols // LANES) * LANES
    here = np.arange(cols)
    target, source = here[:, None], here[None, :]
    local = np.zeros((cols, width))
    local[:, :cols] = step_scale * kernel_values(target - source, total).T
    moments = np.zeros((cols, LANES))
    fields = np.zeros((lon_count, LANES, width))
    lon = np.arange(lon_count)
    edge = edge_columns(cols, lon_count)
    places = [(-1, 0, NEAR), (1, NEAR, NEAR), (2, 2 * NEAR, FAR)]
    for step, start, rank in places:
        block = kernel_values(target - source + step * cols, total)
        left, scale, right = np.linalg.svd(block)
        moments[:, start : start + rank] = right[:rank].T
        back = step_scale * scale[:rank, None] * left[:, :rank].T
        for q in lon:
            origin = (q - step) % lon_count
            sign = 1.0 if q - origin == step else -1.0
            fields[q, start : start + rank, :cols] = sign * back
    piled = []
    for q in lon:
        offset = q * cols + here[None, :] - edge[:, None]
        fields[q, EDGE : EDGE + len(edge), :cols] = step_scale * kernel_values(offset, total)
        high, low, _ = split_table(fields[q])
        used = EDGE + len(edge)
        gap = np.zeros((2 * LANES - 3 * used, width), high.dtype)
        piled.append(np.concatenate([high[:used], high[:used], low[:used], gap]))
    local = stacked(local, cols)
    first = np.concatenate([stacked(moments, cols), local[:, MAIN:]], axis=1)
    return local[:, :MAIN], first, np.stack(piled)


def phase_tables(cols, lon_count):
    total = cols * lon_count
    width = -(-cols // LANES) * LANES
    digit = LANES // 2
    coarse, fine = [], []
    edge = edge_columns(cols, lon_count)
    at_edge = MAIN + EDGE + np.arange(len(edge))
    for q in range(lon_count):
        m = q * cols + np.arange(cols)[None, :]
        for out, unit in ((coarse, digit), (fine, 1)):
            k = unit * np.arange(digit)[:, None]
            table = np.zeros((digit, 2 * width + LANES))
            for columns, places in ((m, np.arange(cols)), (edge[None, :], at_edge)):
                angle = np.pi * ((k * columns) % (2 * total)) / total
                table[:, places] = np.cos(angle)
                table[:, width + places] = np.sin(angle)
            table[:, 2 * width :] = step_scale * k / total
            parts = split_table(table)
            out.append(np.concatenate(parts))
    return np.stack([np.stack(coarse), np.stack(fine)], axis=1)


def geometry_table(lat_total, lon_total):
    j = np.arange(lat_total, dtype=np.float64)

    def cosine(row):
        return np.sin(np.pi * np.minimum(row + 0.5, lat_total - row - 0.5) / lat_total)

    c = cosine(j)
    s = -np.cos(np.pi * (j + 0.5) / lat_total)
    table = np.zeros((lat_total, LANES))
    table[:, 0] = lon_total / (4.0 * lat_total * c)
    table[:, 1] = 0.5 * cosine(j + 1) / c
    table[:, 2] = 0.5 * cosine(j - 1) / c
    table[:, 3] = coriolis * s
    table[:, 4] = np.pi / lat_total * s / c
    return table.astype(np.float32)


def edge_scale(geo, lat_count, lon_count):
    rows = len(geo) // lat_count
    edges = 2 * lon_count
    per = LANES // edges
    count = -(-(rows // SUB) // per)
    table = np.zeros((lat_count, count, SUB, LANES), np.float32)
    for lat in range(lat_count):
        for g in range(rows // SUB):
            zonal = geo[lat * rows + g * SUB : lat * rows + (g + 1) * SUB, 0]
            for k in range(edges):
                table[lat, g // per, :, g % per * edges + k] = zonal if k % 2 == 0 else -zonal
    return table


def dot(a, b):
    return lax.dot_general(a, b, (((1,), (0,)), ((), ())), preferred_element_type=jnp.float32)


def high_low(value):
    high = value.astype(jnp.bfloat16)
    back = high.astype(jnp.float32)
    return high, back, value - back


def step_kernel(
    lat_count, lon_count, chunk,
    x_hbm, old_hbm, geo_hbm, scale_hbm, cut_hbm, phase_hbm, local_hbm, moment_hbm, field_hbm, out_ref,
    old, xp, geo, scale, cut_ref, phase, local, moment, field, wave, lhs, part, send, recv,
    edge_send, edge_recv, delta, load_sem, table_sem, row_send_sem, row_recv_sem, edge_send_sem,
    edge_recv_sem, far_send, far_recv,
):
    rows, cols = out_ref.shape[1], out_ref.shape[2]
    chunks = rows // chunk
    blocks = rows // ROWS
    per_chunk = chunk // ROWS
    groups = rows // SUB
    total = lon_count * cols
    tiles = -(-cols // LANES)
    width = tiles * LANES
    rest = cols % LANES
    lines = 3 * chunk
    edges = 2 * lon_count
    edge_groups = LANES // edges
    edge_vregs = scale.shape[0]
    lat = lax.axis_index("lat")
    lon = lax.axis_index("lon")
    west = lax.rem(lon + lon_count - 1, lon_count)
    east = lax.rem(lon + 1, lon_count)
    across = lax.rem(lon + 2, lon_count)
    polar = jnp.logical_or(lat == 0, lat == lat_count - 1)
    has_south = lat > 0
    has_north = lat < lat_count - 1

    def aligned(i):
        return pl.multiple_of(i, SUB)

    loads = [
        pltpu.make_async_copy(x_hbm.at[c], xp.at[c, pl.ds(SUB, rows), :], load_sem.at[c]) for c in range(3)
    ]
    for copy in loads:
        copy.start()
    geo_load = pltpu.make_async_copy(
        geo_hbm.at[pl.ds(aligned(lat * rows), rows), :], geo, table_sem.at[0]
    )
    wave_loads = [
        pltpu.make_async_copy(cut_hbm, cut_ref, table_sem.at[1]),
        pltpu.make_async_copy(phase_hbm.at[lon], phase, table_sem.at[2]),
    ]
    old_load = pltpu.make_async_copy(old_hbm, old, table_sem.at[3])
    moment_load = pltpu.make_async_copy(moment_hbm, moment, table_sem.at[4])
    local_load = pltpu.make_async_copy(local_hbm, local, table_sem.at[5])
    field_load = pltpu.make_async_copy(field_hbm.at[lon], field, table_sem.at[6])
    scale_load = pltpu.make_async_copy(scale_hbm.at[lat], scale, table_sem.at[7])
    for copy in [geo_load, *wave_loads]:
        copy.start()

    barrier = pltpu.get_barrier_semaphore()
    for k in range(1, lon_count):
        pl.semaphore_signal(
            barrier, inc=1, device_id={"lon": lax.rem(lon + k, lon_count)}, device_id_type=MESH
        )

    @pl.when(has_south)
    def _():
        pl.semaphore_signal(barrier, inc=1, device_id={"lat": lat - 1}, device_id_type=MESH)

    @pl.when(has_north)
    def _():
        pl.semaphore_signal(barrier, inc=1, device_id={"lat": lat + 1}, device_id_type=MESH)

    for copy in loads:
        copy.wait()
    for copy in [old_load, moment_load, scale_load, local_load, field_load]:
        copy.start()
    lane = lax.broadcasted_iota(jnp.int32, (SUB, LANES), 1)
    lane2 = lax.broadcasted_iota(jnp.int32, (ROWS, LANES), 1)
    sub = lax.broadcasted_iota(jnp.int32, (SUB, LANES), 0)

    for first in range(0, 3 * edge_vregs, lon_count):
        packed = jnp.zeros((SUB, LANES), jnp.float32)
        for a in range(first, min(first + lon_count, 3 * edge_vregs)):
            c, w = a // edge_vregs, a % edge_vregs
            for g in range(w * edge_groups, min((w + 1) * edge_groups, groups)):
                block = slice(SUB + g * SUB, 2 * SUB + g * SUB)
                at = g % edge_groups * edges + 2 * (a - first)
                packed = jnp.where(lane == at, xp[c, block, 0:1], packed)
                packed = jnp.where(lane == at + 1, xp[c, block, cols - 1 : cols], packed)
        edge_send[first // lon_count] = packed

    def to_south():
        return pltpu.make_async_remote_copy(
            src_ref=x_hbm.at[:, pl.ds(0, SUB), :], dst_ref=xp.at[:, pl.ds(rows + SUB, SUB), :],
            send_sem=row_send_sem.at[0], recv_sem=row_recv_sem.at[0],
            device_id={"lat": lat - 1}, device_id_type=MESH,
        )

    def to_north():
        return pltpu.make_async_remote_copy(
            src_ref=x_hbm.at[:, pl.ds(rows - SUB, SUB), :], dst_ref=xp.at[:, pl.ds(0, SUB), :],
            send_sem=row_send_sem.at[1], recv_sem=row_recv_sem.at[1],
            device_id={"lat": lat + 1}, device_id_type=MESH,
        )

    zero_rows = jnp.zeros((3, SUB, cols), jnp.float32)

    @pl.when(jnp.logical_not(has_south))
    def _():
        xp[:, 0:SUB, :] = zero_rows

    @pl.when(jnp.logical_not(has_north))
    def _():
        xp[:, rows + SUB : rows + 2 * SUB, :] = zero_rows

    def edge_copy(k, source):
        target = lax.rem(source + k, lon_count)
        return pltpu.make_async_remote_copy(
            src_ref=edge_send, dst_ref=edge_recv.at[k],
            send_sem=edge_send_sem.at[k], recv_sem=edge_recv_sem.at[k],
            device_id={"lon": target}, device_id_type=MESH,
        )

    def neighbours_enter():
        pl.semaphore_wait(
            barrier, lon_count - 1 + has_south.astype(jnp.int32) + has_north.astype(jnp.int32)
        )

        @pl.when(has_south)
        def _():
            to_south().start()

        @pl.when(has_north)
        def _():
            to_north().start()

        for k in (1, lon_count - 1):
            edge_copy(k, lon).start()

        @pl.when(polar)
        def _():
            for k in range(2, lon_count - 1):
                edge_copy(k, lon).start()

    def halos_arrive():
        @pl.when(has_south)
        def _():
            to_south().wait_send()
            to_north().wait_recv()

        @pl.when(has_north)
        def _():
            to_north().wait_send()
            to_south().wait_recv()

    def edges_arrive():
        for k in (1, lon_count - 1):
            edge_copy(k, lon).wait()

        @pl.when(polar)
        def _():
            for k in range(2, lon_count - 1):
                edge_copy(k, lon).wait()

        @pl.when(jnp.logical_not(polar))
        def _():
            for k in range(2, lon_count - 1):
                edge_recv[k] = jnp.zeros(edge_recv.shape[1:], jnp.float32)

        scale_load.wait()
        k_of = lax.rem(lane, edges)

        def beside(value):
            plus = pltpu.roll(value, 1, 1)
            minus = pltpu.roll(value, LANES - 1, 1)
            last = pltpu.roll(value, LANES - edges + 1, 1)
            first = pltpu.roll(value, edges - 1, 1)
            inner = jnp.where(lax.rem(k_of, 2) == 0, plus, minus)
            return jnp.where(k_of == 0, last, jnp.where(k_of == edges - 1, first, inner))

        for w in range(edge_vregs):
            own = []
            for c in range(3):
                a = c * edge_vregs + w
                slot = a % lon_count
                parts = []
                for k in range(lon_count):
                    source = lax.rem(lon + lon_count - k, lon_count)
                    value = edge_recv[k, a // lon_count] if k else edge_send[a // lon_count]
                    value = jnp.where(k_of // 2 == slot, value, 0.0)
                    parts.append(pltpu.roll(value, lax.rem(2 * (source - slot) + LANES, LANES), 1))
                own.append((parts[0] + parts[1]) + (parts[2] + parts[3]))
            h, u, v = [beside(value) for value in own]
            factor = scale[w]
            delta[0, w] = factor * (h * u)
            delta[1, w] = factor * (own[1] * u + h)
            delta[2, w] = factor * (own[1] * v)

    def edge_terms(c, start, count):
        terms = []
        for i in range(count // SUB):
            g = start // SUB + i
            value = delta[c, g // edge_groups]
            shift = lax.rem(EDGE + LANES - lax.rem(g, edge_groups) * edges, LANES)
            value = pltpu.roll(value, shift, 1)
            terms.append(jnp.where(jnp.logical_and(lane >= EDGE, lane < EDGE + edges), value, 0.0))
        return jnp.concatenate(terms, axis=0)

    def add_edges(c, start, count, value):
        at_lane = lax.broadcasted_iota(jnp.int32, (count, LANES), 1)
        first = pltpu.roll(value, LANES - EDGE - 2 * lon, 1)
        last = pltpu.roll(value, LANES - EDGE - 2 * lon - 1 + rest - 1, 1)
        at = pl.ds(start, count)
        out_ref[c, at, :LANES] = out_ref[c, at, :LANES] + jnp.where(at_lane == 0, first, 0.0)
        end = jnp.where(at_lane == rest - 1, last, 0.0)[:, :rest]
        out_ref[c, at, cols - rest :] = out_ref[c, at, cols - rest :] + end

    def tile_of(t):
        return slice(t * LANES, min((t + 1) * LANES, cols))

    def read(ref, c, start, count, t):
        value = ref[c, pl.ds(aligned(start), count), tile_of(t)]
        if t == tiles - 1 and rest:
            value = jnp.concatenate([value, jnp.zeros((count, LANES - rest), jnp.float32)], axis=1)
        return value

    def tendency_block(b, use):
        start = pl.multiple_of(b * ROWS, ROWS)
        terms = geo[pl.ds(start, ROWS), :]
        zonal, up, down, turn, metric = [
            jnp.broadcast_to(terms[:, i : i + 1], (ROWS, LANES)) for i in range(5)
        ]
        held = {}

        def here(c, t):
            if (0, c, t) not in held:
                held[0, c, t] = read(xp, c, start + SUB, ROWS, t)
            return held[0, c, t]

        def moved(c, t, shift):
            if (shift, c, t) not in held:
                held[shift, c, t] = pltpu.roll(here(c, t), shift, 1)
            return held[shift, c, t]

        for t in range(tiles):
            east_of, west_of, north, south = [], [], [], []
            for c in range(3):
                right = moved(c, t + 1, LANES - 1) if t < tiles - 1 else 0.0
                edge_lane = LANES - 1 if t < tiles - 1 else (rest or LANES) - 1
                east_of.append(jnp.where(lane2 == edge_lane, right, moved(c, t, LANES - 1)))
                left = moved(c, t - 1, 1) if t > 0 else 0.0
                west_of.append(jnp.where(lane2 == 0, left, moved(c, t, 1)))
                value = here(c, t)
                low, high = value[:SUB], value[SUB:]
                after = read(xp, c, start + SUB + ROWS, SUB, t)
                before = read(xp, c, start, SUB, t)
                north.append(jnp.concatenate([
                    pltpu.roll(jnp.where(sub == 0, high, low), SUB - 1, 0),
                    pltpu.roll(jnp.where(sub == 0, after, high), SUB - 1, 0),
                ], axis=0))
                south.append(jnp.concatenate([
                    pltpu.roll(jnp.where(sub == SUB - 1, before, low), 1, 0),
                    pltpu.roll(jnp.where(sub == SUB - 1, low, high), 1, 0),
                ], axis=0))
            u, v = here(1, t), here(2, t)
            t_h = -zonal * (east_of[0] * east_of[1] - west_of[0] * west_of[1]) - (
                up * (north[0] * north[2]) - down * (south[0] * south[2])
            )
            turning = turn + metric * u
            zu = zonal * u
            hv = 0.5 * v
            t_u = (
                turning * v - zu * (east_of[1] - west_of[1]) - hv * (north[1] - south[1])
                - zonal * (east_of[0] - west_of[0])
            )
            t_v = (
                -turning * u - zu * (east_of[2] - west_of[2]) - hv * (north[2] - south[2])
                - 0.5 * (north[0] - south[0])
            )
            use(start, t, (t_h, t_u, t_v))

    def put(c, start, t, value):
        out_ref[c, pl.ds(start, ROWS), tile_of(t)] = value[:, : min(LANES, cols - t * LANES)]

    def plain(start, t, values):
        for c in range(3):
            put(c, start, t, read(old, c, start, ROWS, t) + step_scale * values[c])

    span_near = lines // 2
    span_far = lines // 4
    spans = [(0, span_near), (span_near, span_near), (2 * span_near, span_far)]

    def far_copy(i, k):
        first, count = spans[k]
        return pltpu.make_async_remote_copy(
            src_ref=send.at[i, pl.ds(first, count), :], dst_ref=recv.at[i, pl.ds(first, count), :],
            send_sem=far_send.at[i, k], recv_sem=far_recv.at[i, k],
            device_id={"lon": (west, east, across)[k]}, device_id_type=MESH,
        )

    def far_start(i):
        for k in range(3):
            far_copy(i, k).start()

    def ordered(i, count):
        return jnp.where(lat == 0, i, count - 1 - i)

    def operand(i):
        value = lhs[i]
        return jnp.concatenate([value, value[:, :MAIN]], axis=1)

    def turned(value, shift):
        shift = shift % LANES
        return pltpu.roll(value, shift, 1) if shift else value

    def merged(slots, size):
        at = lax.broadcasted_iota(jnp.int32, slots[0].shape, 1)
        whole = slots[-1]
        for s in range(len(slots) - 2, -1, -1):
            whole = jnp.where(at < (s + 1) * size, slots[s], whole)
        return whole

    def modulated(i, b):
        def use(start, t, values):
            at = pl.ds(start, ROWS)
            own = wave[at, 2 * width :]
            turn_cos = wave[at, t * LANES : (t + 1) * LANES]
            turn_sin = wave[at, width + t * LANES : width + (t + 1) * LANES]
            for c in range(3):
                value = values[c]
                put(c, start, t, read(old, c, start, ROWS, t) + own * value)
                for channel, factor in enumerate((turn_cos, turn_sin)):
                    first = channel * lines + c * chunk + lax.rem(b, per_chunk) * ROWS
                    line = pl.ds(pl.multiple_of(first, ROWS), ROWS)
                    high, back, low = high_low(value * factor)
                    if t < tiles - 1:
                        lhs[i, line, t * LANES : (t + 1) * LANES] = high
                        lhs[i, line, MAIN + t * LANES : MAIN + (t + 1) * LANES] = low.astype(jnp.bfloat16)
                    else:
                        mixed = jnp.where(lane2 < rest, back, pltpu.roll(low, rest, 1))
                        lhs[i, line, 2 * MAIN : 2 * MAIN + LANES] = mixed.astype(jnp.bfloat16)
                        lhs[i, line, 2 * MAIN + LANES :] = high

        return use

    def make_lines(i, first, count):
        @pl.loop(first // 2, (first + count) // 2)
        def _(pair):
            for p in range(2):
                b = ordered(pair * 2 + p, blocks)
                tendency_block(b, modulated(i, b))

    def make_moments(i):
        both = dot(operand(i), moment[...])
        part[i, :, MAIN:] = both[:, LANES:]
        moments = both[:, :LANES]
        for k, (first, _, size) in enumerate(RANKS):
            count = spans[k][1]
            slots = []
            for s in range(LANES // size):
                origin = (s % 2) * lines + (s // 2) * count
                slots.append(turned(moments[origin : origin + count], s * size - first))
            send[i, pl.ds(spans[k][0], count), :] = merged(slots, size)

    def make_local(i):
        part[i, :, :MAIN] = dot(operand(i), local[...])

    @pl.when(polar)
    def _():
        cut_start = jnp.where(lat == 0, 0, rows)
        for copy in wave_loads:
            copy.wait()
        cuts = cut_ref[...].astype(jnp.float32)[None, :]

        @pl.loop(0, rows // chunk)
        def _(i):
            start = pl.multiple_of(i * chunk, chunk)
            wanted = cut_start + start + lax.broadcasted_iota(jnp.int32, (chunk, 2 * rows), 0)
            hit = wanted == lax.broadcasted_iota(jnp.int32, (chunk, 2 * rows), 1)
            limit = jnp.sum(jnp.where(hit, cuts, 0.0), axis=1, keepdims=True)
            turns = jnp.minimum(2.0 * limit + 1.0, float(total))
            digit = LANES // 2
            upper = jnp.floor(turns * (1.0 / digit))
            lower = turns - digit * upper
            place = lax.rem(lax.broadcasted_iota(jnp.int32, (chunk, LANES), 1), digit).astype(jnp.float32)

            def lookup(value, k):
                found = (place == value).astype(jnp.bfloat16)
                return dot(jnp.concatenate([found, found[:, :digit]], axis=1), phase[k])

            a, z = lookup(upper, 0), lookup(lower, 1)
            at = pl.ds(start, chunk)
            wave[at, :width] = a[:, :width] * z[:, :width] - a[:, width : 2 * width] * z[:, width : 2 * width]
            wave[at, width : 2 * width] = (
                a[:, width : 2 * width] * z[:, :width] + a[:, :width] * z[:, width : 2 * width]
            )
            wave[at, 2 * width :] = a[:, 2 * width :] + z[:, 2 * width :]

        geo_load.wait()
        old_load.wait()
        moment_load.wait()
        make_lines(0, 0, per_chunk)
        make_moments(0)

    neighbours_enter()

    @pl.when(jnp.logical_not(polar))
    def _():
        for copy in wave_loads:
            copy.wait()
        geo_load.wait()
        old_load.wait()
        moment_load.wait()
        local_load.wait()
        field_load.wait()

        @pl.loop(0, blocks // 2 - 1)
        def _(pair):
            for p in range(2):
                tendency_block(2 * pair + 1 + p, plain)

        halos_arrive()

        @pl.loop(0, 2)
        def _(side):
            tendency_block(side * (blocks - 1), plain)

        edges_arrive()

        @pl.loop(0, blocks)
        def _(b):
            start = pl.multiple_of(b * ROWS, ROWS)
            for c in range(3):
                add_edges(c, start, ROWS, step_scale * edge_terms(c, start, ROWS))

    @pl.when(polar)
    def _():
        far_start(0)

        @pl.loop(1, chunks - 1)
        def _(i):
            make_lines(i, i * per_chunk, per_chunk)
            make_moments(i)
            far_start(i)

        make_lines(chunks - 1, (chunks - 1) * per_chunk, per_chunk - 2)
        halos_arrive()
        make_lines(chunks - 1, blocks - 2, 2)
        make_moments(chunks - 1)
        far_start(chunks - 1)
        local_load.wait()

        @pl.loop(0, chunks)
        def _(i):
            make_local(i)

        edges_arrive()
        field_load.wait()

        @pl.loop(0, chunks)
        def _(i):
            start = pl.multiple_of(ordered(i, chunks) * chunk, ROWS)
            at = pl.ds(start, chunk)
            turn_cos = wave[at, :width]
            turn_sin = wave[at, width : 2 * width]
            terms = [edge_terms(c, start, chunk) for c in range(3)]
            at_edge = jnp.concatenate(
                [term * turn[:, width - LANES :] for turn in (turn_cos, turn_sin) for term in terms], axis=0
            )
            for k in range(3):
                far_copy(i, k).wait_recv()
            gathered = []
            for k, (first, _, size) in enumerate(RANKS):
                value = recv[i, pl.ds(spans[k][0], spans[k][1]), :]
                slots = [turned(value, first - s * size) for s in range(LANES // size)]
                gathered.append(jnp.concatenate(slots[0::2] + slots[1::2], axis=0))
            at_lane = lax.broadcasted_iota(jnp.int32, (2 * lines, LANES), 1)
            coming = jnp.where(
                at_lane < NEAR, gathered[0],
                jnp.where(at_lane < 2 * NEAR, gathered[1], jnp.where(at_lane < EDGE, gathered[2], at_edge)),
            )
            _, high, low = high_low(coming)
            used = EDGE + edges
            low = pltpu.roll(low, used, 1)
            left = jnp.where(at_lane < used, high, low)
            right = jnp.where(at_lane < 2 * used - LANES, low, pltpu.roll(high, 2 * used - LANES, 1))
            factors = jnp.concatenate([left.astype(jnp.bfloat16), right.astype(jnp.bfloat16)], axis=1)
            whole = part[i] + dot(factors, field[...])
            own = wave[at, 2 * width :]
            for c in range(3):
                by_cos = whole[c * chunk : (c + 1) * chunk, :cols]
                by_sin = whole[lines + c * chunk : lines + (c + 1) * chunk, :cols]
                out_ref[c, at, :] = out_ref[c, at, :] + turn_sin[:, :cols] * by_cos - turn_cos[:, :cols] * by_sin
                add_edges(c, start, chunk, own * terms[c])

        @pl.loop(0, chunks)
        def _(i):
            for k in range(3):
                far_copy(i, k).wait_send()


def fused_step(mesh_shape, tables, state_now, state_old, polar_cutoff):
    lat_count, lon_count = mesh_shape
    comps, rows, cols = state_now.shape
    chunk = chunk_rows(rows)
    chunks = rows // chunk
    lines = comps * chunk
    width = -(-cols // LANES) * LANES
    geo, scale, phase, local, moment, field = tables
    operands = [
        pltpu.with_memory_space_constraint(jnp.asarray(a), pltpu.HBM)
        for a in (state_now, state_old, geo, scale, polar_cutoff, phase, local, moment, field)
    ]
    hbm_spec = pl.BlockSpec(memory_space=pltpu.HBM)
    vmem_spec = pl.BlockSpec(memory_space=pltpu.VMEM)
    dma = pltpu.SemaphoreType.DMA
    packed = (-(-comps * scale.shape[1] // lon_count), SUB, LANES)
    exchange = pltpu.VMEM((chunks, lines // 2 * 2 + lines // 4, LANES), jnp.float32)
    return pl.pallas_call(
        functools.partial(step_kernel, lat_count, lon_count, chunk),
        out_shape=jax.ShapeDtypeStruct(state_now.shape, jnp.float32),
        in_specs=[hbm_spec] * 9,
        out_specs=vmem_spec,
        scratch_shapes=[
            pltpu.VMEM((comps, rows, cols), jnp.float32),
            pltpu.VMEM((comps, rows + 2 * SUB, cols), jnp.float32),
            pltpu.VMEM((rows, LANES), jnp.float32),
            pltpu.VMEM(scale.shape[1:], jnp.float32),
            pltpu.VMEM((2 * rows,), jnp.int32),
            pltpu.VMEM(phase.shape[1:], jnp.bfloat16),
            pltpu.VMEM(local.shape, jnp.bfloat16),
            pltpu.VMEM(moment.shape, jnp.bfloat16),
            pltpu.VMEM(field.shape[1:], jnp.bfloat16),
            pltpu.VMEM((rows, 2 * width + LANES), jnp.float32),
            pltpu.VMEM((chunks, 2 * lines, 2 * MAIN + 2 * LANES), jnp.bfloat16),
            pltpu.VMEM((chunks, 2 * lines, width), jnp.float32),
            exchange,
            exchange,
            pltpu.VMEM(packed, jnp.float32),
            pltpu.VMEM((lon_count, *packed), jnp.float32),
            pltpu.VMEM((comps, *scale.shape[1:]), jnp.float32),
            dma((3,)), dma((8,)), dma((2,)), dma((2,)), dma((lon_count,)), dma((lon_count,)),
            dma((chunks, 3)), dma((chunks, 3)),
        ],
        compiler_params=pltpu.CompilerParams(
            collective_id=0, has_side_effects=True, vmem_limit_bytes=40 * 1024 * 1024
        ),
    )(*operands)


def chunk_rows(rows):
    return rows // 3 if rows % 96 == 0 else 0


def solution(mesh):
    lat_count, lon_count = mesh.shape["lat"], mesh.shape["lon"]

    def step(state_now, state_old, polar_cutoff):
        comps, lat_total, lon_total = state_now.shape
        rows, cols = lat_total // lat_count, lon_total // lon_count
        fits = (
            lat_count == 4 and lon_count == 4 and lat_total == 4 * rows and chunk_rows(rows) > 0
            and cols == MAIN + LANES // 2 and rows // SUB <= LANES and comps == 3 * mesh.shape["ens"]
        )
        body = per_device
        if fits:
            geo = geometry_table(lat_total, lon_total)
            tables = (
                geo, edge_scale(geo, lat_count, lon_count), phase_tables(cols, lon_count),
                *convolution_tables(cols, lon_count),
            )
            body = functools.partial(fused_step, (lat_count, lon_count), tables)
        return jax.shard_map(
            body,
            mesh=mesh,
            in_specs=(P("ens", "lat", "lon"), P("ens", "lat", "lon"), P()),
            out_specs=P("ens", "lat", "lon"),
            check_vma=False,
        )(state_now, state_old, polar_cutoff)

    return step
```

```python
import functools
import math

import jax
import jax.numpy as jnp
import numpy as np
from jax import lax
from jax.experimental import pallas as pl
from jax.experimental.pallas import tpu as pltpu
from jax.sharding import PartitionSpec as P

LANES = 128
SUB = 8
MESH = pl.DeviceIdType.MESH
step_scale = 0.2
coriolis = 2.0
gravity = 1.0
highest = lax.Precision.HIGHEST


def padded(value, sides, width, wrap):
    for axis, dim in sides:
        devices, length = (lax.axis_size(axis), value.shape[dim])
        up = [(i, (i + 1) % devices) for i in range(devices if wrap else devices - 1)]
        down = [(j, i) for i, j in up]
        last = lax.slice_in_dim(value, length - width, length, axis=dim)
        leading = lax.slice_in_dim(value, 0, width, axis=dim)
        before = lax.ppermute(last, axis, up)
        after = lax.ppermute(leading, axis, down)
        value = jnp.concatenate([before, value, after], axis=dim)
    return value


def latitude_terms(row_index, lat_total):
    distance = jnp.minimum(row_index + 0.5, lat_total - row_index - 0.5)
    cosine_lat = jnp.sin(math.pi * distance / lat_total)
    sine_lat = -jnp.cos(math.pi * (row_index + 0.5) / lat_total)
    return (cosine_lat, sine_lat)


def tendencies(lat_padded, lon_padded, cos_ext, sine_lat, lat_total, lon_total):
    cosine_lat = cos_ext[1:-1]
    zonal_scale = (lon_total / (4.0 * lat_total) / cosine_lat)[:, None]
    metric = math.pi / lat_total * sine_lat / cosine_lat
    depth_lon, east_lon, north_lon = (lon_padded[0], lon_padded[1], lon_padded[2])
    depth_lat, east_lat, north_lat = (lat_padded[0], lat_padded[1], lat_padded[2])
    east = east_lon[:, 1:-1]
    north = north_lon[:, 1:-1]

    def zonal_change(field):
        return zonal_scale * (field[:, 2:] - field[:, :-2])

    def northward_change(field):
        return 0.5 * (field[2:] - field[:-2])

    mass_flux = depth_lat * north_lat * cos_ext[:, None]
    tend_depth = (
        -zonal_change(depth_lon * east_lon) - northward_change(mass_flux) / cosine_lat[:, None]
    )
    turning = coriolis * sine_lat[:, None] + metric[:, None] * east
    tend_east = (
        -east * zonal_change(east_lon)
        - north * northward_change(east_lat)
        + turning * north
        - gravity * zonal_change(depth_lon)
    )
    tend_north = (
        -east * zonal_change(north_lon)
        - north * northward_change(north_lat)
        - turning * east
        - gravity * northward_change(depth_lat)
    )
    return jnp.stack([tend_depth, tend_east, tend_north])


def angle_table(first_count, second_count, period):
    first_idx = jnp.arange(first_count, dtype=jnp.int32)
    second_idx = jnp.arange(second_count, dtype=jnp.int32)
    turns = first_idx[:, None] * second_idx[None, :] % period
    phase = turns.astype(jnp.float32) * (2.0 * math.pi / period)
    return (jnp.cos(phase), jnp.sin(phase))


def low_pass(signal, cutoff):
    count, length = signal.shape
    first = 1
    probe = 1
    while probe * probe <= length:
        if length % probe == 0:
            first = probe
        probe = probe + 1
    second = length // first
    cos_first, sin_first = angle_table(first, first, first)
    cos_second, sin_second = angle_table(second, second, second)
    cos_twist, sin_twist = angle_table(first, second, length)
    grid = signal.reshape(count, first, second)
    part_re = jnp.einsum("cpq,pk->ckq", grid, cos_first, precision=highest)
    part_im = -jnp.einsum("cpq,pk->ckq", grid, sin_first, precision=highest)
    twist_re = part_re * cos_twist + part_im * sin_twist
    twist_im = part_im * cos_twist - part_re * sin_twist
    spec_re = jnp.einsum("ckq,qm->ckm", twist_re, cos_second, precision=highest) + jnp.einsum(
        "ckq,qm->ckm", twist_im, sin_second, precision=highest
    )
    spec_im = jnp.einsum("ckq,qm->ckm", twist_im, cos_second, precision=highest) - jnp.einsum(
        "ckq,qm->ckm", twist_re, sin_second, precision=highest
    )
    wave = (
        jnp.arange(first, dtype=jnp.int32)[:, None]
        + first * jnp.arange(second, dtype=jnp.int32)[None, :]
    )
    limit = cutoff[:, None, None]
    keep = ((wave[None] <= limit) | (wave[None] >= length - limit)).astype(jnp.float32) * (
        1.0 / length
    )
    spec_re = spec_re * keep
    spec_im = spec_im * keep
    back_re = jnp.einsum("ckm,mq->ckq", spec_re, cos_second, precision=highest) - jnp.einsum(
        "ckm,mq->ckq", spec_im, sin_second, precision=highest
    )
    back_im = jnp.einsum("ckm,mq->ckq", spec_im, cos_second, precision=highest) + jnp.einsum(
        "ckm,mq->ckq", spec_re, sin_second, precision=highest
    )
    turn_re = back_re * cos_twist - back_im * sin_twist
    turn_im = back_im * cos_twist + back_re * sin_twist
    result = jnp.einsum("ckq,kp->cpq", turn_re, cos_first, precision=highest) - jnp.einsum(
        "ckq,kp->cpq", turn_im, sin_first, precision=highest
    )
    return result.reshape(count, length)


def per_device(state_now, state_old, polar_cutoff):
    lat_rows = state_now.shape[1]
    lon_cols = state_now.shape[2]
    lat_count = lax.axis_size("lat")
    lon_count = lax.axis_size("lon")
    lat_total = lat_rows * lat_count
    lon_total = lon_cols * lon_count
    lat_place = lax.axis_index("lat")
    lat_padded = padded(state_now, (("lat", 1),), 1, False)
    lon_padded = padded(state_now, (("lon", 2),), 1, True)
    row_index = (lat_place * lat_rows + jnp.arange(-1, lat_rows + 1, dtype=jnp.int32)).astype(
        jnp.float32
    )
    cos_ext, sin_ext = latitude_terms(row_index, lat_total)
    forcing = tendencies(lat_padded, lon_padded, cos_ext, sin_ext[1:-1], lat_total, lon_total)
    groups = lat_count * lon_count
    share = lat_rows // groups
    member = lax.axis_index(("lat", "lon"))
    south_cut = lax.dynamic_slice_in_dim(polar_cutoff, member * share, share)
    north_cut = lax.dynamic_slice_in_dim(polar_cutoff, lat_rows + member * share, share)
    band_cut = jnp.concatenate([south_cut, north_cut])
    block = lax.all_to_all(forcing, ("lat", "lon"), split_axis=1, concat_axis=2, tiled=True)
    items = block.shape[0]
    wide = block.shape[2]
    south_rows = block[:, :, :lon_total]
    north_rows = block[:, :, wide - lon_total :]
    polar_rows = jnp.concatenate([south_rows, north_rows], axis=1)
    smooth = low_pass(polar_rows.reshape(items * 2 * share, lon_total), jnp.tile(band_cut, items))
    smooth = smooth.reshape(items, 2 * share, lon_total)
    rebuilt = jnp.concatenate(
        [smooth[:, :share], block[:, :, lon_total : wide - lon_total], smooth[:, share:]], axis=2
    )
    filtered = lax.all_to_all(rebuilt, ("lat", "lon"), split_axis=2, concat_axis=1, tiled=True)
    return state_old + step_scale * filtered


NEAR = 28
FAR = 16
MAIN = 4 * LANES
ROWS = 16
EDGE = 2 * NEAR + FAR
RANKS = [(0, NEAR, 32), (NEAR, NEAR, 32), (2 * NEAR, FAR, 16)]


def split_table(table):
    table = np.asarray(table, np.float32)
    high = table.astype(jnp.bfloat16)
    rest = table - high.astype(np.float32)
    middle = rest.astype(jnp.bfloat16)
    low = (rest - middle.astype(np.float32)).astype(jnp.bfloat16)
    return high, middle, low


def kernel_values(offset, total):
    safe = np.where(offset == 0, 1, offset)
    return np.where(offset == 0, 0.0, 1.0 / (total * np.sin(np.pi * safe / total)))


def stacked(table, cols):
    high, low, _ = split_table(table)
    zero = np.zeros((2 * LANES - 3 * (cols - MAIN), table.shape[1]), high.dtype)
    tail = [high[MAIN:], high[MAIN:], low[MAIN:], zero]
    return np.concatenate([high[:MAIN], high[:MAIN], *tail, low[:MAIN]])


def edge_columns(cols, lon_count):
    start = np.arange(lon_count) * cols
    return np.stack([start, start + cols - 1], axis=1).reshape(-1)


def convolution_tables(cols, lon_count):
    total = cols * lon_count
    width = -(-cols // LANES) * LANES
    here = np.arange(cols)
    target, source = here[:, None], here[None, :]
    local = np.zeros((cols, width))
    local[:, :cols] = step_scale * kernel_values(target - source, total).T
    moments = np.zeros((cols, LANES))
    fields = np.zeros((lon_count, LANES, width))
    lon = np.arange(lon_count)
    edge = edge_columns(cols, lon_count)
    places = [(-1, 0, NEAR), (1, NEAR, NEAR), (2, 2 * NEAR, FAR)]
    for step, start, rank in places:
        block = kernel_values(target - source + step * cols, total)
        left, scale, right = np.linalg.svd(block)
        moments[:, start : start + rank] = right[:rank].T
        back = step_scale * scale[:rank, None] * left[:, :rank].T
        for q in lon:
            origin = (q - step) % lon_count
            sign = 1.0 if q - origin == step else -1.0
            fields[q, start : start + rank, :cols] = sign * back
    piled = []
    for q in lon:
        offset = q * cols + here[None, :] - edge[:, None]
        fields[q, EDGE : EDGE + len(edge), :cols] = step_scale * kernel_values(offset, total)
        high, low, _ = split_table(fields[q])
        used = EDGE + len(edge)
        gap = np.zeros((2 * LANES - 3 * used, width), high.dtype)
        piled.append(np.concatenate([high[:used], high[:used], low[:used], gap]))
    local = stacked(local, cols)
    first = np.concatenate([stacked(moments, cols), local[:, MAIN:]], axis=1)
    return local[:, :MAIN], first, np.stack(piled)


def phase_tables(cols, lon_count):
    total = cols * lon_count
    width = -(-cols // LANES) * LANES
    digit = LANES // 2
    coarse, fine = [], []
    edge = edge_columns(cols, lon_count)
    at_edge = MAIN + EDGE + np.arange(len(edge))
    for q in range(lon_count):
        m = q * cols + np.arange(cols)[None, :]
        for out, unit in ((coarse, digit), (fine, 1)):
            k = unit * np.arange(digit)[:, None]
            table = np.zeros((digit, 2 * width + LANES))
            for columns, places in ((m, np.arange(cols)), (edge[None, :], at_edge)):
                angle = np.pi * ((k * columns) % (2 * total)) / total
                table[:, places] = np.cos(angle)
                table[:, width + places] = np.sin(angle)
            table[:, 2 * width :] = step_scale * k / total
            parts = split_table(table)
            out.append(np.concatenate(parts))
    return np.stack([np.stack(coarse), np.stack(fine)], axis=1)


def geometry_table(lat_total, lon_total):
    j = np.arange(lat_total, dtype=np.float64)

    def cosine(row):
        return np.sin(np.pi * np.minimum(row + 0.5, lat_total - row - 0.5) / lat_total)

    c = cosine(j)
    s = -np.cos(np.pi * (j + 0.5) / lat_total)
    table = np.zeros((lat_total, LANES))
    table[:, 0] = lon_total / (4.0 * lat_total * c)
    table[:, 1] = 0.5 * cosine(j + 1) / c
    table[:, 2] = 0.5 * cosine(j - 1) / c
    table[:, 3] = coriolis * s
    table[:, 4] = np.pi / lat_total * s / c
    return table.astype(np.float32)


def edge_scale(geo, lat_count, lon_count, chunk):
    rows = len(geo) // lat_count
    edges = 2 * lon_count
    per = LANES // edges
    count = -(-((rows + chunk) // SUB) // per)
    table = np.zeros((lat_count, count, SUB, LANES), np.float32)
    for lat in range(lat_count):
        first = lat * rows
        held = [first + g * SUB for g in range(rows // SUB)]
        extra = {1: first - chunk, lat_count - 2: first + rows}
        if lat in extra:
            held += [extra[lat] + g * SUB for g in range(chunk // SUB)]
        for g, row in enumerate(held):
            zonal = geo[row : row + SUB, 0]
            for k in range(edges):
                table[lat, g // per, :, g % per * edges + k] = zonal if k % 2 == 0 else -zonal
    return table


def dot(a, b):
    return lax.dot_general(a, b, (((1,), (0,)), ((), ())), preferred_element_type=jnp.float32)


def high_low(value):
    high = value.astype(jnp.bfloat16)
    back = high.astype(jnp.float32)
    return high, back, value - back


def step_kernel(
    lat_count, lon_count, chunk,
    x_hbm, geo_hbm, scale_hbm, cut_hbm, phase_hbm, local_hbm, moment_hbm, field_hbm, out_ref,
    xp, geo, scale, cut_ref, phase, local, moment, field, wave, lhs, part, send, recv,
    edge_send, edge_recv, delta, gain, load_sem, table_sem, row_send_sem, row_recv_sem,
    edge_send_sem, edge_recv_sem, far_send, far_recv, back_send, back_recv,
):
    rows, cols = out_ref.shape[1], out_ref.shape[2]
    blocks = rows // ROWS
    per_chunk = chunk // ROWS
    groups = rows // SUB
    margin = chunk + SUB
    total = lon_count * cols
    tiles = -(-cols // LANES)
    width = tiles * LANES
    rest = cols % LANES
    lines = 3 * chunk
    edges = 2 * lon_count
    edge_groups = LANES // edges
    edge_vregs = scale.shape[0]
    lat = lax.axis_index("lat")
    lon = lax.axis_index("lon")
    west = lax.rem(lon + lon_count - 1, lon_count)
    east = lax.rem(lon + 1, lon_count)
    across = lax.rem(lon + 2, lon_count)
    polar = jnp.logical_or(lat == 0, lat == lat_count - 1)
    helper = jnp.logical_not(polar)
    southern = lat < 2
    odd = lax.rem(lat, 2)
    mate = lat + 1 - 2 * odd
    most = rows // chunk - 1
    chunks = jnp.where(polar, most, 1)

    def aligned(i):
        return pl.multiple_of(i, SUB)

    chunk_zero = jnp.where(
        polar, jnp.where(southern, 0, chunk), jnp.where(southern, -chunk, rows)
    )
    geo_zero = odd * chunk
    cut_zero = jnp.where(southern, 0, rows) + jnp.where(
        polar, jnp.where(southern, 0, chunk), jnp.where(southern, rows - chunk, 0)
    )
    group_zero = jnp.where(polar, jnp.where(southern, 0, chunk // SUB), groups)

    loads = [
        pltpu.make_async_copy(x_hbm.at[c], xp.at[c, pl.ds(margin, rows), :], load_sem.at[c]) for c in range(3)
    ]
    for copy in loads:
        copy.start()
    geo_load = pltpu.make_async_copy(
        geo_hbm.at[pl.ds(aligned(lat * rows - geo_zero), rows + chunk), :], geo, table_sem.at[0]
    )
    wave_loads = [
        pltpu.make_async_copy(cut_hbm, cut_ref, table_sem.at[1]),
        pltpu.make_async_copy(phase_hbm.at[lon], phase, table_sem.at[2]),
    ]
    moment_load = pltpu.make_async_copy(moment_hbm, moment, table_sem.at[4])
    local_load = pltpu.make_async_copy(local_hbm, local, table_sem.at[5])
    field_load = pltpu.make_async_copy(field_hbm.at[lon], field, table_sem.at[6])
    scale_load = pltpu.make_async_copy(scale_hbm.at[lat], scale, table_sem.at[7])
    for copy in [geo_load, *wave_loads]:
        copy.start()

    barrier = pltpu.get_barrier_semaphore()
    for k in range(1, lon_count):
        pl.semaphore_signal(
            barrier, inc=1, device_id={"lon": lax.rem(lon + k, lon_count)}, device_id_type=MESH
        )
    pl.semaphore_signal(barrier, inc=1, device_id={"lat": mate}, device_id_type=MESH)

    @pl.when(helper)
    def _():
        pl.semaphore_signal(
            barrier, inc=1, device_id={"lat": lat_count - 1 - lat}, device_id_type=MESH
        )

    pl.semaphore_wait(barrier, lon_count + helper.astype(jnp.int32))

    def row_copy(which, source, target, count, device):
        return pltpu.make_async_remote_copy(
            src_ref=x_hbm.at[:, pl.ds(aligned(source), count), :],
            dst_ref=xp.at[:, pl.ds(aligned(target), count), :],
            send_sem=row_send_sem.at[which], recv_sem=row_recv_sem.at[which],
            device_id={"lat": device}, device_id_type=MESH,
        )

    def give():
        source = jnp.where(southern, rows - margin, 0)
        target = jnp.where(southern, 0, margin + rows)
        return row_copy(0, source, target, margin, mate)

    def swap():
        source = jnp.where(southern, rows - SUB, 0)
        target = jnp.where(southern, margin - SUB, margin + rows)
        return row_copy(1, source, target, SUB, lat_count - 1 - lat)

    @pl.when(polar)
    def _():
        give().start()

    @pl.when(helper)
    def _():
        swap().start()

    lane = lax.broadcasted_iota(jnp.int32, (SUB, LANES), 1)
    lane2 = lax.broadcasted_iota(jnp.int32, (ROWS, LANES), 1)
    sub = lax.broadcasted_iota(jnp.int32, (SUB, LANES), 0)

    @pl.when(polar)
    def _():
        start = jnp.where(southern, margin - SUB, margin + rows)
        xp[:, pl.ds(aligned(start), SUB), :] = jnp.zeros((3, SUB, cols), jnp.float32)

    for copy in loads:
        copy.wait()
    for copy in [moment_load, scale_load, local_load, field_load]:
        copy.start()

    def edge_copy(k, source):
        target = lax.rem(source + k, lon_count)
        return pltpu.make_async_remote_copy(
            src_ref=edge_send, dst_ref=edge_recv.at[k],
            send_sem=edge_send_sem.at[k], recv_sem=edge_recv_sem.at[k],
            device_id={"lon": target}, device_id_type=MESH,
        )

    def edges_leave(count):
        for first in range(0, 3 * edge_vregs, lon_count):
            packed = jnp.zeros((SUB, LANES), jnp.float32)
            for a in range(first, min(first + lon_count, 3 * edge_vregs)):
                c, w = a // edge_vregs, a % edge_vregs
                for g in range(w * edge_groups, min((w + 1) * edge_groups, count)):
                    start = g * SUB if g < groups else chunk_zero + (g - groups) * SUB
                    block = pl.ds(aligned(margin + start), SUB)
                    at = g % edge_groups * edges + 2 * (a - first)
                    packed = jnp.where(lane == at, xp[c, block, 0:1], packed)
                    packed = jnp.where(lane == at + 1, xp[c, block, cols - 1 : cols], packed)
            edge_send[first // lon_count] = packed
        for k in range(1, lon_count):
            edge_copy(k, lon).start()

    def edges_arrive():
        for k in range(1, lon_count):
            edge_copy(k, lon).wait()
        scale_load.wait()
        k_of = lax.rem(lane, edges)

        def beside(value):
            plus = pltpu.roll(value, 1, 1)
            minus = pltpu.roll(value, LANES - 1, 1)
            last = pltpu.roll(value, LANES - edges + 1, 1)
            first = pltpu.roll(value, edges - 1, 1)
            inner = jnp.where(lax.rem(k_of, 2) == 0, plus, minus)
            return jnp.where(k_of == 0, last, jnp.where(k_of == edges - 1, first, inner))

        for w in range(edge_vregs):
            own = []
            for c in range(3):
                a = c * edge_vregs + w
                slot = a % lon_count
                parts = []
                for k in range(lon_count):
                    source = lax.rem(lon + lon_count - k, lon_count)
                    value = edge_recv[k, a // lon_count] if k else edge_send[a // lon_count]
                    value = jnp.where(k_of // 2 == slot, value, 0.0)
                    parts.append(pltpu.roll(value, lax.rem(2 * (source - slot) + LANES, LANES), 1))
                own.append((parts[0] + parts[1]) + (parts[2] + parts[3]))
            h, u, v = [beside(value) for value in own]
            factor = scale[w]
            delta[0, w] = factor * (h * u)
            delta[1, w] = factor * (own[1] * u + h)
            delta[2, w] = factor * (own[1] * v)

    def edge_terms(c, i):
        terms = []
        for n in range(chunk // SUB):
            g = group_zero + i * (chunk // SUB) + n
            shift = lax.rem(EDGE + LANES - lax.rem(g, edge_groups) * edges, LANES)
            value = pltpu.roll(delta[c, g // edge_groups], shift, 1)
            terms.append(jnp.where(jnp.logical_and(lane >= EDGE, lane < EDGE + edges), value, 0.0))
        return jnp.concatenate(terms, axis=0)

    def edge_places(value):
        at_lane = lax.broadcasted_iota(jnp.int32, value.shape, 1)
        first = pltpu.roll(value, LANES - EDGE - 2 * lon, 1)
        last = pltpu.roll(value, LANES - EDGE - 2 * lon - 1 + rest - 1, 1)
        return jnp.where(at_lane == 0, first, 0.0), jnp.where(at_lane == rest - 1, last, 0.0)[:, :rest]

    def own_edges():
        for w in range(-(-groups // edge_groups)):
            for c in range(3):
                value = step_scale * pltpu.roll(delta[c, w], lax.rem(LANES - 2 * lon, LANES), 1)
                for g in range(w * edge_groups, min((w + 1) * edge_groups, groups)):
                    at, place = pl.ds(g * SUB, SUB), g % edge_groups * edges
                    first = turned(value, -place)
                    last = turned(value, rest - 2 - place)
                    out_ref[c, at, :LANES] = out_ref[c, at, :LANES] + jnp.where(lane == 0, first, 0.0)
                    end = jnp.where(lane == rest - 1, last, 0.0)[:, :rest]
                    out_ref[c, at, cols - rest :] = out_ref[c, at, cols - rest :] + end

    def tile_of(t):
        return slice(t * LANES, min((t + 1) * LANES, cols))

    def read(ref, c, start, count, t):
        value = ref[c, pl.ds(aligned(start), count), tile_of(t)]
        if t == tiles - 1 and rest:
            value = jnp.concatenate([value, jnp.zeros((count, LANES - rest), jnp.float32)], axis=1)
        return value

    def tendency_block(start, use):
        terms = geo[pl.ds(aligned(start + geo_zero), ROWS), :]
        zonal, up, down, turn, metric = [
            jnp.broadcast_to(terms[:, i : i + 1], (ROWS, LANES)) for i in range(5)
        ]
        held = {}

        def here(c, t):
            if (0, c, t) not in held:
                held[0, c, t] = read(xp, c, start + margin, ROWS, t)
            return held[0, c, t]

        def moved(c, t, shift):
            if (shift, c, t) not in held:
                held[shift, c, t] = pltpu.roll(here(c, t), shift, 1)
            return held[shift, c, t]

        for t in range(tiles):
            east_of, west_of, north, south = [], [], [], []
            for c in range(3):
                right = moved(c, t + 1, LANES - 1) if t < tiles - 1 else 0.0
                edge_lane = LANES - 1 if t < tiles - 1 else (rest or LANES) - 1
                east_of.append(jnp.where(lane2 == edge_lane, right, moved(c, t, LANES - 1)))
                left = moved(c, t - 1, 1) if t > 0 else 0.0
                west_of.append(jnp.where(lane2 == 0, left, moved(c, t, 1)))
                value = here(c, t)
                low, high = value[:SUB], value[SUB:]
                after = read(xp, c, start + margin + ROWS, SUB, t)
                before = read(xp, c, start + margin - SUB, SUB, t)
                north.append(jnp.concatenate([
                    pltpu.roll(jnp.where(sub == 0, high, low), SUB - 1, 0),
                    pltpu.roll(jnp.where(sub == 0, after, high), SUB - 1, 0),
                ], axis=0))
                south.append(jnp.concatenate([
                    pltpu.roll(jnp.where(sub == SUB - 1, before, low), 1, 0),
                    pltpu.roll(jnp.where(sub == SUB - 1, low, high), 1, 0),
                ], axis=0))
            u, v = here(1, t), here(2, t)
            t_h = -zonal * (east_of[0] * east_of[1] - west_of[0] * west_of[1]) - (
                up * (north[0] * north[2]) - down * (south[0] * south[2])
            )
            turning = turn + metric * u
            zu = zonal * u
            hv = 0.5 * v
            t_u = (
                turning * v - zu * (east_of[1] - west_of[1]) - hv * (north[1] - south[1])
                - zonal * (east_of[0] - west_of[0])
            )
            t_v = (
                -turning * u - zu * (east_of[2] - west_of[2]) - hv * (north[2] - south[2])
                - 0.5 * (north[0] - south[0])
            )
            use(t, (t_h, t_u, t_v))

    def cut_short(value, t):
        return value[:, : min(LANES, cols - t * LANES)]

    def plain(start):
        def use(t, values):
            for c in range(3):
                out_ref[c, pl.ds(aligned(start), ROWS), tile_of(t)] = cut_short(step_scale * values[c], t)

        return use

    span_near = lines // 2
    span_far = -(-lines // (4 * SUB)) * SUB
    spans = [(0, span_near), (span_near, span_near), (2 * span_near, span_far)]

    def far_copy(i, k):
        first, count = spans[k]
        return pltpu.make_async_remote_copy(
            src_ref=send.at[i, pl.ds(first, count), :], dst_ref=recv.at[i, pl.ds(first, count), :],
            send_sem=far_send.at[i, k], recv_sem=far_recv.at[i, k],
            device_id={"lon": (west, east, across)[k]}, device_id_type=MESH,
        )

    def far_start(i):
        for k in range(3):
            far_copy(i, k).start()

    def operand(i):
        value = lhs[i]
        return jnp.concatenate([value, value[:, :MAIN]], axis=1)

    def turned(value, shift):
        shift = shift % LANES
        return pltpu.roll(value, shift, 1) if shift else value

    def merged(slots, size):
        at = lax.broadcasted_iota(jnp.int32, slots[0].shape, 1)
        whole = slots[-1]
        for s in range(len(slots) - 2, -1, -1):
            whole = jnp.where(at < (s + 1) * size, slots[s], whole)
        return whole

    def kept(i, give_away):
        if give_away:
            return gain, 0
        return out_ref, pl.multiple_of(chunk_zero + i * chunk, ROWS)

    def modulated(i, b, give_away):
        keep, first_row = kept(i, give_away)
        keep_at = pl.ds(pl.multiple_of(first_row + b * ROWS, ROWS), ROWS)
        at = pl.ds(pl.multiple_of(i * chunk + b * ROWS, ROWS), ROWS)

        def use(t, values):
            own = wave[at, 2 * width :]
            turn_cos = wave[at, t * LANES : (t + 1) * LANES]
            turn_sin = wave[at, width + t * LANES : width + (t + 1) * LANES]
            for c in range(3):
                value = values[c]
                keep[c, keep_at, tile_of(t)] = cut_short(own * value, t)
                for channel, factor in enumerate((turn_cos, turn_sin)):
                    first = channel * lines + c * chunk + b * ROWS
                    line = pl.ds(pl.multiple_of(first, ROWS), ROWS)
                    high, back_value, low = high_low(value * factor)
                    if t < tiles - 1:
                        lhs[i, line, t * LANES : (t + 1) * LANES] = high
                        lhs[i, line, MAIN + t * LANES : MAIN + (t + 1) * LANES] = low.astype(jnp.bfloat16)
                    else:
                        mixed = jnp.where(lane2 < rest, back_value, pltpu.roll(low, rest, 1))
                        lhs[i, line, 2 * MAIN : 2 * MAIN + LANES] = mixed.astype(jnp.bfloat16)
                        lhs[i, line, 2 * MAIN + LANES :] = high

        return use

    def make_lines(i, give_away):
        @pl.loop(0, per_chunk // 3)
        def _(three):
            for p in range(3):
                b = three * 3 + p
                tendency_block(chunk_zero + i * chunk + b * ROWS, modulated(i, b, give_away))

    def make_moments(i):
        both = dot(operand(i), moment[...])
        part[i, :, MAIN:] = both[:, LANES:]
        moments = both[:, :LANES]
        for k, (first, _, size) in enumerate(RANKS):
            count = spans[k][1]
            slots = []
            for s in range(LANES // size):
                origin = (s % 2) * lines + min((s // 2) * count, lines - count)
                slots.append(turned(moments[origin : origin + count], s * size - first))
            send[i, pl.ds(spans[k][0], count), :] = merged(slots, size)

    def make_local(count):
        value = lhs[:count].reshape(count * 2 * lines, lhs.shape[2])
        value = jnp.concatenate([value, value[:, :MAIN]], axis=1)
        part[:count, :, :MAIN] = dot(value, local[...]).reshape(count, 2 * lines, MAIN)

    geo_load.wait()

    @pl.when(helper)
    def _():
        @pl.loop(0, blocks // 2 - 1)
        def _(pair):
            for p in range(2):
                start = (2 * pair + 1 + p) * ROWS
                tendency_block(start, plain(start))

    @pl.when(polar)
    def _():
        edges_leave(groups)

    for copy in wave_loads:
        copy.wait()
    cuts = cut_ref[...].astype(jnp.float32)[None, :]

    def make_wave(count):
        wanted = cut_zero + lax.broadcasted_iota(jnp.int32, (count, 2 * rows), 0)
        hit = wanted == lax.broadcasted_iota(jnp.int32, (count, 2 * rows), 1)
        limit = jnp.sum(jnp.where(hit, cuts, 0.0), axis=1, keepdims=True)
        turns = jnp.minimum(2.0 * limit + 1.0, float(total))
        digit = LANES // 2
        upper = jnp.floor(turns * (1.0 / digit))
        lower = turns - digit * upper
        place = lax.rem(lax.broadcasted_iota(jnp.int32, (count, LANES), 1), digit).astype(jnp.float32)

        def lookup(value, k):
            found = (place == value).astype(jnp.bfloat16)
            return dot(jnp.concatenate([found, found[:, :digit]], axis=1), phase[k])

        a, z = lookup(upper, 0), lookup(lower, 1)
        wave[:count, :width] = a[:, :width] * z[:, :width] - a[:, width : 2 * width] * z[:, width : 2 * width]
        wave[:count, width : 2 * width] = (
            a[:, width : 2 * width] * z[:, :width] + a[:, :width] * z[:, width : 2 * width]
        )
        wave[:count, 2 * width :] = a[:, 2 * width :] + z[:, 2 * width :]

    @pl.when(polar)
    def _():
        make_wave(most * chunk)

    @pl.when(helper)
    def _():
        make_wave(chunk)

    moment_load.wait()

    @pl.when(helper)
    def _():
        give().wait_recv()
        edges_leave(groups + chunk // SUB)
        make_lines(0, True)
        make_moments(0)
        far_start(0)

    @pl.when(polar)
    def _():
        @pl.loop(0, most)
        def _(i):
            make_lines(i, False)
            make_moments(i)
            far_start(i)

    @pl.when(helper)
    def _():
        swap().wait()

        @pl.loop(0, 2)
        def _(side):
            start = side * (rows - ROWS)
            tendency_block(start, plain(start))

    local_load.wait()

    @pl.when(polar)
    def _():
        make_local(most)

    @pl.when(helper)
    def _():
        make_local(1)

    edges_arrive()

    @pl.when(helper)
    def _():
        own_edges()

    field_load.wait()

    def give_back(c):
        start = jnp.where(southern, rows - chunk, 0)
        return pltpu.make_async_remote_copy(
            src_ref=gain.at[c], dst_ref=out_ref.at[c, pl.ds(pl.multiple_of(start, ROWS), chunk), :],
            send_sem=back_send.at[c], recv_sem=back_recv.at[c],
            device_id={"lat": mate}, device_id_type=MESH,
        )

    def complete(i, give_away):
        keep, first_row = kept(i, give_away)
        keep_at = pl.ds(first_row, chunk)
        at = pl.ds(pl.multiple_of(i * chunk, chunk), chunk)
        turn_cos = wave[at, :width]
        turn_sin = wave[at, width : 2 * width]
        terms = [edge_terms(c, i) for c in range(3)]
        at_edge = jnp.concatenate(
            [term * turn[:, width - LANES :] for turn in (turn_cos, turn_sin) for term in terms], axis=0
        )
        for k in range(3):
            far_copy(i, k).wait_recv()
        gathered = []
        for k, (first, _, size) in enumerate(RANKS):
            value = recv[i, pl.ds(spans[k][0], spans[k][1]), :]
            slots = [turned(value, first - s * size) for s in range(LANES // size)]
            for s in (-2, -1):
                slots[s] = slots[s][spans[k][1] * (LANES // size // 2) - lines :]
            gathered.append(jnp.concatenate(slots[0::2] + slots[1::2], axis=0))
        at_lane = lax.broadcasted_iota(jnp.int32, (2 * lines, LANES), 1)
        coming = jnp.where(
            at_lane < NEAR, gathered[0],
            jnp.where(at_lane < 2 * NEAR, gathered[1], jnp.where(at_lane < EDGE, gathered[2], at_edge)),
        )
        _, high, low = high_low(coming)
        used = EDGE + edges
        low = pltpu.roll(low, used, 1)
        left = jnp.where(at_lane < used, high, low)
        right = jnp.where(at_lane < 2 * used - LANES, low, pltpu.roll(high, 2 * used - LANES, 1))
        factors = jnp.concatenate([left.astype(jnp.bfloat16), right.astype(jnp.bfloat16)], axis=1)
        whole = part[i] + dot(factors, field[...])
        own = wave[at, 2 * width :]
        for c in range(3):
            by_cos = whole[c * chunk : (c + 1) * chunk, :cols]
            by_sin = whole[lines + c * chunk : lines + (c + 1) * chunk, :cols]
            change = turn_sin[:, :cols] * by_cos - turn_cos[:, :cols] * by_sin
            first, end = edge_places(own * terms[c])
            keep[c, keep_at, :] = keep[c, keep_at, :] + change
            keep[c, keep_at, :LANES] = keep[c, keep_at, :LANES] + first
            keep[c, keep_at, cols - rest :] = keep[c, keep_at, cols - rest :] + end
            if give_away:
                give_back(c).start()

    @pl.when(polar)
    def _():
        @pl.loop(0, most)
        def _(i):
            complete(i, False)

        give().wait_send()
        for c in range(3):
            give_back(c).wait_recv()

    @pl.when(helper)
    def _():
        complete(0, True)
        for c in range(3):
            give_back(c).wait_send()

    @pl.loop(0, chunks)
    def _(i):
        for k in range(3):
            far_copy(i, k).wait_send()


def fused_step(mesh_shape, tables, state_now, state_old, polar_cutoff):
    lat_count, lon_count = mesh_shape
    comps, rows, cols = state_now.shape
    chunk = chunk_rows(rows)
    chunks = rows // chunk - 1
    lines = comps * chunk
    width = -(-cols // LANES) * LANES
    geo, scale, phase, local, moment, field = tables
    operands = [
        pltpu.with_memory_space_constraint(jnp.asarray(a), pltpu.HBM)
        for a in (state_now, geo, scale, polar_cutoff, phase, local, moment, field)
    ]
    hbm_spec = pl.BlockSpec(memory_space=pltpu.HBM)
    vmem_spec = pl.BlockSpec(memory_space=pltpu.VMEM)
    dma = pltpu.SemaphoreType.DMA
    packed = (-(-comps * scale.shape[1] // lon_count), SUB, LANES)
    exchange = pltpu.VMEM((chunks, lines + -(-lines // (4 * SUB)) * SUB, LANES), jnp.float32)
    change = pl.pallas_call(
        functools.partial(step_kernel, lat_count, lon_count, chunk),
        out_shape=jax.ShapeDtypeStruct(state_now.shape, jnp.float32),
        in_specs=[hbm_spec] * 8,
        out_specs=vmem_spec,
        scratch_shapes=[
            pltpu.VMEM((comps, rows + 2 * (chunk + SUB), cols), jnp.float32),
            pltpu.VMEM((rows + chunk, LANES), jnp.float32),
            pltpu.VMEM(scale.shape[1:], jnp.float32),
            pltpu.VMEM((2 * rows,), jnp.int32),
            pltpu.VMEM(phase.shape[1:], jnp.bfloat16),
            pltpu.VMEM(local.shape, jnp.bfloat16),
            pltpu.VMEM(moment.shape, jnp.bfloat16),
            pltpu.VMEM(field.shape[1:], jnp.bfloat16),
            pltpu.VMEM((chunks * chunk, 2 * width + LANES), jnp.float32),
            pltpu.VMEM((chunks, 2 * lines, 2 * MAIN + 2 * LANES), jnp.bfloat16),
            pltpu.VMEM((chunks, 2 * lines, width), jnp.float32),
            exchange,
            exchange,
            pltpu.VMEM(packed, jnp.float32),
            pltpu.VMEM((lon_count, *packed), jnp.float32),
            pltpu.VMEM((comps, *scale.shape[1:]), jnp.float32),
            pltpu.VMEM((comps, chunk, cols), jnp.float32),
            dma((3,)), dma((8,)), dma((2,)), dma((2,)), dma((lon_count,)), dma((lon_count,)),
            dma((chunks, 3)), dma((chunks, 3)), dma((3,)), dma((3,)),
        ],
        compiler_params=pltpu.CompilerParams(
            collective_id=0, has_side_effects=True, vmem_limit_bytes=40 * 1024 * 1024
        ),
    )(*operands)
    return state_old + change


def chunk_rows(rows):
    return rows // 6 if rows % 96 == 0 else 0


def solution(mesh):
    lat_count, lon_count = mesh.shape["lat"], mesh.shape["lon"]

    def step(state_now, state_old, polar_cutoff):
        comps, lat_total, lon_total = state_now.shape
        rows, cols = lat_total // lat_count, lon_total // lon_count
        fits = (
            lat_count == 4 and lon_count == 4 and lat_total == 4 * rows and chunk_rows(rows) > 0
            and cols == MAIN + LANES // 2 and rows // SUB <= LANES and comps == 3 * mesh.shape["ens"]
        )
        body = per_device
        if fits:
            geo = geometry_table(lat_total, lon_total)
            tables = (
                geo, edge_scale(geo, lat_count, lon_count, chunk_rows(rows)), phase_tables(cols, lon_count),
                *convolution_tables(cols, lon_count),
            )
            body = functools.partial(fused_step, (lat_count, lon_count), tables)
        return jax.shard_map(
            body,
            mesh=mesh,
            in_specs=(P("ens", "lat", "lon"), P("ens", "lat", "lon"), P()),
            out_specs=P("ens", "lat", "lon"),
            check_vma=False,
        )(state_now, state_old, polar_cutoff)

    return step
```

```python
import functools
import math

import jax
import jax.numpy as jnp
import numpy as np
from jax import lax
from jax.experimental import pallas as pl
from jax.experimental.pallas import tpu as pltpu
from jax.sharding import PartitionSpec as P

LANES = 128
SUB = 8
MESH = pl.DeviceIdType.MESH
step_scale = 0.2
coriolis = 2.0
gravity = 1.0
highest = lax.Precision.HIGHEST


def padded(value, sides, width, wrap):
    for axis, dim in sides:
        devices, length = (lax.axis_size(axis), value.shape[dim])
        up = [(i, (i + 1) % devices) for i in range(devices if wrap else devices - 1)]
        down = [(j, i) for i, j in up]
        last = lax.slice_in_dim(value, length - width, length, axis=dim)
        leading = lax.slice_in_dim(value, 0, width, axis=dim)
        before = lax.ppermute(last, axis, up)
        after = lax.ppermute(leading, axis, down)
        value = jnp.concatenate([before, value, after], axis=dim)
    return value


def latitude_terms(row_index, lat_total):
    distance = jnp.minimum(row_index + 0.5, lat_total - row_index - 0.5)
    cosine_lat = jnp.sin(math.pi * distance / lat_total)
    sine_lat = -jnp.cos(math.pi * (row_index + 0.5) / lat_total)
    return (cosine_lat, sine_lat)


def tendencies(lat_padded, lon_padded, cos_ext, sine_lat, lat_total, lon_total):
    cosine_lat = cos_ext[1:-1]
    zonal_scale = (lon_total / (4.0 * lat_total) / cosine_lat)[:, None]
    metric = math.pi / lat_total * sine_lat / cosine_lat
    depth_lon, east_lon, north_lon = (lon_padded[0], lon_padded[1], lon_padded[2])
    depth_lat, east_lat, north_lat = (lat_padded[0], lat_padded[1], lat_padded[2])
    east = east_lon[:, 1:-1]
    north = north_lon[:, 1:-1]

    def zonal_change(field):
        return zonal_scale * (field[:, 2:] - field[:, :-2])

    def northward_change(field):
        return 0.5 * (field[2:] - field[:-2])

    mass_flux = depth_lat * north_lat * cos_ext[:, None]
    tend_depth = (
        -zonal_change(depth_lon * east_lon) - northward_change(mass_flux) / cosine_lat[:, None]
    )
    turning = coriolis * sine_lat[:, None] + metric[:, None] * east
    tend_east = (
        -east * zonal_change(east_lon)
        - north * northward_change(east_lat)
        + turning * north
        - gravity * zonal_change(depth_lon)
    )
    tend_north = (
        -east * zonal_change(north_lon)
        - north * northward_change(north_lat)
        - turning * east
        - gravity * northward_change(depth_lat)
    )
    return jnp.stack([tend_depth, tend_east, tend_north])


def angle_table(first_count, second_count, period):
    first_idx = jnp.arange(first_count, dtype=jnp.int32)
    second_idx = jnp.arange(second_count, dtype=jnp.int32)
    turns = first_idx[:, None] * second_idx[None, :] % period
    phase = turns.astype(jnp.float32) * (2.0 * math.pi / period)
    return (jnp.cos(phase), jnp.sin(phase))


def low_pass(signal, cutoff):
    count, length = signal.shape
    first = 1
    probe = 1
    while probe * probe <= length:
        if length % probe == 0:
            first = probe
        probe = probe + 1
    second = length // first
    cos_first, sin_first = angle_table(first, first, first)
    cos_second, sin_second = angle_table(second, second, second)
    cos_twist, sin_twist = angle_table(first, second, length)
    grid = signal.reshape(count, first, second)
    part_re = jnp.einsum("cpq,pk->ckq", grid, cos_first, precision=highest)
    part_im = -jnp.einsum("cpq,pk->ckq", grid, sin_first, precision=highest)
    twist_re = part_re * cos_twist + part_im * sin_twist
    twist_im = part_im * cos_twist - part_re * sin_twist
    spec_re = jnp.einsum("ckq,qm->ckm", twist_re, cos_second, precision=highest) + jnp.einsum(
        "ckq,qm->ckm", twist_im, sin_second, precision=highest
    )
    spec_im = jnp.einsum("ckq,qm->ckm", twist_im, cos_second, precision=highest) - jnp.einsum(
        "ckq,qm->ckm", twist_re, sin_second, precision=highest
    )
    wave = (
        jnp.arange(first, dtype=jnp.int32)[:, None]
        + first * jnp.arange(second, dtype=jnp.int32)[None, :]
    )
    limit = cutoff[:, None, None]
    keep = ((wave[None] <= limit) | (wave[None] >= length - limit)).astype(jnp.float32) * (
        1.0 / length
    )
    spec_re = spec_re * keep
    spec_im = spec_im * keep
    back_re = jnp.einsum("ckm,mq->ckq", spec_re, cos_second, precision=highest) - jnp.einsum(
        "ckm,mq->ckq", spec_im, sin_second, precision=highest
    )
    back_im = jnp.einsum("ckm,mq->ckq", spec_im, cos_second, precision=highest) + jnp.einsum(
        "ckm,mq->ckq", spec_re, sin_second, precision=highest
    )
    turn_re = back_re * cos_twist - back_im * sin_twist
    turn_im = back_im * cos_twist + back_re * sin_twist
    result = jnp.einsum("ckq,kp->cpq", turn_re, cos_first, precision=highest) - jnp.einsum(
        "ckq,kp->cpq", turn_im, sin_first, precision=highest
    )
    return result.reshape(count, length)


def per_device(state_now, state_old, polar_cutoff):
    lat_rows = state_now.shape[1]
    lon_cols = state_now.shape[2]
    lat_count = lax.axis_size("lat")
    lon_count = lax.axis_size("lon")
    lat_total = lat_rows * lat_count
    lon_total = lon_cols * lon_count
    lat_place = lax.axis_index("lat")
    lat_padded = padded(state_now, (("lat", 1),), 1, False)
    lon_padded = padded(state_now, (("lon", 2),), 1, True)
    row_index = (lat_place * lat_rows + jnp.arange(-1, lat_rows + 1, dtype=jnp.int32)).astype(
        jnp.float32
    )
    cos_ext, sin_ext = latitude_terms(row_index, lat_total)
    forcing = tendencies(lat_padded, lon_padded, cos_ext, sin_ext[1:-1], lat_total, lon_total)
    groups = lat_count * lon_count
    share = lat_rows // groups
    member = lax.axis_index(("lat", "lon"))
    south_cut = lax.dynamic_slice_in_dim(polar_cutoff, member * share, share)
    north_cut = lax.dynamic_slice_in_dim(polar_cutoff, lat_rows + member * share, share)
    band_cut = jnp.concatenate([south_cut, north_cut])
    block = lax.all_to_all(forcing, ("lat", "lon"), split_axis=1, concat_axis=2, tiled=True)
    items = block.shape[0]
    wide = block.shape[2]
    south_rows = block[:, :, :lon_total]
    north_rows = block[:, :, wide - lon_total :]
    polar_rows = jnp.concatenate([south_rows, north_rows], axis=1)
    smooth = low_pass(polar_rows.reshape(items * 2 * share, lon_total), jnp.tile(band_cut, items))
    smooth = smooth.reshape(items, 2 * share, lon_total)
    rebuilt = jnp.concatenate(
        [smooth[:, :share], block[:, :, lon_total : wide - lon_total], smooth[:, share:]], axis=2
    )
    filtered = lax.all_to_all(rebuilt, ("lat", "lon"), split_axis=2, concat_axis=1, tiled=True)
    return state_old + step_scale * filtered


NEAR = 28
FAR = 16
MAIN = 4 * LANES
ROWS = 16
EDGE = 2 * NEAR + FAR
RANKS = [(0, NEAR, 32), (NEAR, NEAR, 32), (2 * NEAR, FAR, 16)]


def split_table(table):
    table = np.asarray(table, np.float32)
    high = table.astype(jnp.bfloat16)
    rest = table - high.astype(np.float32)
    middle = rest.astype(jnp.bfloat16)
    low = (rest - middle.astype(np.float32)).astype(jnp.bfloat16)
    return high, middle, low


def kernel_values(offset, total):
    safe = np.where(offset == 0, 1, offset)
    return np.where(offset == 0, 0.0, 1.0 / (total * np.sin(np.pi * safe / total)))


def stacked(table, cols):
    high, low, _ = split_table(table)
    zero = np.zeros((2 * LANES - 3 * (cols - MAIN), table.shape[1]), high.dtype)
    tail = [high[MAIN:], high[MAIN:], low[MAIN:], zero]
    return np.concatenate([high[:MAIN], high[:MAIN], *tail, low[:MAIN]])


def edge_columns(cols, lon_count):
    start = np.arange(lon_count) * cols
    return np.stack([start, start + cols - 1], axis=1).reshape(-1)


def convolution_tables(cols, lon_count):
    total = cols * lon_count
    width = -(-cols // LANES) * LANES
    here = np.arange(cols)
    target, source = here[:, None], here[None, :]
    local = np.zeros((cols, width))
    local[:, :cols] = step_scale * kernel_values(target - source, total).T
    moments = np.zeros((cols, LANES))
    fields = np.zeros((lon_count, LANES, width))
    lon = np.arange(lon_count)
    edge = edge_columns(cols, lon_count)
    places = [(-1, 0, NEAR), (1, NEAR, NEAR), (2, 2 * NEAR, FAR)]
    for step, start, rank in places:
        block = kernel_values(target - source + step * cols, total)
        left, scale, right = np.linalg.svd(block)
        moments[:, start : start + rank] = right[:rank].T
        back = step_scale * scale[:rank, None] * left[:, :rank].T
        for q in lon:
            origin = (q - step) % lon_count
            sign = 1.0 if q - origin == step else -1.0
            fields[q, start : start + rank, :cols] = sign * back
    piled = []
    for q in lon:
        offset = q * cols + here[None, :] - edge[:, None]
        fields[q, EDGE : EDGE + len(edge), :cols] = step_scale * kernel_values(offset, total)
        high, low, _ = split_table(fields[q])
        used = EDGE + len(edge)
        gap = np.zeros((2 * LANES - 3 * used, width), high.dtype)
        piled.append(np.concatenate([high[:used], high[:used], low[:used], gap]))
    local = stacked(local, cols)
    first = np.concatenate([stacked(moments, cols), local[:, MAIN:]], axis=1)
    return local[:, :MAIN], first, np.stack(piled)


def phase_tables(cols, lon_count):
    total = cols * lon_count
    width = -(-cols // LANES) * LANES
    digit = LANES // 2
    coarse, fine = [], []
    edge = edge_columns(cols, lon_count)
    at_edge = MAIN + EDGE + np.arange(len(edge))
    for q in range(lon_count):
        m = q * cols + np.arange(cols)[None, :]
        for out, unit in ((coarse, digit), (fine, 1)):
            k = unit * np.arange(digit)[:, None]
            table = np.zeros((digit, 2 * width + LANES))
            for columns, places in ((m, np.arange(cols)), (edge[None, :], at_edge)):
                angle = np.pi * ((k * columns) % (2 * total)) / total
                table[:, places] = np.cos(angle)
                table[:, width + places] = np.sin(angle)
            table[:, 2 * width :] = step_scale * k / total
            parts = split_table(table)
            out.append(np.concatenate(parts))
    return np.stack([np.stack(coarse), np.stack(fine)], axis=1)


def geometry_table(lat_total, lon_total):
    j = np.arange(lat_total, dtype=np.float64)

    def cosine(row):
        return np.sin(np.pi * np.minimum(row + 0.5, lat_total - row - 0.5) / lat_total)

    c = cosine(j)
    s = -np.cos(np.pi * (j + 0.5) / lat_total)
    table = np.zeros((lat_total, LANES))
    table[:, 0] = lon_total / (4.0 * lat_total * c)
    table[:, 1] = 0.5 * cosine(j + 1) / c
    table[:, 2] = 0.5 * cosine(j - 1) / c
    table[:, 3] = coriolis * s
    table[:, 4] = np.pi / lat_total * s / c
    return table.astype(np.float32)


def edge_scale(geo, lat_count, lon_count, chunk):
    rows = len(geo) // lat_count
    edges = 2 * lon_count
    per = LANES // edges
    count = -(-((rows + chunk) // SUB) // per)
    table = np.zeros((lat_count, count, SUB, LANES), np.float32)
    for lat in range(lat_count):
        first = lat * rows
        held = [first + g * SUB for g in range(rows // SUB)]
        extra = {1: first - chunk, lat_count - 2: first + rows}
        if lat in extra:
            held += [extra[lat] + g * SUB for g in range(chunk // SUB)]
        for g, row in enumerate(held):
            zonal = geo[row : row + SUB, 0]
            for k in range(edges):
                table[lat, g // per, :, g % per * edges + k] = zonal if k % 2 == 0 else -zonal
    return table


def dot(a, b):
    return lax.dot_general(a, b, (((1,), (0,)), ((), ())), preferred_element_type=jnp.float32)


def high_low(value):
    high = value.astype(jnp.bfloat16)
    back = high.astype(jnp.float32)
    return high, back, value - back


def step_kernel(
    lat_count, lon_count, chunk,
    x_hbm, geo_hbm, scale_hbm, cut_hbm, phase_hbm, local_hbm, moment_hbm, field_hbm, out_ref,
    xp, geo, scale, cut_ref, phase, local, moment, field, wave, lhs, part, send, recv,
    edge_send, edge_recv, delta, gain, load_sem, table_sem, row_send_sem, row_recv_sem,
    edge_send_sem, edge_recv_sem, far_send, far_recv, back_send, back_recv,
):
    rows, cols = out_ref.shape[1], out_ref.shape[2]
    blocks = rows // ROWS
    per_chunk = chunk // ROWS
    groups = rows // SUB
    margin = chunk + SUB
    total = lon_count * cols
    tiles = -(-cols // LANES)
    width = tiles * LANES
    rest = cols % LANES
    lines = 3 * chunk
    edges = 2 * lon_count
    edge_groups = LANES // edges
    edge_vregs = scale.shape[0]
    lat = lax.axis_index("lat")
    lon = lax.axis_index("lon")
    west = lax.rem(lon + lon_count - 1, lon_count)
    east = lax.rem(lon + 1, lon_count)
    across = lax.rem(lon + 2, lon_count)
    polar = jnp.logical_or(lat == 0, lat == lat_count - 1)
    helper = jnp.logical_not(polar)
    southern = lat < 2
    odd = lax.rem(lat, 2)
    mate = lat + 1 - 2 * odd
    most = rows // chunk - 1
    chunks = jnp.where(polar, most, 1)

    def aligned(i):
        return pl.multiple_of(i, SUB)

    chunk_zero = jnp.where(
        polar, jnp.where(southern, 0, chunk), jnp.where(southern, -chunk, rows)
    )
    geo_zero = odd * chunk
    cut_zero = jnp.where(southern, 0, rows) + jnp.where(
        polar, jnp.where(southern, 0, chunk), jnp.where(southern, rows - chunk, 0)
    )
    group_zero = jnp.where(polar, jnp.where(southern, 0, chunk // SUB), groups)

    loads = [
        pltpu.make_async_copy(x_hbm.at[c], xp.at[c, pl.ds(margin, rows), :], load_sem.at[c]) for c in range(3)
    ]
    for copy in loads:
        copy.start()
    geo_load = pltpu.make_async_copy(
        geo_hbm.at[pl.ds(aligned(lat * rows - geo_zero), rows + chunk), :], geo, table_sem.at[0]
    )
    wave_loads = [
        pltpu.make_async_copy(cut_hbm, cut_ref, table_sem.at[1]),
        pltpu.make_async_copy(phase_hbm.at[lon], phase, table_sem.at[2]),
    ]
    moment_load = pltpu.make_async_copy(moment_hbm, moment, table_sem.at[4])
    local_load = pltpu.make_async_copy(local_hbm, local, table_sem.at[5])
    field_load = pltpu.make_async_copy(field_hbm.at[lon], field, table_sem.at[6])
    scale_load = pltpu.make_async_copy(scale_hbm.at[lat], scale, table_sem.at[7])
    for copy in [geo_load, *wave_loads]:
        copy.start()

    barrier = pltpu.get_barrier_semaphore()
    for k in range(1, lon_count):
        pl.semaphore_signal(
            barrier, inc=1, device_id={"lon": lax.rem(lon + k, lon_count)}, device_id_type=MESH
        )
    pl.semaphore_signal(barrier, inc=1, device_id={"lat": mate}, device_id_type=MESH)

    @pl.when(helper)
    def _():
        pl.semaphore_signal(
            barrier, inc=1, device_id={"lat": lat_count - 1 - lat}, device_id_type=MESH
        )

    lane = lax.broadcasted_iota(jnp.int32, (SUB, LANES), 1)
    lane2 = lax.broadcasted_iota(jnp.int32, (ROWS, LANES), 1)
    sub = lax.broadcasted_iota(jnp.int32, (SUB, LANES), 0)

    def edges_leave(count):
        for first in range(0, 3 * edge_vregs, lon_count):
            packed = jnp.zeros((SUB, LANES), jnp.float32)
            for a in range(first, min(first + lon_count, 3 * edge_vregs)):
                c, w = a // edge_vregs, a % edge_vregs
                for g in range(w * edge_groups, min((w + 1) * edge_groups, count)):
                    start = g * SUB if g < groups else chunk_zero + (g - groups) * SUB
                    block = pl.ds(aligned(margin + start), SUB)
                    at = g % edge_groups * edges + 2 * (a - first)
                    packed = jnp.where(lane == at, xp[c, block, 0:1], packed)
                    packed = jnp.where(lane == at + 1, xp[c, block, cols - 1 : cols], packed)
            edge_send[first // lon_count] = packed

    for copy in loads:
        copy.wait()
    for copy in [moment_load, scale_load, local_load, field_load]:
        copy.start()

    @pl.when(polar)
    def _():
        edges_leave(groups)

    pl.semaphore_wait(barrier, lon_count + helper.astype(jnp.int32))

    def row_copy(which, source, target, count, device):
        return pltpu.make_async_remote_copy(
            src_ref=x_hbm.at[:, pl.ds(aligned(source), count), :],
            dst_ref=xp.at[:, pl.ds(aligned(target), count), :],
            send_sem=row_send_sem.at[which], recv_sem=row_recv_sem.at[which],
            device_id={"lat": device}, device_id_type=MESH,
        )

    def give():
        source = jnp.where(southern, rows - margin, 0)
        target = jnp.where(southern, 0, margin + rows)
        return row_copy(0, source, target, margin, mate)

    def swap():
        source = jnp.where(southern, rows - SUB, 0)
        target = jnp.where(southern, margin - SUB, margin + rows)
        return row_copy(1, source, target, SUB, lat_count - 1 - lat)

    @pl.when(polar)
    def _():
        give().start()

    @pl.when(helper)
    def _():
        swap().start()


    @pl.when(polar)
    def _():
        start = jnp.where(southern, margin - SUB, margin + rows)
        xp[:, pl.ds(aligned(start), SUB), :] = jnp.zeros((3, SUB, cols), jnp.float32)


    def edge_copy(k, source):
        target = lax.rem(source + k, lon_count)
        return pltpu.make_async_remote_copy(
            src_ref=edge_send, dst_ref=edge_recv.at[k],
            send_sem=edge_send_sem.at[k], recv_sem=edge_recv_sem.at[k],
            device_id={"lon": target}, device_id_type=MESH,
        )

    def edges_start():
        for k in range(1, lon_count):
            edge_copy(k, lon).start()

    def edges_arrive():
        for k in range(1, lon_count):
            edge_copy(k, lon).wait()
        scale_load.wait()
        k_of = lax.rem(lane, edges)

        def beside(value):
            plus = pltpu.roll(value, 1, 1)
            minus = pltpu.roll(value, LANES - 1, 1)
            last = pltpu.roll(value, LANES - edges + 1, 1)
            first = pltpu.roll(value, edges - 1, 1)
            inner = jnp.where(lax.rem(k_of, 2) == 0, plus, minus)
            return jnp.where(k_of == 0, last, jnp.where(k_of == edges - 1, first, inner))

        for w in range(edge_vregs):
            own = []
            for c in range(3):
                a = c * edge_vregs + w
                slot = a % lon_count
                parts = []
                for k in range(lon_count):
                    source = lax.rem(lon + lon_count - k, lon_count)
                    value = edge_recv[k, a // lon_count] if k else edge_send[a // lon_count]
                    value = jnp.where(k_of // 2 == slot, value, 0.0)
                    parts.append(pltpu.roll(value, lax.rem(2 * (source - slot) + LANES, LANES), 1))
                own.append((parts[0] + parts[1]) + (parts[2] + parts[3]))
            h, u, v = [beside(value) for value in own]
            factor = scale[w]
            delta[0, w] = factor * (h * u)
            delta[1, w] = factor * (own[1] * u + h)
            delta[2, w] = factor * (own[1] * v)

    def edge_terms(c, i):
        terms = []
        for n in range(chunk // SUB):
            g = group_zero + i * (chunk // SUB) + n
            shift = lax.rem(EDGE + LANES - lax.rem(g, edge_groups) * edges, LANES)
            value = pltpu.roll(delta[c, g // edge_groups], shift, 1)
            terms.append(jnp.where(jnp.logical_and(lane >= EDGE, lane < EDGE + edges), value, 0.0))
        return jnp.concatenate(terms, axis=0)

    def edge_places(value):
        at_lane = lax.broadcasted_iota(jnp.int32, value.shape, 1)
        first = pltpu.roll(value, LANES - EDGE - 2 * lon, 1)
        last = pltpu.roll(value, LANES - EDGE - 2 * lon - 1 + rest - 1, 1)
        return jnp.where(at_lane == 0, first, 0.0), jnp.where(at_lane == rest - 1, last, 0.0)[:, :rest]

    def own_edges():
        for w in range(-(-groups // edge_groups)):
            for c in range(3):
                value = step_scale * pltpu.roll(delta[c, w], lax.rem(LANES - 2 * lon, LANES), 1)
                for g in range(w * edge_groups, min((w + 1) * edge_groups, groups)):
                    at, place = pl.ds(g * SUB, SUB), g % edge_groups * edges
                    first = turned(value, -place)
                    last = turned(value, rest - 2 - place)
                    out_ref[c, at, :LANES] = out_ref[c, at, :LANES] + jnp.where(lane == 0, first, 0.0)
                    end = jnp.where(lane == rest - 1, last, 0.0)[:, :rest]
                    out_ref[c, at, cols - rest :] = out_ref[c, at, cols - rest :] + end

    def tile_of(t):
        return slice(t * LANES, min((t + 1) * LANES, cols))

    def read(ref, c, start, count, t):
        value = ref[c, pl.ds(aligned(start), count), tile_of(t)]
        if t == tiles - 1 and rest:
            value = jnp.concatenate([value, jnp.zeros((count, LANES - rest), jnp.float32)], axis=1)
        return value

    def tendency_block(start, use):
        terms = geo[pl.ds(aligned(start + geo_zero), ROWS), :]
        zonal, up, down, turn, metric = [
            jnp.broadcast_to(terms[:, i : i + 1], (ROWS, LANES)) for i in range(5)
        ]
        held = {}

        def here(c, t):
            if (0, c, t) not in held:
                held[0, c, t] = read(xp, c, start + margin, ROWS, t)
            return held[0, c, t]

        def moved(c, t, shift):
            if (shift, c, t) not in held:
                held[shift, c, t] = pltpu.roll(here(c, t), shift, 1)
            return held[shift, c, t]

        for t in range(tiles):
            east_of, west_of, north, south = [], [], [], []
            for c in range(3):
                right = moved(c, t + 1, LANES - 1) if t < tiles - 1 else 0.0
                edge_lane = LANES - 1 if t < tiles - 1 else (rest or LANES) - 1
                east_of.append(jnp.where(lane2 == edge_lane, right, moved(c, t, LANES - 1)))
                left = moved(c, t - 1, 1) if t > 0 else 0.0
                west_of.append(jnp.where(lane2 == 0, left, moved(c, t, 1)))
                value = here(c, t)
                low, high = value[:SUB], value[SUB:]
                after = read(xp, c, start + margin + ROWS, SUB, t)
                before = read(xp, c, start + margin - SUB, SUB, t)
                north.append(jnp.concatenate([
                    pltpu.roll(jnp.where(sub == 0, high, low), SUB - 1, 0),
                    pltpu.roll(jnp.where(sub == 0, after, high), SUB - 1, 0),
                ], axis=0))
                south.append(jnp.concatenate([
                    pltpu.roll(jnp.where(sub == SUB - 1, before, low), 1, 0),
                    pltpu.roll(jnp.where(sub == SUB - 1, low, high), 1, 0),
                ], axis=0))
            u, v = here(1, t), here(2, t)
            t_h = -zonal * (east_of[0] * east_of[1] - west_of[0] * west_of[1]) - (
                up * (north[0] * north[2]) - down * (south[0] * south[2])
            )
            turning = turn + metric * u
            zu = zonal * u
            hv = 0.5 * v
            t_u = (
                turning * v - zu * (east_of[1] - west_of[1]) - hv * (north[1] - south[1])
                - zonal * (east_of[0] - west_of[0])
            )
            t_v = (
                -turning * u - zu * (east_of[2] - west_of[2]) - hv * (north[2] - south[2])
                - 0.5 * (north[0] - south[0])
            )
            use(t, (t_h, t_u, t_v))

    def cut_short(value, t):
        return value[:, : min(LANES, cols - t * LANES)]

    def plain(start):
        def use(t, values):
            for c in range(3):
                out_ref[c, pl.ds(aligned(start), ROWS), tile_of(t)] = cut_short(step_scale * values[c], t)

        return use

    span_near = lines // 2
    span_far = -(-lines // (4 * SUB)) * SUB
    pairs = [(i, min(2, most - i)) for i in range(0, most, 2)]
    spans = [(0, span_near), (span_near, span_near), (2 * span_near, span_far)]

    def far_copy(i, k):
        first, count = spans[k]
        return pltpu.make_async_remote_copy(
            src_ref=send.at[i, pl.ds(first, count), :], dst_ref=recv.at[i, pl.ds(first, count), :],
            send_sem=far_send.at[i, k], recv_sem=far_recv.at[i, k],
            device_id={"lon": (west, east, across)[k]}, device_id_type=MESH,
        )

    def far_start(i):
        for k in range(3):
            far_copy(i, (k + 2) % 3).start()

    def turned(value, shift):
        shift = shift % LANES
        return pltpu.roll(value, shift, 1) if shift else value

    def merged(slots, size):
        at = lax.broadcasted_iota(jnp.int32, slots[0].shape, 1)
        whole = slots[-1]
        for s in range(len(slots) - 2, -1, -1):
            whole = jnp.where(at < (s + 1) * size, slots[s], whole)
        return whole

    def kept(i, give_away):
        if give_away:
            return gain, 0
        return out_ref, pl.multiple_of(chunk_zero + i * chunk, ROWS)

    def modulated(i, b, give_away):
        keep, first_row = kept(i, give_away)
        keep_at = pl.ds(pl.multiple_of(first_row + b * ROWS, ROWS), ROWS)
        at = pl.ds(pl.multiple_of(i * chunk + b * ROWS, ROWS), ROWS)

        def use(t, values):
            own = wave[at, 2 * width :]
            turn_cos = wave[at, t * LANES : (t + 1) * LANES]
            turn_sin = wave[at, width + t * LANES : width + (t + 1) * LANES]
            for c in range(3):
                value = values[c]
                keep[c, keep_at, tile_of(t)] = cut_short(own * value, t)
                for channel, factor in enumerate((turn_cos, turn_sin)):
                    first = channel * lines + c * chunk + b * ROWS
                    line = pl.ds(pl.multiple_of(first, ROWS), ROWS)
                    high, back_value, low = high_low(value * factor)
                    if t < tiles - 1:
                        lhs[i, line, t * LANES : (t + 1) * LANES] = high
                        lhs[i, line, MAIN + t * LANES : MAIN + (t + 1) * LANES] = low.astype(jnp.bfloat16)
                    else:
                        mixed = jnp.where(lane2 < rest, back_value, pltpu.roll(low, rest, 1))
                        lhs[i, line, 2 * MAIN : 2 * MAIN + LANES] = mixed.astype(jnp.bfloat16)
                        lhs[i, line, 2 * MAIN + LANES :] = high

        return use

    def make_lines(i, give_away):
        @pl.loop(0, per_chunk // 3)
        def _(three):
            for p in range(3):
                b = three * 3 + p
                tendency_block(chunk_zero + i * chunk + b * ROWS, modulated(i, b, give_away))

    def operands(first, count):
        value = lhs[first : first + count].reshape(count * 2 * lines, lhs.shape[2])
        return jnp.concatenate([value, value[:, :MAIN]], axis=1)

    def make_moments(first, count):
        both = dot(operands(first, count), moment[...])
        part[first : first + count, :, MAIN:] = both[:, LANES:].reshape(count, 2 * lines, width - MAIN)
        for i in range(count):
            pack_moments(first + i, both[i * 2 * lines : (i + 1) * 2 * lines, :LANES])

    def pack_moments(i, moments):
        for k, (first, _, size) in enumerate(RANKS):
            count = spans[k][1]
            slots = []
            for s in range(LANES // size):
                origin = (s % 2) * lines + min((s // 2) * count, lines - count)
                slots.append(turned(moments[origin : origin + count], s * size - first))
            send[i, pl.ds(spans[k][0], count), :] = merged(slots, size)

    def make_local(count):
        part[:count, :, :MAIN] = dot(operands(0, count), local[...]).reshape(count, 2 * lines, MAIN)

    geo_load.wait()

    @pl.when(helper)
    def _():
        @pl.loop(0, blocks // 2 - 1)
        def _(pair):
            for p in range(2):
                start = (2 * pair + 1 + p) * ROWS
                tendency_block(start, plain(start))

    @pl.when(polar)
    def _():
        edges_start()

    for copy in wave_loads:
        copy.wait()
    cuts = cut_ref[...].astype(jnp.float32)[None, :]

    def make_wave(count):
        wanted = cut_zero + lax.broadcasted_iota(jnp.int32, (count, 2 * rows), 0)
        hit = wanted == lax.broadcasted_iota(jnp.int32, (count, 2 * rows), 1)
        limit = jnp.sum(jnp.where(hit, cuts, 0.0), axis=1, keepdims=True)
        turns = jnp.minimum(2.0 * limit + 1.0, float(total))
        digit = LANES // 2
        upper = jnp.floor(turns * (1.0 / digit))
        lower = turns - digit * upper
        place = lax.rem(lax.broadcasted_iota(jnp.int32, (count, LANES), 1), digit).astype(jnp.float32)

        def lookup(value, k):
            found = (place == value).astype(jnp.bfloat16)
            return dot(jnp.concatenate([found, found[:, :digit]], axis=1), phase[k])

        a, z = lookup(upper, 0), lookup(lower, 1)
        wave[:count, :width] = a[:, :width] * z[:, :width] - a[:, width : 2 * width] * z[:, width : 2 * width]
        wave[:count, width : 2 * width] = (
            a[:, width : 2 * width] * z[:, :width] + a[:, :width] * z[:, width : 2 * width]
        )
        wave[:count, 2 * width :] = a[:, 2 * width :] + z[:, 2 * width :]

    @pl.when(polar)
    def _():
        make_wave(most * chunk)

    @pl.when(helper)
    def _():
        make_wave(chunk)

    @pl.when(helper)
    def _():
        give().wait_recv()
        edges_leave(groups + chunk // SUB)
        edges_start()
        make_lines(0, True)
        moment_load.wait()
        make_moments(0, 1)
        far_start(0)

    @pl.when(polar)
    def _():
        for first, count in [(i, 1) for i in range(most)]:
            for i in range(first, first + count):
                make_lines(i, False)
            if first == 0:
                moment_load.wait()
            make_moments(first, count)
            for i in range(first, first + count):
                far_start(i)

    @pl.when(helper)
    def _():
        swap().wait()

        @pl.loop(0, 2)
        def _(side):
            start = side * (rows - ROWS)
            tendency_block(start, plain(start))

    local_load.wait()

    @pl.when(polar)
    def _():
        make_local(most)

    @pl.when(helper)
    def _():
        make_local(1)

    edges_arrive()

    @pl.when(helper)
    def _():
        own_edges()

    field_load.wait()

    def give_back(c):
        start = jnp.where(southern, rows - chunk, 0)
        return pltpu.make_async_remote_copy(
            src_ref=gain.at[c], dst_ref=out_ref.at[c, pl.ds(pl.multiple_of(start, ROWS), chunk), :],
            send_sem=back_send.at[c], recv_sem=back_recv.at[c],
            device_id={"lat": mate}, device_id_type=MESH,
        )

    def complete(first, count, give_away):
        arrived = [arrive(i) for i in range(first, first + count)]
        factors = jnp.concatenate([value for value, _ in arrived], axis=0)
        whole = part[first : first + count].reshape(count * 2 * lines, width) + dot(factors, field[...])
        for i in range(count):
            finish(first + i, whole[i * 2 * lines : (i + 1) * 2 * lines], arrived[i][1], give_away)

    def arrive(i):
        at = pl.ds(i * chunk, chunk)
        turn_cos = wave[at, :width]
        turn_sin = wave[at, width : 2 * width]
        terms = [edge_terms(c, i) for c in range(3)]
        at_edge = jnp.concatenate(
            [term * turn[:, width - LANES :] for turn in (turn_cos, turn_sin) for term in terms], axis=0
        )
        for k in range(3):
            far_copy(i, k).wait_recv()
        gathered = []
        for k, (first, _, size) in enumerate(RANKS):
            value = recv[i, pl.ds(spans[k][0], spans[k][1]), :]
            slots = [turned(value, first - s * size) for s in range(LANES // size)]
            for s in (-2, -1):
                slots[s] = slots[s][spans[k][1] * (LANES // size // 2) - lines :]
            gathered.append(jnp.concatenate(slots[0::2] + slots[1::2], axis=0))
        at_lane = lax.broadcasted_iota(jnp.int32, (2 * lines, LANES), 1)
        coming = jnp.where(
            at_lane < NEAR, gathered[0],
            jnp.where(at_lane < 2 * NEAR, gathered[1], jnp.where(at_lane < EDGE, gathered[2], at_edge)),
        )
        _, high, low = high_low(coming)
        used = EDGE + edges
        low = pltpu.roll(low, used, 1)
        left = jnp.where(at_lane < used, high, low)
        right = jnp.where(at_lane < 2 * used - LANES, low, pltpu.roll(high, 2 * used - LANES, 1))
        return jnp.concatenate([left.astype(jnp.bfloat16), right.astype(jnp.bfloat16)], axis=1), terms

    def finish(i, whole, terms, give_away):
        keep, first_row = kept(i, give_away)
        keep_at = pl.ds(first_row, chunk)
        at = pl.ds(i * chunk, chunk)
        turn_cos = wave[at, :width]
        turn_sin = wave[at, width : 2 * width]
        own = wave[at, 2 * width :]
        for c in range(3):
            by_cos = whole[c * chunk : (c + 1) * chunk, :cols]
            by_sin = whole[lines + c * chunk : lines + (c + 1) * chunk, :cols]
            change = turn_sin[:, :cols] * by_cos - turn_cos[:, :cols] * by_sin
            first, end = edge_places(own * terms[c])
            for t in range(tiles):
                value = keep[c, keep_at, tile_of(t)] + change[:, tile_of(t)]
                if t == 0:
                    value = value + first
                if t == tiles - 1:
                    value = value + end
                keep[c, keep_at, tile_of(t)] = value
            if give_away:
                give_back(c).start()

    @pl.when(polar)
    def _():
        for first, count in pairs:
            complete(first, count, False)

        give().wait_send()
        for c in range(3):
            give_back(c).wait_recv()

    @pl.when(helper)
    def _():
        complete(0, 1, True)
        for c in range(3):
            give_back(c).wait_send()

    @pl.loop(0, chunks)
    def _(i):
        for k in range(3):
            far_copy(i, k).wait_send()


def fused_step(mesh_shape, tables, state_now, state_old, polar_cutoff):
    lat_count, lon_count = mesh_shape
    comps, rows, cols = state_now.shape
    chunk = chunk_rows(rows)
    chunks = rows // chunk - 1
    lines = comps * chunk
    width = -(-cols // LANES) * LANES
    geo, scale, phase, local, moment, field = tables
    operands = [
        pltpu.with_memory_space_constraint(jnp.asarray(a), pltpu.HBM)
        for a in (state_now, geo, scale, polar_cutoff, phase, local, moment, field)
    ]
    hbm_spec = pl.BlockSpec(memory_space=pltpu.HBM)
    vmem_spec = pl.BlockSpec(memory_space=pltpu.VMEM)
    dma = pltpu.SemaphoreType.DMA
    packed = (-(-comps * scale.shape[1] // lon_count), SUB, LANES)
    exchange = pltpu.VMEM((chunks, lines + -(-lines // (4 * SUB)) * SUB, LANES), jnp.float32)
    change = pl.pallas_call(
        functools.partial(step_kernel, lat_count, lon_count, chunk),
        out_shape=jax.ShapeDtypeStruct(state_now.shape, jnp.float32),
        in_specs=[hbm_spec] * 8,
        out_specs=vmem_spec,
        scratch_shapes=[
            pltpu.VMEM((comps, rows + 2 * (chunk + SUB), cols), jnp.float32),
            pltpu.VMEM((rows + chunk, LANES), jnp.float32),
            pltpu.VMEM(scale.shape[1:], jnp.float32),
            pltpu.VMEM((2 * rows,), jnp.int32),
            pltpu.VMEM(phase.shape[1:], jnp.bfloat16),
            pltpu.VMEM(local.shape, jnp.bfloat16),
            pltpu.VMEM(moment.shape, jnp.bfloat16),
            pltpu.VMEM(field.shape[1:], jnp.bfloat16),
            pltpu.VMEM((chunks * chunk, 2 * width + LANES), jnp.float32),
            pltpu.VMEM((chunks, 2 * lines, 2 * MAIN + 2 * LANES), jnp.bfloat16),
            pltpu.VMEM((chunks, 2 * lines, width), jnp.float32),
            exchange,
            exchange,
            pltpu.VMEM(packed, jnp.float32),
            pltpu.VMEM((lon_count, *packed), jnp.float32),
            pltpu.VMEM((comps, *scale.shape[1:]), jnp.float32),
            pltpu.VMEM((comps, chunk, cols), jnp.float32),
            dma((3,)), dma((8,)), dma((2,)), dma((2,)), dma((lon_count,)), dma((lon_count,)),
            dma((chunks, 3)), dma((chunks, 3)), dma((3,)), dma((3,)),
        ],
        compiler_params=pltpu.CompilerParams(
            collective_id=0, has_side_effects=True, vmem_limit_bytes=40 * 1024 * 1024
        ),
    )(*operands)
    return state_old + change


def chunk_rows(rows):
    return rows // 6 if rows % 96 == 0 else 0


def solution(mesh):
    lat_count, lon_count = mesh.shape["lat"], mesh.shape["lon"]

    def step(state_now, state_old, polar_cutoff):
        comps, lat_total, lon_total = state_now.shape
        rows, cols = lat_total // lat_count, lon_total // lon_count
        fits = (
            lat_count == 4 and lon_count == 4 and lat_total == 4 * rows and chunk_rows(rows) > 0
            and cols == MAIN + LANES // 2 and rows // SUB <= LANES and comps == 3 * mesh.shape["ens"]
        )
        body = per_device
        if fits:
            geo = geometry_table(lat_total, lon_total)
            tables = (
                geo, edge_scale(geo, lat_count, lon_count, chunk_rows(rows)), phase_tables(cols, lon_count),
                *convolution_tables(cols, lon_count),
            )
            body = functools.partial(fused_step, (lat_count, lon_count), tables)
        return jax.shard_map(
            body,
            mesh=mesh,
            in_specs=(P("ens", "lat", "lon"), P("ens", "lat", "lon"), P()),
            out_specs=P("ens", "lat", "lon"),
            check_vma=False,
        )(state_now, state_old, polar_cutoff)

    return step
```
